32 devices in a mesh: groups: 2 (over y), tr: 8 (over z, x), tc: 2 (over core).
Axes of the slice: x: 2, y: 2, z: 4, core: 2. Of those that a mesh axis runs over, the one named last changes fastest.
Arguments:
- shift_plane: float32 [2, 8192, 4096], P(None, ('groups', 'tr'), 'tc'), parts along dimension 1, may hold values from -0.2 to 0.2
- height: float32 [8192, 4096], P(('groups', 'tr'), 'tc'), parts along dimension 0, may hold values from -4 to 4
- dipole: float32 [8192, 4096], P(('groups', 'tr'), 'tc'), parts along dimension 0, may hold values from -6 to 6
Outputs:
- velocity_update: float32 [3, 8192, 4096], P(None, ('groups', 'tr'), 'tc'), parts along dimension 1
- dipole_update: float32 [8192, 4096], P(('groups', 'tr'), 'tc'), parts along dimension 0
The draws below stay inside these ranges and needn't reach their ends.
There are 2 independent parts, one for each index of `groups`. The reference program is written for one: setup_inputs(seed, part) draws one part's arguments, and reference() takes and returns one part's arrays. A program takes and returns all parts, laid end to end along the dimension named above; each array names one. Nothing has to cross between parts.
All inputs are finite; a program needn't handle non-finite values.
Results may differ from the reference program's by a relative error of at most 0.00009.
Values sent between devices are 32-bit elements; how exact they have to be, the bound alone decides.
A program may use at most 256 MiB of HBM per device.

```python
import jax
import jax.numpy as jnp

NB = 4096
NA = 4096


def block_scale(stream_key, dims, pieces, low, top_value):
    def one(position, blocks):
        draws = jax.random.uniform(jax.random.fold_in(jax.random.fold_in(stream_key, 6), position), (blocks,), jnp.float32, low / len(pieces), top_value / len(pieces))
        return jnp.repeat(jnp.exp(draws), dims[position] // blocks).reshape((-1,) + (1,) * (len(dims) - position - 1))

    gain = one(*pieces[0])
    for cut in pieces[1:]:
        gain = gain * one(*cut)
    return gain


def gaussian(rng, dims, width, limit, shards=(), kind=jnp.bfloat16):
    loudness = block_scale(rng, dims, shards, -0.22, 0.18) if shards else 1.0
    array = jax.random.normal(rng, dims, jnp.float32) * width * loudness
    return jnp.minimum(jnp.maximum(array, -limit), limit).astype(kind)


def setup_inputs(seed: int = 0, part: int = 0) -> dict:
    key_list = jax.random.split(jax.random.key(seed), 4)
    part_keys = jax.random.split(jax.random.fold_in(key_list[3], part), 4)
    shift_plane = jnp.clip(jax.random.uniform(part_keys[0], (2, NA, NB), jnp.float32, -0.2, 0.2) * block_scale(part_keys[0], (2, NA, NB), ((1, 8), (2, 2)), -0.4, 0.0), -0.2, 0.2)
    height = gaussian(part_keys[1], (NA, NB), 1.0, 4.0, ((0, 8), (1, 2)), jnp.float32)
    dipole = gaussian(part_keys[2], (NA, NB), 1.0, 6.0, ((0, 8), (1, 2)), jnp.float32)
    return {"shift_plane": shift_plane, "height": height, "dipole": dipole}


def first_diff(field, axis):
    return (jnp.roll(field, 2, axis) - 8.0 * jnp.roll(field, 1, axis) + 8.0 * jnp.roll(field, -1, axis) - jnp.roll(field, -2, axis)) / 12.0

def second_diff(field, axis):
    return (-jnp.roll(field, 2, axis) + 16.0 * jnp.roll(field, 1, axis) - 30.0 * field + 16.0 * jnp.roll(field, -1, axis) - jnp.roll(field, -2, axis)) / 12.0

def surface(grad_a, grad_b, curve_aa, curve_bb, curve_ab):
    tan_a = (1.0 + grad_a[0], grad_a[1], grad_a[2])
    tan_b = (grad_b[0], 1.0 + grad_b[1], grad_b[2])
    normal = (tan_a[1] * tan_b[2] - tan_a[2] * tan_b[1], tan_a[2] * tan_b[0] - tan_a[0] * tan_b[2], tan_a[0] * tan_b[1] - tan_a[1] * tan_b[0])
    area_stretch_factor = jnp.sqrt(normal[0] * normal[0] + normal[1] * normal[1] + normal[2] * normal[2])
    unit = (normal[0] / area_stretch_factor, normal[1] / area_stretch_factor, normal[2] / area_stretch_factor)
    first_edge_term = tan_a[0] * tan_a[0] + tan_a[1] * tan_a[1] + tan_a[2] * tan_a[2]
    first_f = tan_a[0] * tan_b[0] + tan_a[1] * tan_b[1] + tan_a[2] * tan_b[2]
    first_g = tan_b[0] * tan_b[0] + tan_b[1] * tan_b[1] + tan_b[2] * tan_b[2]
    second_l = curve_aa[0] * unit[0] + curve_aa[1] * unit[1] + curve_aa[2] * unit[2]
    second_m = curve_ab[0] * unit[0] + curve_ab[1] * unit[1] + curve_ab[2] * unit[2]
    second_n = curve_bb[0] * unit[0] + curve_bb[1] * unit[1] + curve_bb[2] * unit[2]
    curvature = (first_edge_term * second_n - 2.0 * first_f * second_m + first_g * second_l) / (2.0 * area_stretch_factor * area_stretch_factor)
    omega = (grad_a[3] / area_stretch_factor, grad_b[3] / area_stretch_factor)
    return (unit, curvature, omega)

def reference(shift_plane, height, dipole):
    fields = jnp.concatenate([shift_plane, height[None], dipole[None]], 0)
    grad_a = first_diff(fields, 1)
    grad_b = first_diff(fields, 2)
    curve_aa = second_diff(fields[:3], 1)
    curve_bb = second_diff(fields[:3], 2)
    curve_ab = first_diff(first_diff(fields[:3], 2), 1)
    unit, curvature, omega = surface(grad_a, grad_b, curve_aa, curve_bb, curve_ab)
    spec_one = jnp.fft.fft2(omega[0])
    spec_two = jnp.fft.fft2(omega[1])
    freq_one = jnp.fft.fftfreq(NA).astype(omega[0].dtype)[:, None]
    freq_two = jnp.fft.fftfreq(NB).astype(omega[0].dtype)[None, :]
    radius = jnp.sqrt(freq_one * freq_one + freq_two * freq_two)
    live = (jnp.abs(freq_one) < 0.5) & (jnp.abs(freq_two) < 0.5) & (radius > 0.0)
    factor = jnp.where(live, 0.5 / jnp.where(live, radius, 1.0), 0.0)
    summed = factor * (freq_one * spec_one + freq_two * spec_two)
    speed_hat = summed * -1j
    speed = jnp.real(jnp.fft.ifft2(speed_hat)).astype(height.dtype)
    velocity_update = jnp.stack([speed * unit[0], speed * unit[1], speed * unit[2]])
    dipole_update = -2.0 * 0.5 * 0.5 * height + 0.3 * curvature + 0.5 * speed * speed
    return (velocity_update.astype(jnp.float32), dipole_update.astype(jnp.float32))
```

```python
import math

import jax
import jax.numpy as jnp
import numpy as np
from jax import lax
from jax.experimental import pallas as pl
from jax.experimental.pallas import tpu as pltpu
from jax.sharding import PartitionSpec as P

largest_wavenumber = lax.Precision.HIGHEST


def padded_2(x, sides, width):
    for axis, dim in sides:
        devices, length = (lax.axis_size(axis), x.shape[dim])
        up = [(i, (i + 1) % devices) for i in range(devices)]
        down = [(j, i) for i, j in up]
        last = lax.slice_in_dim(x, length - width, length, axis=dim)
        initial = lax.slice_in_dim(x, 0, width, axis=dim)
        before = lax.ppermute(last, axis, up)
        after = lax.ppermute(initial, axis, down)
        x = jnp.concatenate([before, x, after], axis=dim)
    return x


def rows_first(field):
    return (
        field[..., :-4, :]
        - 8.0 * field[..., 1:-3, :]
        + 8.0 * field[..., 3:-1, :]
        - field[..., 4:, :]
    ) / 12.0


def cols_first(field):
    return (
        field[..., :-4] - 8.0 * field[..., 1:-3] + 8.0 * field[..., 3:-1] - field[..., 4:]
    ) / 12.0


def rows_second(field):
    return (
        -field[..., :-4, :]
        + 16.0 * field[..., 1:-3, :]
        - 30.0 * field[..., 2:-2, :]
        + 16.0 * field[..., 3:-1, :]
        - field[..., 4:, :]
    ) / 12.0


def second_column_split(field):
    return (
        -field[..., :-4]
        + 16.0 * field[..., 1:-3]
        - 30.0 * field[..., 2:-2]
        + 16.0 * field[..., 3:-1]
        - field[..., 4:]
    ) / 12.0


def surface(grad_a, grad_b, curve_aa, curve_bb, curve_ab):
    tan_a = (1.0 + grad_a[0], grad_a[1], grad_a[2])
    tan_b = (grad_b[0], 1.0 + grad_b[1], grad_b[2])
    normal = (
        tan_a[1] * tan_b[2] - tan_a[2] * tan_b[1],
        tan_a[2] * tan_b[0] - tan_a[0] * tan_b[2],
        tan_a[0] * tan_b[1] - tan_a[1] * tan_b[0],
    )
    area_stretch_factor = jnp.sqrt(
        normal[0] * normal[0] + normal[1] * normal[1] + normal[2] * normal[2]
    )
    unit = (
        normal[0] / area_stretch_factor,
        normal[1] / area_stretch_factor,
        normal[2] / area_stretch_factor,
    )
    first_edge_term = tan_a[0] * tan_a[0] + tan_a[1] * tan_a[1] + tan_a[2] * tan_a[2]
    first_f = tan_a[0] * tan_b[0] + tan_a[1] * tan_b[1] + tan_a[2] * tan_b[2]
    first_g = tan_b[0] * tan_b[0] + tan_b[1] * tan_b[1] + tan_b[2] * tan_b[2]
    second_l = curve_aa[0] * unit[0] + curve_aa[1] * unit[1] + curve_aa[2] * unit[2]
    second_m = curve_ab[0] * unit[0] + curve_ab[1] * unit[1] + curve_ab[2] * unit[2]
    second_n = curve_bb[0] * unit[0] + curve_bb[1] * unit[1] + curve_bb[2] * unit[2]
    curvature = (first_edge_term * second_n - 2.0 * first_f * second_m + first_g * second_l) / (
        2.0 * area_stretch_factor * area_stretch_factor
    )
    omega = (grad_a[3] / area_stretch_factor, grad_b[3] / area_stretch_factor)
    return (unit, curvature, omega)


def factors(length):
    inner = min(length, 256)
    return (length // inner, inner)


def angles(count_one, count_two, modulus):
    sample_lattice = (
        jnp.arange(count_one, dtype=jnp.int32)[:, None]
        * jnp.arange(count_two, dtype=jnp.int32)[None, :]
        % modulus
    )
    theta = sample_lattice.astype(jnp.float32) * (2.0 * math.pi / modulus)
    return (jnp.cos(theta), jnp.sin(theta))


def rotation(cos_table, sin_table, sense):
    top = jnp.stack([cos_table, sense * sin_table])
    low = jnp.stack([-sense * sin_table, cos_table])
    return jnp.stack([top, low])


def twisted(sheet_portion, cos_table, sin_table, sense):
    twist_re = sheet_portion[0] * cos_table + sense * sheet_portion[1] * sin_table
    twist_im = sheet_portion[1] * cos_table - sense * sheet_portion[0] * sin_table
    return jnp.stack([twist_re, twist_im])


def forward(values, length, kept, real_input):
    outer, inner = factors(length)
    cos_outer, sin_outer = angles(outer, outer, outer)
    if real_input:
        leading = values.shape[:-1]
        sample_lattice = values.reshape(leading + (outer, inner))
        lookup_array = jnp.stack([cos_outer, -sin_outer])
        sheet_portion = jnp.einsum(
            "...lm,zln->z...nm", sample_lattice, lookup_array, precision=largest_wavenumber
        )
    else:
        leading = values.shape[1:-1]
        sample_lattice = values.reshape((2,) + leading + (outer, inner))
        sheet_portion = jnp.einsum(
            "s...ab,tsac->t...cb",
            sample_lattice,
            rotation(cos_outer, sin_outer, 1.0),
            precision=largest_wavenumber,
        )
    cos_twist, sin_twist = angles(outer, inner, length)
    sheet_portion = twisted(sheet_portion, cos_twist, sin_twist, 1.0)
    cos_inner, sin_inner = angles(inner, kept, inner)
    result = jnp.einsum(
        "s...cb,tsbd->t...cd",
        sheet_portion,
        rotation(cos_inner, sin_inner, 1.0),
        precision=largest_wavenumber,
    )
    return result.reshape((2,) + leading + (outer * kept,))


def inverse(values, length, kept, want_imag):
    outer, inner = factors(length)
    leading = values.shape[1:-1]
    sample_lattice = values.reshape((2,) + leading + (outer, kept))
    cos_inner, sin_inner = angles(kept, inner, inner)
    sheet_portion = jnp.einsum(
        "s...cd,tsdb->t...cb",
        sample_lattice,
        rotation(cos_inner, sin_inner, -1.0),
        precision=largest_wavenumber,
    )
    cos_twist, sin_twist = angles(outer, inner, length)
    sheet_portion = twisted(sheet_portion, cos_twist, sin_twist, -1.0)
    cos_outer, sin_outer = angles(outer, outer, outer)
    if want_imag:
        result = jnp.einsum(
            "s...cb,tsca->t...ab",
            sheet_portion,
            rotation(cos_outer, sin_outer, -1.0),
            precision=largest_wavenumber,
        )
        return result.reshape((2,) + leading + (length,)) / length
    lookup_array = jnp.stack([cos_outer, -sin_outer])
    result = jnp.einsum(
        "s...cb,sca->...ab", sheet_portion, lookup_array, precision=largest_wavenumber
    )
    return result.reshape(leading + (length,)) / length


def wavenumbers(length, kept, positions):
    outer, _ = factors(length)
    number = positions // kept + outer * (positions % kept)
    signed = jnp.where(number >= length // 2, number - length, number)
    return (signed.astype(jnp.float32) / length, number == length // 2)


def local(shift_plane, height, dipole):
    fields = jnp.concatenate([shift_plane, height[None], dipole[None]], 0)
    padded = padded_2(fields, (("tr", 1), ("tc", 2)), 2)
    grad_a = rows_first(padded)[..., 2:-2]
    grad_b = cols_first(padded)[..., 2:-2, :]
    curve_aa = rows_second(padded[:3])[..., 2:-2]
    curve_bb = second_column_split(padded[:3])[..., 2:-2, :]
    curve_ab = rows_first(cols_first(padded[:3]))
    unit, curvature, omega = surface(grad_a, grad_b, curve_aa, curve_bb, curve_ab)
    vorticity = jnp.stack([omega[0], omega[1]])
    sheet_rows = lax.all_to_all(vorticity, "tc", split_axis=1, concat_axis=2, tiled=True)
    col_count = sheet_rows.shape[-1]
    row_count = height.shape[0] * lax.axis_size("tr")
    col_outer, col_inner = factors(col_count)
    _, row_inner = factors(row_count)
    kept = col_inner // 2
    row_spec = forward(sheet_rows, col_count, kept, True)
    stacked = row_spec.reshape((4,) + row_spec.shape[2:])
    columns = lax.all_to_all(stacked, ("tr", "tc"), split_axis=2, concat_axis=1, tiled=True)
    columns = jnp.swapaxes(columns, 1, 2)
    local_width = columns.shape[1]
    full = forward(columns.reshape((2, 2) + columns.shape[1:]), row_count, row_inner, False)
    complete_real_part = full[0]
    full_im = full[1]
    place = lax.axis_index(("tr", "tc")) * local_width + jnp.arange(local_width, dtype=jnp.int32)
    freq_two, nyquist_two = wavenumbers(col_count, kept, place)
    freq_one, nyquist_one = wavenumbers(
        row_count, row_inner, jnp.arange(row_count, dtype=jnp.int32)
    )
    freq_one = freq_one[None, :]
    freq_two = freq_two[:, None]
    radius = jnp.sqrt(freq_one * freq_one + freq_two * freq_two)
    live = (
        jnp.logical_not(nyquist_one[None, :])
        & jnp.logical_not(nyquist_two[:, None])
        & (radius > 0.0)
    )
    factor = jnp.where(live, 0.5 / jnp.where(live, radius, 1.0), 0.0)
    summed_re = factor * (freq_one * complete_real_part[0] + freq_two * complete_real_part[1])
    summed_im = factor * (freq_one * full_im[0] + freq_two * full_im[1])
    speed_parts = inverse(jnp.stack([summed_im, -summed_re]), row_count, row_inner, True)
    partial_value = jnp.swapaxes(speed_parts, 1, 2)
    back_rows = lax.all_to_all(partial_value, ("tr", "tc"), split_axis=1, concat_axis=2, tiled=True)
    weights = (
        jnp.full((col_outer, kept), 2.0, jnp.float32).at[0, 0].set(1.0).reshape(col_outer * kept)
    )
    speed_rows = inverse(back_rows * weights, col_count, kept, False)
    speed = lax.all_to_all(speed_rows, "tc", split_axis=1, concat_axis=0, tiled=True)
    velocity_update = jnp.stack([speed * unit[0], speed * unit[1], speed * unit[2]])
    dipole_update = -2.0 * 0.5 * 0.5 * height + 0.3 * curvature + 0.5 * speed * speed
    return (velocity_update, dipole_update)


LANES = 128
SUB = 8
VMEM_BYTES = 58 * 1024 * 1024


def params():
    return pltpu.CompilerParams(vmem_limit_bytes=VMEM_BYTES)


def two_halves(table):
    table = np.asarray(table, np.float32)
    high = table.astype(jnp.bfloat16)
    low = (table - high.astype(np.float32)).astype(jnp.bfloat16)
    return np.stack([high, low])


def unit_circle(count_one, count_two, modulus):
    theta = np.arange(count_one)[:, None] * np.arange(count_two)[None, :] % modulus
    theta = theta * (2.0 * math.pi / modulus)
    return np.cos(theta), np.sin(theta)


def split(x):
    high = x.astype(jnp.bfloat16)
    low = (x - high.astype(jnp.float32)).astype(jnp.bfloat16)
    return high, low


def product(a, b):
    dot = lambda p, q: jnp.dot(p, q, preferred_element_type=jnp.float32)
    return dot(a[0], b[0]) + (dot(a[0], b[1]) + dot(a[1], b[0]))


def plus(p, q):
    return q if p is None else p if q is None else p + q


def minus(p, q):
    if q is None:
        return p
    return -q if p is None else p - q


def turned(z, number, size, sense):
    re, im = z
    number = number % size
    if number == 0:
        return z
    if 4 * number == size:
        if sense > 0:
            return (im, None if re is None else -re)
        return (None if im is None else -im, re)
    c = math.cos(2.0 * math.pi * number / size)
    s = -sense * math.sin(2.0 * math.pi * number / size)
    if 8 * number == size:
        r = math.sqrt(0.5)
        if im is None:
            return (re * r, re * (-sense * r))
        if sense > 0:
            return ((re + im) * r, (im - re) * r)
        return ((re - im) * r, (im + re) * r)
    if im is None:
        return (re * c, re * s)
    return (re * c - im * s, re * s + im * c)


def butterflies(z, sense):
    size = len(z)
    if size == 1:
        return z
    even = butterflies(z[0::2], sense)
    odd = butterflies(z[1::2], sense)
    odd = [turned(o, k, size, sense) for k, o in enumerate(odd)]
    head = [(plus(e[0], o[0]), plus(e[1], o[1])) for e, o in zip(even, odd)]
    tail = [(minus(e[0], o[0]), minus(e[1], o[1])) for e, o in zip(even, odd)]
    return head + tail


def twist(z, c, s, sense):
    re, im = z
    if im is None:
        return (re * c, re * s * (-sense))
    if sense > 0:
        return (re * c + im * s, im * c - re * s)
    return (re * c - im * s, im * c + re * s)


def row_tables(outer, inner, length):
    c, s = unit_circle(outer, inner, length)
    table = np.stack([c, s]).astype(np.float32)
    return jnp.broadcast_to(jnp.asarray(table)[:, :, None, :], (2, outer, SUB, inner))


def column_table(outer, inner, width):
    c, s = unit_circle(outer, inner, outer * inner)
    table = jnp.asarray(np.stack([c, s]).astype(np.float32))
    return jnp.broadcast_to(table[..., None], (2, outer, inner, width))


def column_middle(spectra, table, freq_two, live_two, outer, inner, parts):
    length = outer * inner
    width = spectra.shape[-1]
    c, s = unit_circle(inner, inner, inner)
    matrix = two_halves(np.concatenate([c, s], 0))

    def kernel(x_ref, tw_ref, m_ref, f_ref, live_ref, *refs):
        out_refs, mid = (refs[:-1], refs[-1])

        def down(g, carry):
            r = pl.ds(pl.multiple_of(g * SUB, SUB), SUB)
            for p in range(2):
                z = [(x_ref[a, 0, p, r, :], x_ref[a, 1, p, r, :]) for a in range(outer)]
                z = butterflies(z, 1.0)
                for k in range(outer):
                    v = z[k]
                    if k:
                        v = twist(v, tw_ref[0, k, r], tw_ref[1, k, r], 1.0)
                    mid[k, r, (2 * p) * width : (2 * p + 1) * width] = v[0]
                    mid[k, r, (2 * p + 1) * width : (2 * p + 2) * width] = v[1]
            return carry

        lax.fori_loop(0, inner // SUB, down, 0)

        fre_two = f_ref[...]
        live_cols = live_ref[...]
        weights = (m_ref[0], m_ref[1])

        def turn(k, carry):
            y = product(weights, split(mid[k]))
            parts = []
            for p in range(2):
                lo = slice((2 * p) * width, (2 * p + 1) * width)
                hi = slice((2 * p + 1) * width, (2 * p + 2) * width)
                parts.append((y[:inner, lo] + y[inner:, hi], y[:inner, hi] - y[inner:, lo]))
            number = k + outer * lax.broadcasted_iota(jnp.int32, (inner, width), 0)
            signed = jnp.where(number >= length // 2, number - length, number)
            fre_one = signed.astype(jnp.float32) * (1.0 / length)
            radius = jnp.sqrt(fre_one * fre_one + fre_two * fre_two)
            live = (number != length // 2) & (live_cols > 0.0) & (radius > 0.0)
            factor = jnp.where(live, 0.5 / jnp.where(live, radius, 1.0), 0.0)
            one = factor * fre_one
            two = factor * fre_two
            sum_re = one * parts[0][0] + two * parts[1][0]
            sum_im = one * parts[0][1] + two * parts[1][1]
            w = jnp.concatenate([sum_im, -sum_re], 1)
            y = product(weights, split(w))
            mid[k, :, :width] = y[:inner, :width] - y[inner:, width:]
            mid[k, :, width : 2 * width] = y[:inner, width:] + y[inner:, :width]
            return carry

        lax.fori_loop(0, outer, turn, 0)

        for h, out_ref in enumerate(out_refs):

            def up(g, carry):
                r = pl.ds(pl.multiple_of(g * SUB + h * length // outer // parts, SUB), SUB)
                t = pl.ds(pl.multiple_of(g * SUB, SUB), SUB)
                z = []
                for k in range(outer):
                    v = (mid[k, r, :width], mid[k, r, width : 2 * width])
                    z.append(v if k == 0 else twist(v, tw_ref[0, k, r], tw_ref[1, k, r], -1.0))
                z = butterflies(z, -1.0)
                for a in range(outer):
                    out_ref[a, 0, t, :] = z[a][0] * (1.0 / length)
                    out_ref[a, 1, t, :] = z[a][1] * (1.0 / length)
                return carry

            lax.fori_loop(0, inner // parts // SUB, up, 0)

    return pl.pallas_call(
        kernel,
        out_shape=[jax.ShapeDtypeStruct((outer, 2, inner // parts, width), jnp.float32)] * parts,
        scratch_shapes=[pltpu.VMEM((outer, inner, 4 * width), jnp.float32)],
        compiler_params=params(),
        name="columns",
    )(spectra, table, jnp.asarray(matrix), freq_two, live_two)


def row_inverse(partial, outer, inner, tc):
    _, _, rows, kept = partial.shape
    length = outer * inner
    cols = length // tc
    per = outer // tc
    block = min(64, rows)
    c, s = unit_circle(kept, inner, inner)
    matrix = two_halves(np.block([[c, s], [-s, c]]) * (2.0 / length))

    def kernel(x_ref, tw_ref, m_ref, out_ref, mid):
        lane = lax.broadcasted_iota(jnp.int32, (block, kept), 1)

        def start(n, carry):
            weight = jnp.where((lane == 0) & (n == 0), 0.5, 1.0)
            w = jnp.concatenate([x_ref[n, 0] * weight, x_ref[n, 1] * weight], 1)
            mid[n] = product(split(w), (m_ref[0], m_ref[1]))
            return carry

        lax.fori_loop(0, outer, start, 0, unroll=4)

        def step(g, carry):
            r = pl.ds(pl.multiple_of(g * SUB, SUB), SUB)
            for j in range(0, inner, LANES):
                z = []
                for n in range(outer):
                    v = (mid[n, r, j : j + LANES], mid[n, r, inner + j : inner + j + LANES])
                    if n:
                        v = twist(
                            v,
                            tw_ref[0, n, :, j : j + LANES],
                            tw_ref[1, n, :, j : j + LANES],
                            -1.0,
                        )
                    z.append(v)
                z = butterflies(z, -1.0)
                for l in range(outer):
                    at = (l % per) * inner + j
                    out_ref[l // per, r, at : at + LANES] = z[l][0]
            return carry

        lax.fori_loop(0, block // SUB, step, 0)

    return pl.pallas_call(
        kernel,
        grid=(rows // block,),
        in_specs=[
            pl.BlockSpec((outer, 2, block, kept), lambda i: (0, 0, i, 0)),
            pl.BlockSpec((2, outer, SUB, inner), lambda i: (0, 0, 0, 0)),
            pl.BlockSpec(matrix.shape, lambda i: (0, 0, 0)),
        ],
        out_specs=pl.BlockSpec((tc, block, cols), lambda i: (0, i, 0)),
        out_shape=jax.ShapeDtypeStruct((tc, rows, cols), jnp.float32),
        scratch_shapes=[pltpu.VMEM((outer, block, 2 * inner), jnp.float32)],
        compiler_params=params(),
        name="rows_inverse",
    )(partial, row_tables(outer, inner, length), jnp.asarray(matrix))


MESH = pl.DeviceIdType.MESH


def front(shift_plane, height, dipole, outer, inner):
    rows, cols = height.shape
    tr, tc = lax.axis_size("tr"), lax.axis_size("tc")
    peers = tr * tc
    half = rows // tc
    block = min(32, half)
    steps = half // block
    kept = inner // 2
    per = outer // tc
    tall = block + 2 * SUB
    full = rows + 2 * SUB
    wide = min(1024, cols)
    chunk = LANES
    groups = block // SUB
    span = 4
    c, s = unit_circle(inner, kept, inner)
    matrix = two_halves(np.block([[c, -s], [s, c]]))
    loads = 4

    def kernel(
        sp_ref, h_ref, d_ref, tw_ref, m_ref, spec_ref, unit_ref, base_ref,
        pad, slope, bend, whole, mid, stage, unit_buf, base_buf,
        load_sem, edge_send, edge_recv, swap_send, swap_recv, send_sem, recv_sem, keep_sem, unit_sem, base_sem,
    ):
        my_tr, my_tc = lax.axis_index("tr"), lax.axis_index("tc")
        me = my_tr * tc + my_tc
        fields = ((sp_ref, slice(0, 2)), (h_ref, 2), (d_ref, 3))
        local = []
        for n, (ref, f) in enumerate(fields):
            for q in range(loads):
                r = rows // loads
                source = ref.at[:, q * r : (q + 1) * r] if n == 0 else ref.at[q * r : (q + 1) * r]
                target = pad.at[f, SUB + q * r : SUB + (q + 1) * r, LANES : LANES + cols]
                local.append(pltpu.make_async_copy(source, target, load_sem.at[n * loads + q]))
        for copy in local:
            copy.start()
        barrier = pltpu.get_barrier_semaphore()
        for d in range(1, peers):
            q = me ^ d
            pl.semaphore_signal(
                barrier, inc=1, device_id={"tr": q // tc, "tc": q % tc}, device_id_type=MESH
            )
        pl.semaphore_wait(barrier, peers - 1)

        down, up, across_core = (my_tr + 1) % tr, (my_tr + tr - 1) % tr, 1 - my_tc
        first, final = slice(0, SUB), slice(rows - SUB, rows)
        left, right = slice(0, LANES), slice(cols - LANES, cols)
        every, body = slice(0, rows), slice(SUB, SUB + rows)
        before, after = slice(0, SUB), slice(SUB + rows, full)
        inside, beyond = slice(LANES, LANES + cols), slice(LANES + cols, 2 * LANES + cols)
        moves = (
            (final, slice(0, cols), before, inside, down, my_tc),
            (first, slice(0, cols), after, inside, up, my_tc),
            (final, right, before, left, down, across_core),
            (final, left, before, beyond, down, across_core),
            (first, right, after, left, up, across_core),
            (first, left, after, beyond, up, across_core),
            (every, right, body, left, my_tr, across_core),
            (every, left, body, beyond, my_tr, across_core),
        )
        edges = []
        for k, (r, lanes, to_r, to_lanes, to_tr, to_tc) in enumerate(moves):
            for n, (ref, f) in enumerate(fields):
                source = ref.at[:, r, lanes] if n == 0 else ref.at[r, lanes]
                edges.append(
                    pltpu.make_async_remote_copy(
                        source,
                        pad.at[f, to_r, to_lanes],
                        edge_send.at[3 * k + n],
                        edge_recv.at[3 * k + n],
                        device_id={"tr": to_tr, "tc": to_tc},
                        device_id_type=MESH,
                    )
                )
        for copy in edges:
            copy.start()
        for copy in local:
            copy.wait()
        for copy in edges:
            copy.wait_recv()

        def along(base, begin, end, count, curved):
            def body(g, carry):
                source = pl.ds(pl.multiple_of(base + g * SUB, SUB), SUB)
                r = pl.ds(pl.multiple_of(g * SUB, SUB), SUB)
                for f in range(count):
                    for j in range(cols // wide):
                        width = wide + 2 * LANES
                        x = pad[f, source, j * wide : j * wide + width]
                        roll = lambda k: pltpu.roll(x, k % width, 1)[:, LANES : LANES + wide]
                        m2, m1, p1, p2 = roll(2), roll(1), roll(-1), roll(-2)
                        here = slice(j * wide, (j + 1) * wide)
                        slope[f, r, here] = ((m2 - p2) + 8.0 * (p1 - m1)) * (1.0 / 12.0)
                        if curved:
                            centre = x[:, LANES : LANES + wide]
                            bend[f, r, here] = (16.0 * (m1 + p1) - (m2 + p2) - 30.0 * centre) * (
                                1.0 / 12.0
                            )
                return carry

            lax.fori_loop(begin, end, body, 0)

        def at(ref, f, g, k, lanes):
            return ref[f, SUB * (g + 1) + k : SUB * (g + 2) + k, lanes]

        def slant(ref, f, g, lanes):
            return (
                (at(ref, f, g, -2, lanes) - at(ref, f, g, 2, lanes))
                + 8.0 * (at(ref, f, g, 1, lanes) - at(ref, f, g, -1, lanes))
            ) * (1.0 / 12.0)

        def tangents(window, g, count, outer_lanes, inner_lanes):
            ga = [slant(window, f, g, outer_lanes) for f in range(count)]
            gb = [at(slope, f, g, 0, inner_lanes) for f in range(count)]
            ta = (1.0 + ga[0], ga[1], ga[2])
            tb = (gb[0], 1.0 + gb[1], gb[2])
            n = (
                ta[1] * tb[2] - ta[2] * tb[1],
                ta[2] * tb[0] - ta[0] * tb[2],
                ta[0] * tb[1] - ta[1] * tb[0],
            )
            inv = 1.0 / jnp.sqrt(n[0] * n[0] + n[1] * n[1] + n[2] * n[2])
            return ga, gb, ta, tb, n, inv

        def lanes_of(j):
            return (
                pl.ds(pl.multiple_of(j * chunk, LANES), chunk),
                pl.ds(pl.multiple_of(j * chunk + LANES, LANES), chunk),
            )

        def omega(i):
            def side(t, carry):
                base = t * half + i * block
                along(base, 1, 1 + groups, 4, False)
                window = pad.at[:, pl.ds(pl.multiple_of(base, SUB), tall), :]

                def across(j, carry):
                    inner_lanes, outer_lanes = lanes_of(j)
                    for g in range(groups):
                        ga, gb, _, _, _, inv = tangents(window, g, 4, outer_lanes, inner_lanes)
                        out = slice(g * SUB, (g + 1) * SUB)
                        whole[i, t, 0, out, inner_lanes] = ga[3] * inv
                        whole[i, t, 1, out, inner_lanes] = gb[3] * inv
                    return carry

                lax.fori_loop(0, cols // chunk, across, 0)
                return carry

            lax.fori_loop(0, tc, side, 0)

        def out_copies(i, t):
            r = pl.ds(pl.multiple_of(t * half + i * block, SUB), block)
            return (
                pltpu.make_async_copy(unit_buf.at[t], unit_ref.at[:, r, :], unit_sem.at[t]),
                pltpu.make_async_copy(base_buf.at[t], base_ref.at[r, :], base_sem.at[t]),
            )

        def geometry(i):
            def side(t, carry):
                base = t * half + i * block
                along(base, 0, tall // SUB, 3, True)
                window = pad.at[:, pl.ds(pl.multiple_of(base, SUB), tall), :]

                @pl.when(i > 0)
                def _():
                    for copy in out_copies(i, t):
                        copy.wait()

                def across(j, carry):
                    inner_lanes, outer_lanes = lanes_of(j)
                    for g in range(groups):
                        _, _, ta, tb, n, inv = tangents(window, g, 3, outer_lanes, inner_lanes)
                        out = slice(g * SUB, (g + 1) * SUB)
                        unit = [v * inv for v in n]
                        for f in range(3):
                            unit_buf[t, f, out, inner_lanes] = unit[f]
                        big_e = ta[0] * ta[0] + ta[1] * ta[1] + ta[2] * ta[2]
                        big_f = ta[0] * tb[0] + ta[1] * tb[1] + ta[2] * tb[2]
                        big_g = tb[0] * tb[0] + tb[1] * tb[1] + tb[2] * tb[2]
                        sl = sm = sn = None
                        for f in range(3):
                            centre = at(window, f, g, 0, outer_lanes)
                            aa = (
                                16.0
                                * (
                                    at(window, f, g, -1, outer_lanes)
                                    + at(window, f, g, 1, outer_lanes)
                                )
                                - (
                                    at(window, f, g, -2, outer_lanes)
                                    + at(window, f, g, 2, outer_lanes)
                                )
                                - 30.0 * centre
                            ) * (1.0 / 12.0)
                            sl = plus(sl, aa * unit[f])
                            sm = plus(sm, slant(slope, f, g, inner_lanes) * unit[f])
                            sn = plus(sn, at(bend, f, g, 0, inner_lanes) * unit[f])
                        curvature = (big_e * sn - 2.0 * big_f * sm + big_g * sl) * (0.5 * inv * inv)
                        base_buf[t, out, inner_lanes] = (
                            -0.5 * at(window, 2, g, 0, outer_lanes) + 0.3 * curvature
                        )
                    return carry

                lax.fori_loop(0, cols // chunk, across, 0)
                for copy in out_copies(i, t):
                    copy.start()
                return carry

            lax.fori_loop(0, tc, side, 0)

        def swap(i):
            return pltpu.make_async_remote_copy(
                whole.at[i, 1 - my_tc],
                whole.at[i, tc],
                swap_send.at[i],
                swap_recv.at[i],
                device_id={"tr": my_tr, "tc": 1 - my_tc},
                device_id_type=MESH,
            )

        def transform(i):
            slots = [jnp.where(my_tc == k, k, tc) for k in range(tc)]

            def part(p, carry):
                def step(g, carry):
                    r = pl.ds(pl.multiple_of(g * SUB, SUB), SUB)
                    for j in range(0, inner, LANES):
                        z = []
                        for l in range(outer):
                            lane = (l % per) * inner + j
                            z.append((whole[i, slots[l // per], p, r, lane : lane + LANES], None))
                        z = butterflies(z, 1.0)
                        for n in range(outer):
                            re, im = z[n]
                            if n:
                                re, im = twist(
                                    z[n],
                                    tw_ref[0, n, :, j : j + LANES],
                                    tw_ref[1, n, :, j : j + LANES],
                                    1.0,
                                )
                            if im is None:
                                im = jnp.zeros_like(re)
                            mid[n, r, j : j + LANES] = re
                            mid[n, r, inner + j : inner + j + LANES] = im
                    return carry

                lax.fori_loop(0, block // SUB, step, 0)

                def finish(n, carry):
                    some = pl.ds(n * span, span)
                    x = mid[some].reshape(span * block, 2 * inner)
                    y = product(split(x), (m_ref[0], m_ref[1]))
                    stage[i, some, 0, p] = y[:, :kept].reshape(span, block, kept)
                    stage[i, some, 1, p] = y[:, kept:].reshape(span, block, kept)
                    return carry

                lax.fori_loop(0, outer // span, finish, 0)
                return carry

            lax.fori_loop(0, 2, part, 0)

        def keep(i):
            r = pl.ds(pl.multiple_of(i * block, SUB), block)
            return pltpu.make_async_copy(
                stage.at[i, me], spec_ref.at[me, :, :, r, :], keep_sem.at[i]
            )

        def send(i):
            r = pl.ds(pl.multiple_of(i * block, SUB), block)
            for d in range(1, peers):
                q = me ^ d
                pltpu.make_async_remote_copy(
                    stage.at[i, q],
                    spec_ref.at[me, :, :, r, :],
                    send_sem.at[d],
                    recv_sem.at[d],
                    device_id={"tr": q // tc, "tc": q % tc},
                    device_id_type=MESH,
                ).start()
            keep(i).start()

        def turn(i, carry):
            @pl.when(i < steps)
            def _():
                omega(i)
                swap(i).start()

            @pl.when(i > 0)
            def _():
                geometry(i - 1)

            @pl.when(i < steps)
            def _():
                swap(i).wait_recv()
                transform(i)
                send(i)

            return carry

        lax.fori_loop(0, steps + 1, turn, 0)
        for copy in edges:
            copy.wait_send()
        for t in range(tc):
            for copy in out_copies(steps - 1, t):
                copy.wait()

        def settle(i, carry):
            swap(i).wait_send()
            keep(i).wait()
            return carry

        lax.fori_loop(0, steps, settle, 0)
        for d in range(1, peers):
            q = me ^ d
            copy = pltpu.make_async_remote_copy(
                spec_ref.at[q],
                spec_ref.at[q],
                send_sem.at[d],
                recv_sem.at[d],
                device_id={"tr": q // tc, "tc": q % tc},
                device_id_type=MESH,
            )
            copy.wait_send()
            copy.wait_recv()

    f32 = lambda *dims: jax.ShapeDtypeStruct(dims, jnp.float32)
    anywhere = pl.BlockSpec(memory_space=pl.ANY)
    inside = pl.BlockSpec(memory_space=pltpu.VMEM)
    dma = pltpu.SemaphoreType.DMA
    return pl.pallas_call(
        kernel,
        in_specs=[anywhere] * 3 + [inside] * 2,
        out_specs=[anywhere] * 3,
        out_shape=(f32(peers, 2, 2, half, kept), f32(3, rows, cols), f32(rows, cols)),
        scratch_shapes=[
            pltpu.VMEM((4, full, cols + 2 * LANES), jnp.float32),
            pltpu.VMEM((4, tall, cols), jnp.float32),
            pltpu.VMEM((3, tall, cols), jnp.float32),
            pltpu.VMEM((steps, tc + 1, 2, block, cols), jnp.float32),
            pltpu.VMEM((outer, block, 2 * inner), jnp.float32),
            pltpu.VMEM((steps, outer, 2, 2, block, kept), jnp.float32),
            pltpu.VMEM((tc, 3, block, cols), jnp.float32),
            pltpu.VMEM((tc, block, cols), jnp.float32),
            dma((3 * loads,)),
            dma((24,)),
            dma((24,)),
            dma((steps,)),
            dma((steps,)),
            dma((peers,)),
            dma((peers,)),
            dma((steps,)),
            dma((tc,)),
            dma((tc,)),
        ],
        compiler_params=pltpu.CompilerParams(
            vmem_limit_bytes=VMEM_BYTES, collective_id=0, has_side_effects=True
        ),
        name="front",
    )(shift_plane, height, dipole, row_tables(outer, inner, outer * inner), jnp.asarray(matrix))


def ring(axis):
    devices = lax.axis_size(axis)
    up = [(i, (i + 1) % devices) for i in range(devices)]
    return up, [(j, i) for i, j in up]


def exchange(x):
    other = 1 - lax.axis_index("tc")
    sent = lax.dynamic_index_in_dim(x, other, 0, keepdims=True)
    got = lax.ppermute(sent, "tc", ring("tc")[0])
    return lax.dynamic_update_slice_in_dim(x, got, other, 0)


def local_kernels(shift_plane, height, dipole):
    tc = lax.axis_size("tc")
    rows, cols = height.shape
    col_outer, col_inner = factors(cols * tc)
    row_outer, row_inner = factors(rows * lax.axis_size("tr"))
    kept = col_inner // 2
    parts = rows // row_inner
    place = lax.axis_index(("tr", "tc")) * kept + jnp.arange(kept, dtype=jnp.int32)
    freq_two, nyquist_two = wavenumbers(cols * tc, kept, place)
    live_two = jnp.where(nyquist_two, 0.0, 1.0)
    table = column_table(row_outer, row_inner, kept)
    spectra, unit, base = front(shift_plane, height, dipole, col_outer, col_inner)
    partial = column_middle(
        spectra, table, freq_two[None, :], live_two[None, :], row_outer, row_inner, parts
    )
    results = ()
    for part in range(parts):
        block = lax.all_to_all(partial[part], ("tr", "tc"), split_axis=0, concat_axis=0, tiled=True)
        speed = row_inverse(block, col_outer, col_inner, tc)
        speed = exchange(speed)
        results = finish(speed, unit, base, part, parts, results)
    return tuple(results)


def finish(speed, unit, base, part, parts, earlier):
    _, cols = base.shape
    tc, short, _ = speed.shape
    block = min(64, short)
    steps = short // block

    def kernel(s_ref, u_ref, b_ref, *refs):
        v_ref, d_ref = refs[len(earlier) :]
        s = s_ref[0]
        for f in range(3):
            v_ref[f] = s * u_ref[f]
        d_ref[...] = b_ref[...] + 0.5 * s * s

    row = lambda t, j: (t * parts + part) * steps + j
    plane = pl.BlockSpec((block, cols), lambda t, j: (row(t, j), 0))
    triple = pl.BlockSpec((3, block, cols), lambda t, j: (0, row(t, j), 0))
    return pl.pallas_call(
        kernel,
        grid=(tc, steps),
        in_specs=[pl.BlockSpec((1, block, cols), lambda t, j: (t, j, 0)), triple, plane]
        + [pl.BlockSpec(memory_space=pl.ANY)] * len(earlier),
        out_specs=(triple, plane),
        out_shape=(
            jax.ShapeDtypeStruct(unit.shape, jnp.float32),
            jax.ShapeDtypeStruct(base.shape, jnp.float32),
        ),
        input_output_aliases={3 + k: k for k in range(len(earlier))},
        compiler_params=params(),
        name="finish",
    )(speed, unit, base, *earlier)


def fits(rows, cols, tr, tc):
    col_outer, col_inner = factors(cols * tc)
    row_outer, row_inner = factors(rows * tr)
    peers = tr * tc
    return (
        tc == 2
        and col_outer == row_outer == peers == 16
        and col_inner // 2 == LANES
        and rows // tc == row_inner
        and rows % (tc * tc * SUB) == 0
        and rows % (SUB * tc) == 0
        and col_outer % tc == 0
    )


def solution(mesh):
    in_specs = (
        P(None, ("groups", "tr"), "tc"),
        P(("groups", "tr"), "tc"),
        P(("groups", "tr"), "tc"),
    )
    out_specs = (P(None, ("groups", "tr"), "tc"), P(("groups", "tr"), "tc"))

    def chosen(shift_plane, height, dipole):
        rows, cols = height.shape
        if fits(rows, cols, lax.axis_size("tr"), lax.axis_size("tc")):
            return local_kernels(shift_plane, height, dipole)
        return local(shift_plane, height, dipole)

    return jax.shard_map(
        chosen, mesh=mesh, in_specs=in_specs, out_specs=out_specs, check_vma=False
    )
```

```python
import math

import jax
import jax.numpy as jnp
import numpy as np
from jax import lax
from jax.experimental import pallas as pl
from jax.experimental.pallas import tpu as pltpu
from jax.sharding import PartitionSpec as P

largest_wavenumber = lax.Precision.HIGHEST


def padded_2(x, sides, width):
    for axis, dim in sides:
        devices, length = (lax.axis_size(axis), x.shape[dim])
        up = [(i, (i + 1) % devices) for i in range(devices)]
        down = [(j, i) for i, j in up]
        last = lax.slice_in_dim(x, length - width, length, axis=dim)
        initial = lax.slice_in_dim(x, 0, width, axis=dim)
        before = lax.ppermute(last, axis, up)
        after = lax.ppermute(initial, axis, down)
        x = jnp.concatenate([before, x, after], axis=dim)
    return x


def rows_first(field):
    return (
        field[..., :-4, :]
        - 8.0 * field[..., 1:-3, :]
        + 8.0 * field[..., 3:-1, :]
        - field[..., 4:, :]
    ) / 12.0


def cols_first(field):
    return (
        field[..., :-4] - 8.0 * field[..., 1:-3] + 8.0 * field[..., 3:-1] - field[..., 4:]
    ) / 12.0


def rows_second(field):
    return (
        -field[..., :-4, :]
        + 16.0 * field[..., 1:-3, :]
        - 30.0 * field[..., 2:-2, :]
        + 16.0 * field[..., 3:-1, :]
        - field[..., 4:, :]
    ) / 12.0


def second_column_split(field):
    return (
        -field[..., :-4]
        + 16.0 * field[..., 1:-3]
        - 30.0 * field[..., 2:-2]
        + 16.0 * field[..., 3:-1]
        - field[..., 4:]
    ) / 12.0


def surface(grad_a, grad_b, curve_aa, curve_bb, curve_ab):
    tan_a = (1.0 + grad_a[0], grad_a[1], grad_a[2])
    tan_b = (grad_b[0], 1.0 + grad_b[1], grad_b[2])
    normal = (
        tan_a[1] * tan_b[2] - tan_a[2] * tan_b[1],
        tan_a[2] * tan_b[0] - tan_a[0] * tan_b[2],
        tan_a[0] * tan_b[1] - tan_a[1] * tan_b[0],
    )
    area_stretch_factor = jnp.sqrt(
        normal[0] * normal[0] + normal[1] * normal[1] + normal[2] * normal[2]
    )
    unit = (
        normal[0] / area_stretch_factor,
        normal[1] / area_stretch_factor,
        normal[2] / area_stretch_factor,
    )
    first_edge_term = tan_a[0] * tan_a[0] + tan_a[1] * tan_a[1] + tan_a[2] * tan_a[2]
    first_f = tan_a[0] * tan_b[0] + tan_a[1] * tan_b[1] + tan_a[2] * tan_b[2]
    first_g = tan_b[0] * tan_b[0] + tan_b[1] * tan_b[1] + tan_b[2] * tan_b[2]
    second_l = curve_aa[0] * unit[0] + curve_aa[1] * unit[1] + curve_aa[2] * unit[2]
    second_m = curve_ab[0] * unit[0] + curve_ab[1] * unit[1] + curve_ab[2] * unit[2]
    second_n = curve_bb[0] * unit[0] + curve_bb[1] * unit[1] + curve_bb[2] * unit[2]
    curvature = (first_edge_term * second_n - 2.0 * first_f * second_m + first_g * second_l) / (
        2.0 * area_stretch_factor * area_stretch_factor
    )
    omega = (grad_a[3] / area_stretch_factor, grad_b[3] / area_stretch_factor)
    return (unit, curvature, omega)


def factors(length):
    inner = min(length, 256)
    return (length // inner, inner)


def angles(count_one, count_two, modulus):
    sample_lattice = (
        jnp.arange(count_one, dtype=jnp.int32)[:, None]
        * jnp.arange(count_two, dtype=jnp.int32)[None, :]
        % modulus
    )
    theta = sample_lattice.astype(jnp.float32) * (2.0 * math.pi / modulus)
    return (jnp.cos(theta), jnp.sin(theta))


def rotation(cos_table, sin_table, sense):
    top = jnp.stack([cos_table, sense * sin_table])
    low = jnp.stack([-sense * sin_table, cos_table])
    return jnp.stack([top, low])


def twisted(sheet_portion, cos_table, sin_table, sense):
    twist_re = sheet_portion[0] * cos_table + sense * sheet_portion[1] * sin_table
    twist_im = sheet_portion[1] * cos_table - sense * sheet_portion[0] * sin_table
    return jnp.stack([twist_re, twist_im])


def forward(values, length, kept, real_input):
    outer, inner = factors(length)
    cos_outer, sin_outer = angles(outer, outer, outer)
    if real_input:
        leading = values.shape[:-1]
        sample_lattice = values.reshape(leading + (outer, inner))
        lookup_array = jnp.stack([cos_outer, -sin_outer])
        sheet_portion = jnp.einsum(
            "...lm,zln->z...nm", sample_lattice, lookup_array, precision=largest_wavenumber
        )
    else:
        leading = values.shape[1:-1]
        sample_lattice = values.reshape((2,) + leading + (outer, inner))
        sheet_portion = jnp.einsum(
            "s...ab,tsac->t...cb",
            sample_lattice,
            rotation(cos_outer, sin_outer, 1.0),
            precision=largest_wavenumber,
        )
    cos_twist, sin_twist = angles(outer, inner, length)
    sheet_portion = twisted(sheet_portion, cos_twist, sin_twist, 1.0)
    cos_inner, sin_inner = angles(inner, kept, inner)
    result = jnp.einsum(
        "s...cb,tsbd->t...cd",
        sheet_portion,
        rotation(cos_inner, sin_inner, 1.0),
        precision=largest_wavenumber,
    )
    return result.reshape((2,) + leading + (outer * kept,))


def inverse(values, length, kept, want_imag):
    outer, inner = factors(length)
    leading = values.shape[1:-1]
    sample_lattice = values.reshape((2,) + leading + (outer, kept))
    cos_inner, sin_inner = angles(kept, inner, inner)
    sheet_portion = jnp.einsum(
        "s...cd,tsdb->t...cb",
        sample_lattice,
        rotation(cos_inner, sin_inner, -1.0),
        precision=largest_wavenumber,
    )
    cos_twist, sin_twist = angles(outer, inner, length)
    sheet_portion = twisted(sheet_portion, cos_twist, sin_twist, -1.0)
    cos_outer, sin_outer = angles(outer, outer, outer)
    if want_imag:
        result = jnp.einsum(
            "s...cb,tsca->t...ab",
            sheet_portion,
            rotation(cos_outer, sin_outer, -1.0),
            precision=largest_wavenumber,
        )
        return result.reshape((2,) + leading + (length,)) / length
    lookup_array = jnp.stack([cos_outer, -sin_outer])
    result = jnp.einsum(
        "s...cb,sca->...ab", sheet_portion, lookup_array, precision=largest_wavenumber
    )
    return result.reshape(leading + (length,)) / length


def wavenumbers(length, kept, positions):
    outer, inner = factors(length)
    number = positions // kept + outer * (positions % kept)
    signed = jnp.where(number >= length // 2, number - length, number)
    return (signed.astype(jnp.float32) / length, number == length // 2)


def local(shift_plane, height, dipole):
    fields = jnp.concatenate([shift_plane, height[None], dipole[None]], 0)
    padded = padded_2(fields, (("tr", 1), ("tc", 2)), 2)
    grad_a = rows_first(padded)[..., 2:-2]
    grad_b = cols_first(padded)[..., 2:-2, :]
    curve_aa = rows_second(padded[:3])[..., 2:-2]
    curve_bb = second_column_split(padded[:3])[..., 2:-2, :]
    curve_ab = rows_first(cols_first(padded[:3]))
    unit, curvature, omega = surface(grad_a, grad_b, curve_aa, curve_bb, curve_ab)
    vorticity = jnp.stack([omega[0], omega[1]])
    sheet_rows = lax.all_to_all(vorticity, "tc", split_axis=1, concat_axis=2, tiled=True)
    col_count = sheet_rows.shape[-1]
    row_count = height.shape[0] * lax.axis_size("tr")
    col_outer, col_inner = factors(col_count)
    row_outer, row_inner = factors(row_count)
    kept = col_inner // 2
    row_spec = forward(sheet_rows, col_count, kept, True)
    stacked = row_spec.reshape((4,) + row_spec.shape[2:])
    columns = lax.all_to_all(stacked, ("tr", "tc"), split_axis=2, concat_axis=1, tiled=True)
    columns = jnp.swapaxes(columns, 1, 2)
    local_width = columns.shape[1]
    full = forward(columns.reshape((2, 2) + columns.shape[1:]), row_count, row_inner, False)
    complete_real_part = full[0]
    full_im = full[1]
    place = lax.axis_index(("tr", "tc")) * local_width + jnp.arange(local_width, dtype=jnp.int32)
    freq_two, nyquist_two = wavenumbers(col_count, kept, place)
    freq_one, nyquist_one = wavenumbers(
        row_count, row_inner, jnp.arange(row_count, dtype=jnp.int32)
    )
    freq_one = freq_one[None, :]
    freq_two = freq_two[:, None]
    radius = jnp.sqrt(freq_one * freq_one + freq_two * freq_two)
    live = (
        jnp.logical_not(nyquist_one[None, :])
        & jnp.logical_not(nyquist_two[:, None])
        & (radius > 0.0)
    )
    factor = jnp.where(live, 0.5 / jnp.where(live, radius, 1.0), 0.0)
    summed_re = factor * (freq_one * complete_real_part[0] + freq_two * complete_real_part[1])
    summed_im = factor * (freq_one * full_im[0] + freq_two * full_im[1])
    speed_parts = inverse(jnp.stack([summed_im, -summed_re]), row_count, row_inner, True)
    partial_value = jnp.swapaxes(speed_parts, 1, 2)
    back_rows = lax.all_to_all(partial_value, ("tr", "tc"), split_axis=1, concat_axis=2, tiled=True)
    weights = (
        jnp.full((col_outer, kept), 2.0, jnp.float32).at[0, 0].set(1.0).reshape(col_outer * kept)
    )
    speed_rows = inverse(back_rows * weights, col_count, kept, False)
    speed = lax.all_to_all(speed_rows, "tc", split_axis=1, concat_axis=0, tiled=True)
    velocity_update = jnp.stack([speed * unit[0], speed * unit[1], speed * unit[2]])
    dipole_update = -2.0 * 0.5 * 0.5 * height + 0.3 * curvature + 0.5 * speed * speed
    return (velocity_update, dipole_update)


LANES = 128
SUB = 8
VMEM_BYTES = 58 * 1024 * 1024


def params():
    return pltpu.CompilerParams(vmem_limit_bytes=VMEM_BYTES)


def two_halves(table):
    table = np.asarray(table, np.float32)
    high = table.astype(jnp.bfloat16)
    low = (table - high.astype(np.float32)).astype(jnp.bfloat16)
    return np.stack([high, low])


def unit_circle(count_one, count_two, modulus):
    theta = np.arange(count_one)[:, None] * np.arange(count_two)[None, :] % modulus
    theta = theta * (2.0 * math.pi / modulus)
    return np.cos(theta), np.sin(theta)


def split(x):
    high = x.astype(jnp.bfloat16)
    low = (x - high.astype(jnp.float32)).astype(jnp.bfloat16)
    return high, low


def product(a, b):
    dot = lambda p, q: jnp.dot(p, q, preferred_element_type=jnp.float32)
    return dot(a[0], b[0]) + (dot(a[0], b[1]) + dot(a[1], b[0]))


def plus(p, q):
    return q if p is None else p if q is None else p + q


def minus(p, q):
    if q is None:
        return p
    return -q if p is None else p - q


def turned(z, number, size, sense):
    re, im = z
    number = number % size
    if number == 0:
        return z
    if 4 * number == size:
        if sense > 0:
            return (im, None if re is None else -re)
        return (None if im is None else -im, re)
    c = math.cos(2.0 * math.pi * number / size)
    s = -sense * math.sin(2.0 * math.pi * number / size)
    if 8 * number == size:
        r = math.sqrt(0.5)
        if im is None:
            return (re * r, re * (-sense * r))
        if sense > 0:
            return ((re + im) * r, (im - re) * r)
        return ((re - im) * r, (im + re) * r)
    if im is None:
        return (re * c, re * s)
    return (re * c - im * s, re * s + im * c)


def butterflies(z, sense):
    size = len(z)
    if size == 1:
        return z
    even = butterflies(z[0::2], sense)
    odd = butterflies(z[1::2], sense)
    if odd[0] is None:
        return even + even
    odd = [turned(o, k, size, sense) for k, o in enumerate(odd)]
    head = [(plus(e[0], o[0]), plus(e[1], o[1])) for e, o in zip(even, odd)]
    tail = [(minus(e[0], o[0]), minus(e[1], o[1])) for e, o in zip(even, odd)]
    return head + tail


def twist(z, c, s, sense):
    re, im = z
    if im is None:
        return (re * c, re * s * (-sense))
    if sense > 0:
        return (re * c + im * s, im * c - re * s)
    return (re * c - im * s, im * c + re * s)


MESH = pl.DeviceIdType.MESH


def window(ref, start, size):
    return ref.at[pl.ds(pl.multiple_of(start, SUB), size), :]


def mega(shift_plane, height, dipole, outer, inner):
    rows, cols = height.shape
    tr, tc = lax.axis_size("tr"), lax.axis_size("tc")
    peers = tr * tc
    some = peers // 2
    half = rows // tc
    block = min(32, half)
    steps = half // block
    kept = inner // 2
    per = outer // tc
    tall = block + 2 * SUB
    full = rows + 2 * SUB
    strips = cols // LANES
    wide = min(1024, cols)
    groups = block // SUB
    span = 4
    parts = 4
    short = inner // parts
    piece = 4 * block
    slab = 4 * inner
    plane = outer * 4 * inner
    length = outer * inner
    c, s = unit_circle(inner, kept, inner)
    row_matrix = two_halves(np.block([[c, -s], [s, c]]))
    c, s = unit_circle(inner, inner, inner)
    col_matrix = two_halves(np.concatenate([c, s], 0))
    c, s = unit_circle(kept, inner, inner)
    back_matrix = two_halves(np.block([[c, s], [-s, c]]) * (2.0 / length))
    c, s = unit_circle(outer, inner, length)
    row_angles = np.stack([c, s]).astype(np.float32)
    col_angles = np.concatenate([c, s]).T.astype(np.float32)
    loads = 4

    def kernel(
        sp_ref, h_ref, d_ref, row_tw, row_m, col_tw, col_m, back_m,
        speed_ref, unit_ref, base_ref, plain_ref,
        pad, slope, bend, work, mid, stage, unit_buf, base_buf, split_in, back, tw_row, tw_col,
        load_sem, edge_send, edge_recv, swap_send, swap_recv, keep_sem, unit_sem, base_sem,
        split_send, split_recv, plain_send, plain_recv,
        over_send, over_recv, home_send, home_recv, stay_sem, speed_sem, cross_send, cross_recv,
    ):
        my_tr, my_tc = lax.axis_index("tr"), lax.axis_index("tc")
        me = my_tr * tc + my_tc
        mine = me % some
        side = me // some
        opens = side * some
        place = lambda q: {"tr": q // tc, "tc": q % tc}

        def remote(source, target, send, recv, q):
            return pltpu.make_async_remote_copy(
                source, target, send, recv, device_id=place(q), device_id_type=MESH
            )

        fields = ((sp_ref, slice(0, 2)), (h_ref, 2), (d_ref, 3))
        local = []
        for n, (ref, f) in enumerate(fields):
            for q in range(loads):
                r = rows // loads
                source = ref.at[:, q * r : (q + 1) * r] if n == 0 else ref.at[q * r : (q + 1) * r]
                target = pad.at[f, SUB + q * r : SUB + (q + 1) * r, LANES : LANES + cols]
                local.append(pltpu.make_async_copy(source, target, load_sem.at[n * loads + q]))
        for copy in local:
            copy.start()
        barrier = pltpu.get_barrier_semaphore()
        for d in range(1, peers):
            pl.semaphore_signal(barrier, inc=1, device_id=place(me ^ d), device_id_type=MESH)
        pl.semaphore_wait(barrier, peers - 1)

        down, up, other = (my_tr + 1) % tr, (my_tr + tr - 1) % tr, 1 - my_tc
        first, final = slice(0, SUB), slice(rows - SUB, rows)
        left, right = slice(0, LANES), slice(cols - LANES, cols)
        every, body = slice(0, rows), slice(SUB, SUB + rows)
        before, after = slice(0, SUB), slice(SUB + rows, full)
        inside, beyond = slice(LANES, LANES + cols), slice(LANES + cols, 2 * LANES + cols)
        moves = (
            (final, slice(0, cols), before, inside, down, my_tc),
            (first, slice(0, cols), after, inside, up, my_tc),
            (final, right, before, left, down, other),
            (final, left, before, beyond, down, other),
            (first, right, after, left, up, other),
            (first, left, after, beyond, up, other),
            (every, right, body, left, my_tr, other),
            (every, left, body, beyond, my_tr, other),
        )
        edges = []
        for k, (r, lanes, to_r, to_lanes, to_tr, to_tc) in enumerate(moves):
            for n, (ref, f) in enumerate(fields):
                source = ref.at[:, r, lanes] if n == 0 else ref.at[r, lanes]
                at_k = 3 * k + n
                edges.append(
                    remote(
                        source,
                        pad.at[f, to_r, to_lanes],
                        edge_send.at[at_k],
                        edge_recv.at[at_k],
                        to_tr * tc + to_tc,
                    )
                )
        for copy in edges:
            copy.start()

        for t in range(2):
            for n in range(outer):
                tw_row[t, n] = jnp.broadcast_to(row_tw[t, n : n + 1, :], (SUB, inner))

        def fill(g, carry):
            r = pl.ds(pl.multiple_of(g * SUB, SUB), SUB)
            x = col_tw[r, :]
            for k in range(2 * outer):
                tw_col[k, r, :] = jnp.broadcast_to(x[:, k : k + 1], (SUB, kept))
            return carry

        lax.fori_loop(0, inner // SUB, fill, 0)
        for copy in local:
            copy.wait()
        for copy in edges:
            copy.wait_recv()

        def rolls(f, source, j):
            width = wide + 2 * LANES
            x = pad[f, source, j * wide : j * wide + width]
            return x, lambda v, k: pltpu.roll(v, k % width, 1)

        def at(ref, f, g, k, lanes):
            return ref[f, SUB * (g + 1) + k : SUB * (g + 2) + k, lanes]

        def slant(ref, f, g, lanes):
            return 8.0 * (at(ref, f, g, 1, lanes) - at(ref, f, g, -1, lanes)) - (
                at(ref, f, g, 2, lanes) - at(ref, f, g, -2, lanes)
            )

        def cross(ta, tb):
            return (
                ta[1] * tb[2] - ta[2] * tb[1],
                ta[2] * tb[0] - ta[0] * tb[2],
                ta[0] * tb[1] - ta[1] * tb[0],
            )

        def lanes_of(j):
            return (
                pl.ds(pl.multiple_of(j * LANES, LANES), LANES),
                pl.ds(pl.multiple_of(j * LANES + LANES, LANES), LANES),
            )

        def omega(i):
            def one(t, carry):
                base = t * half + i * block

                def along(g, carry):
                    source = pl.ds(pl.multiple_of(base + g * SUB, SUB), SUB)
                    r = pl.ds(pl.multiple_of(g * SUB, SUB), SUB)
                    for f in range(4):
                        for j in range(cols // wide):
                            x, roll = rolls(f, source, j)
                            y = roll(x, -2) - x
                            z = 8.0 * roll(y, 1) - (y + roll(y, 2))
                            slope[f, r, j * wide : (j + 1) * wide] = z[:, LANES : LANES + wide]
                    return carry

                lax.fori_loop(1, 1 + groups, along, 0)
                near = pad.at[:, pl.ds(pl.multiple_of(base, SUB), tall), :]

                def across(j, carry):
                    inner_lanes, outer_lanes = lanes_of(j)
                    for g in range(groups):
                        ga = [slant(near, f, g, outer_lanes) for f in range(4)]
                        gb = [at(slope, f, g, 0, inner_lanes) for f in range(4)]
                        n = cross((12.0 + ga[0], ga[1], ga[2]), (gb[0], 12.0 + gb[1], gb[2]))
                        inv = 12.0 * lax.rsqrt(n[0] * n[0] + n[1] * n[1] + n[2] * n[2])
                        for p, v in enumerate((ga[3], gb[3])):
                            start = (((i * (tc + 1) + t) * 2 + p) * strips + j) * block + g * SUB
                            window(work, start, SUB)[...] = v * inv
                    return carry

                lax.fori_loop(0, strips, across, 0)
                return carry

            lax.fori_loop(0, tc, one, 0)

        def out_copies(i, t):
            r = pl.ds(pl.multiple_of(t * half + i * block, SUB), block)
            return (
                pltpu.make_async_copy(unit_buf.at[t], unit_ref.at[:, r, :], unit_sem.at[t]),
                pltpu.make_async_copy(base_buf.at[t], base_ref.at[r, :], base_sem.at[t]),
            )

        def geometry(i, carry):
            def one(t, carry):
                base = t * half + i * block

                def along(g, carry):
                    source = pl.ds(pl.multiple_of(base + g * SUB, SUB), SUB)
                    r = pl.ds(pl.multiple_of(g * SUB, SUB), SUB)
                    for f in range(3):
                        for j in range(cols // wide):
                            x, roll = rolls(f, source, j)
                            here = slice(LANES, LANES + wide)
                            m2, m1, p1, p2 = (roll(x, k)[:, here] for k in (2, 1, -1, -2))
                            to = slice(j * wide, (j + 1) * wide)
                            slope[f, r, to] = ((m2 - p2) + 8.0 * (p1 - m1)) * (1.0 / 12.0)
                            bend[f, r, to] = (
                                16.0 * (m1 + p1) - (m2 + p2) - 30.0 * x[:, here]
                            ) * (1.0 / 12.0)
                    return carry

                lax.fori_loop(0, tall // SUB, along, 0)
                near = pad.at[:, pl.ds(pl.multiple_of(base, SUB), tall), :]

                @pl.when(i > 0)
                def _():
                    for copy in out_copies(i, t):
                        copy.wait()

                def across(j, carry):
                    inner_lanes, outer_lanes = lanes_of(j)
                    for g in range(groups):
                        ga = [slant(near, f, g, outer_lanes) * (1.0 / 12.0) for f in range(3)]
                        gb = [at(slope, f, g, 0, inner_lanes) for f in range(3)]
                        ta = (1.0 + ga[0], ga[1], ga[2])
                        tb = (gb[0], 1.0 + gb[1], gb[2])
                        n = cross(ta, tb)
                        inv = lax.rsqrt(n[0] * n[0] + n[1] * n[1] + n[2] * n[2])
                        out = slice(g * SUB, (g + 1) * SUB)
                        unit = [v * inv for v in n]
                        for f in range(3):
                            unit_buf[t, f, out, inner_lanes] = unit[f]
                        big_e = ta[0] * ta[0] + ta[1] * ta[1] + ta[2] * ta[2]
                        big_f = ta[0] * tb[0] + ta[1] * tb[1] + ta[2] * tb[2]
                        big_g = tb[0] * tb[0] + tb[1] * tb[1] + tb[2] * tb[2]
                        sl = sm = sn = None
                        for f in range(3):
                            pair = lambda k: (
                                at(near, f, g, -k, outer_lanes) + at(near, f, g, k, outer_lanes)
                            )
                            aa = 16.0 * pair(1) - pair(2) - 30.0 * at(near, f, g, 0, outer_lanes)
                            sl = plus(sl, aa * unit[f])
                            sm = plus(sm, slant(slope, f, g, inner_lanes) * unit[f])
                            sn = plus(sn, at(bend, f, g, 0, inner_lanes) * unit[f])
                        top = big_e * sn + (1.0 / 12.0) * (big_g * sl - 2.0 * big_f * sm)
                        base_buf[t, out, inner_lanes] = (
                            -0.5 * at(near, 2, g, 0, outer_lanes) + top * (0.15 * inv * inv)
                        )
                    return carry

                lax.fori_loop(0, strips, across, 0)
                for copy in out_copies(i, t):
                    copy.start()
                return carry

            lax.fori_loop(0, tc, one, 0)
            return carry

        lump = 2 * strips * block

        def swap(i):
            start = i * (tc + 1)
            return remote(
                window(work, (start + 1 - my_tc) * lump, lump),
                window(work, (start + tc) * lump, lump),
                swap_send.at[i],
                swap_recv.at[i],
                my_tr * tc + 1 - my_tc,
            )

        def transform(i):
            slots = [i * (tc + 1) + jnp.where(my_tc == k, k, tc) for k in range(tc)]

            def part(p, carry):
                def step(g, carry):
                    r = pl.ds(pl.multiple_of(g * SUB, SUB), SUB)
                    for j in range(inner // LANES):
                        lanes = slice(j * LANES, (j + 1) * LANES)
                        z = []
                        for l in range(outer):
                            strip = (l % per) * (inner // LANES) + j
                            start = ((slots[l // per] * 2 + p) * strips + strip) * block + g * SUB
                            z.append((window(work, start, SUB)[...], None))
                        z = butterflies(z, 1.0)
                        for n in range(outer):
                            re, im = z[n]
                            if n:
                                re, im = twist(z[n], tw_row[0, n, :, lanes], tw_row[1, n, :, lanes], 1.0)
                            if im is None:
                                im = jnp.zeros_like(re)
                            mid[n, r, lanes] = re
                            mid[n, r, inner + j * LANES : inner + (j + 1) * LANES] = im
                    return carry

                lax.fori_loop(0, groups, step, 0)

                def close(n, carry):
                    x = mid[pl.ds(n * span, span)].reshape(span * block, 2 * inner)
                    y = product(split(x), (row_m[0], row_m[1]))
                    for k in range(span):
                        for c in range(2):
                            start = (((i * outer + n * span + k) * 2 + c) * 2 + p) * block
                            window(stage, start, block)[...] = y[
                                k * block : (k + 1) * block, c * kept : (c + 1) * kept
                            ]
                    return carry

                lax.fori_loop(0, outer // span, close, 0)
                return carry

            lax.fori_loop(0, 2, part, 0)

        def cut(i, n):
            return window(stage, (i * outer + n) * piece, piece)

        def landing(ref, who, i):
            return window(ref, who * slab + i * piece, piece)

        def keep(i):
            return pltpu.make_async_copy(
                cut(i, 2 * mine + 1), landing(split_in, mine, i), keep_sem.at[i]
            )

        def keep_plain(i):
            return pltpu.make_async_copy(
                cut(i, 2 * my_tr), landing(plain_ref, me, i), stay_sem.at[i]
            )

        def send_plain(i, d):
            j = my_tr ^ d
            remote(
                cut(i, 2 * j),
                landing(plain_ref, me, i),
                plain_send.at[d],
                plain_recv.at[me],
                j * tc,
            ).start()

        def send(i):
            for d in range(1, some):
                remote(
                    cut(i, 2 * (mine ^ d) + 1),
                    landing(split_in, mine, i),
                    split_send.at[d],
                    split_recv.at[mine],
                    me ^ d,
                ).start()
            keep(i).start()

            @pl.when(my_tc == 0)
            def _():
                keep_plain(i).start()

            @pl.when(my_tc != 0)
            def _():
                send_plain(i, 0)

            for d in range(1, tr):
                send_plain(i, d)

        def turn(i, carry):
            @pl.when(i < steps)
            def _():
                omega(i)
                swap(i).start()

            @pl.when(i != 1)
            def _():
                k = jnp.where(i == 0, 0, i - 1)
                swap(k).wait_recv()
                transform(k)
                send(k)

            return carry

        lax.fori_loop(0, steps + 1, turn, 0)

        def columns(x_ref, count, residue, out_ref, out_start, dispatch):
            def fall(g, carry):
                r = pl.ds(pl.multiple_of(g * SUB, SUB), SUB)
                row = (g // groups) * piece + (g % groups) * SUB
                for p in range(2):
                    z = [
                        tuple(
                            window(x_ref, a * slab + row + (2 * c + p) * block, SUB)[...]
                            for c in range(2)
                        )
                        for a in range(count)
                    ] + [None] * (outer - count)
                    z = butterflies(z, 1.0)
                    for k in range(outer):
                        v = z[k]
                        if k:
                            v = twist(v, tw_col[k, r, :], tw_col[outer + k, r, :], 1.0)
                        for c in range(2):
                            start = (k * 4 + 2 * p + c) * inner + g * SUB
                            window(work, start, SUB)[...] = v[c]
                return carry

            lax.fori_loop(0, inner // SUB, fall, 0)
            lane = lax.broadcasted_iota(jnp.int32, (1, kept), 1)
            fre_two = (residue + outer * lane).astype(jnp.float32) * (1.0 / length)
            weights = (col_m[0], col_m[1])

            def spin(k, carry):
                x = [window(work, (k * 4 + b) * inner, inner)[...] for b in range(4)]
                y = product(weights, split(jnp.concatenate(x, 1)))
                both = []
                for p in range(2):
                    lo = slice((2 * p) * kept, (2 * p + 1) * kept)
                    hi = slice((2 * p + 1) * kept, (2 * p + 2) * kept)
                    both.append((y[:inner, lo] + y[inner:, hi], y[:inner, hi] - y[inner:, lo]))
                number = k + outer * lax.broadcasted_iota(jnp.int32, (inner, kept), 0)
                signed = jnp.where(number >= length // 2, number - length, number)
                fre_one = signed.astype(jnp.float32) * (1.0 / length)
                square = fre_one * fre_one + fre_two * fre_two
                live = (number != length // 2) & (square > 0.0)
                factor = jnp.where(live, 0.5 * lax.rsqrt(jnp.where(live, square, 1.0)), 0.0)
                one = factor * fre_one
                two = factor * fre_two
                sum_re = one * both[0][0] + two * both[1][0]
                sum_im = one * both[0][1] + two * both[1][1]
                y = product(weights, split(jnp.concatenate([sum_im, -sum_re], 1)))
                window(work, k * 4 * inner, inner)[...] = y[:inner, :kept] - y[inner:, kept:]
                window(work, (k * 4 + 1) * inner, inner)[...] = y[:inner, kept:] + y[inner:, :kept]
                return carry

            lax.fori_loop(0, outer, spin, 0)

            def leave(h, carry):
                def rise(g, carry):
                    row = h * short + g * SUB
                    r = pl.ds(pl.multiple_of(row, SUB), SUB)
                    z = []
                    for k in range(outer):
                        v = tuple(
                            window(work, (k * 4 + c) * inner + row, SUB)[...] for c in range(2)
                        )
                        if k:
                            v = twist(v, tw_col[k, r, :], tw_col[outer + k, r, :], -1.0)
                        z.append(v)
                    z = butterflies(z, -1.0)
                    for a in range(outer):
                        for c in range(2):
                            start = out_start + ((a * parts + h) * 2 + c) * short + g * SUB
                            window(out_ref, start, SUB)[...] = z[a][c] * (1.0 / length)
                    return carry

                lax.fori_loop(0, short // SUB, rise, 0)
                dispatch(h)
                return carry

            lax.fori_loop(0, parts, leave, 0)

        def slot(n, h):
            return window(back, (n * parts + h) * 2 * short, 2 * short)

        split_slot = tr + side * some + mine
        plain_slot = my_tr

        def over(h, d):
            q = me ^ d
            a = q ^ opens
            return remote(
                window(work, plane + (a * parts + h) * 2 * short, 2 * short),
                slot(split_slot, h),
                over_send.at[h, d],
                over_recv.at[h, side * some + mine],
                q,
            )

        def over_here(h):
            a = me ^ opens
            return pltpu.make_async_copy(
                window(work, plane + (a * parts + h) * 2 * short, 2 * short),
                slot(split_slot, h),
                over_send.at[h, 0],
            )

        def home(h, d):
            q = me ^ d
            return remote(
                window(split_in, (q * parts + h) * 2 * short, 2 * short),
                slot(plain_slot, h),
                home_send.at[h, d],
                home_recv.at[h, my_tr],
                q,
            )

        def home_here(h):
            return pltpu.make_async_copy(
                window(split_in, (me * parts + h) * 2 * short, 2 * short),
                slot(plain_slot, h),
                home_send.at[h, 0],
            )

        def dispatch_split(h):
            over_here(h).start()
            for d in range(1, peers):
                over(h, d).start()

        def dispatch_plain(h):
            home_here(h).start()
            for d in range(1, peers):
                home(h, d).start()

        for i in range(steps):
            swap(i).wait_send()
            keep(i).wait()

        def arrived(ref, who, sem, send):
            return remote(
                window(ref, who * slab, slab), window(ref, who * slab, slab), send, sem, me ^ 1
            )

        for d in range(1, some):
            arrived(split_in, mine ^ d, split_recv.at[mine ^ d], split_send.at[d]).wait_recv()
        columns(split_in, some, 2 * mine + 1, work, plane, dispatch_split)

        for d in range(1, some):
            arrived(split_in, mine, split_recv.at[mine], split_send.at[d]).wait_send()
        for d in range(1, tr):
            arrived(plain_ref, me, plain_recv.at[me], plain_send.at[d]).wait_send()

        @pl.when(my_tc != 0)
        def _():
            arrived(plain_ref, me, plain_recv.at[me], plain_send.at[0]).wait_send()

        @pl.when(my_tc == 0)
        def _():
            for i in range(steps):
                keep_plain(i).wait()
            for d in range(1, peers):
                arrived(plain_ref, me ^ d, plain_recv.at[me ^ d], plain_send.at[0]).wait_recv()
            copy = pltpu.make_async_copy(plain_ref, stage, stay_sem.at[0])
            copy.start()
            copy.wait()
            columns(stage, outer, 2 * my_tr, split_in, 0, dispatch_plain)

        lax.fori_loop(0, steps, geometry, 0)
        for t in range(tc):
            for copy in out_copies(steps - 1, t):
                copy.wait()
        for copy in edges:
            copy.wait_send()

        roomy = outer * 4 * short

        def spread(h):
            start = roomy + (h * tc + my_tc) * strips * short
            r = pl.ds(pl.multiple_of(my_tc * half + h * short, SUB), short)
            return [
                pltpu.make_async_copy(
                    stage.at[pl.ds(pl.multiple_of(start + j * short, SUB), short), :],
                    speed_ref.at[j, r, :],
                    speed_sem.at[h, j],
                )
                for j in range(strips)
            ]

        def give(h):
            start = roomy + (h * tc + 1 - my_tc) * strips * short
            r = pl.ds(pl.multiple_of(my_tc * half + h * short, SUB), short)
            return [
                remote(
                    stage.at[pl.ds(pl.multiple_of(start + j * short, SUB), short), :],
                    speed_ref.at[j, r, :],
                    cross_send.at[h, j],
                    cross_recv.at[h, j],
                    my_tr * tc + 1 - my_tc,
                )
                for j in range(strips)
            ]

        def inverse(h, carry):
            over_here(h).wait()

            @pl.when(my_tc == 0)
            def _():
                home_here(h).wait()

            for d in range(1, peers):
                n = (side * some + mine) ^ d
                remote(
                    slot(0, h), slot(0, h), over_send.at[h, d], over_recv.at[h, n], me ^ d
                ).wait_recv()
            for d in range(tr):
                n = my_tr ^ d
                copy = remote(
                    slot(0, h), slot(0, h), home_send.at[h, d], home_recv.at[h, n], me ^ 1
                )
                if d:
                    copy.wait_recv()
                else:
                    pl.when(my_tc != 0)(copy.wait_recv)

            lane = lax.broadcasted_iota(jnp.int32, (short, kept), 1)
            weights = (back_m[0], back_m[1])

            def start(j, carry):
                weight = jnp.where((lane == 0) & (j == 0), 0.5, 1.0)
                take = lambda n, c: window(back, ((n * parts + h) * 2 + c) * short, short)[...]
                even = jnp.concatenate([take(j, c) * weight for c in range(2)], 1)
                odd = jnp.concatenate(
                    [take(tr + j, c) + take(tr + some + j, c) for c in range(2)], 1
                )
                y = product(split(jnp.concatenate([even, odd], 0)), weights)
                for k in range(2):
                    for b in range(4):
                        window(stage, ((2 * j + k) * 4 + b) * short, short)[...] = y[
                            k * short : (k + 1) * short, b * LANES : (b + 1) * LANES
                        ]
                return carry

            lax.fori_loop(0, outer // 2, start, 0)

            def step(g, carry):
                for j in range(inner // LANES):
                    lanes = slice(j * LANES, (j + 1) * LANES)
                    z = []
                    for n in range(outer):
                        v = tuple(
                            window(
                                stage,
                                (n * 4 + c * (inner // LANES) + j) * short + g * SUB,
                                SUB,
                            )[...]
                            for c in range(2)
                        )
                        if n:
                            v = twist(v, tw_row[0, n, :, lanes], tw_row[1, n, :, lanes], -1.0)
                        z.append(v)
                    z = butterflies(z, -1.0)
                    for l in range(outer):
                        strip = (l % per) * (inner // LANES) + j
                        at_row = roomy + ((h * tc + l // per) * strips + strip) * short + g * SUB
                        window(stage, at_row, SUB)[...] = z[l][0]
                return carry

            lax.fori_loop(0, short // SUB, step, 0)
            for copy in spread(h) + give(h):
                copy.start()
            return carry

        lax.fori_loop(0, parts, inverse, 0)

        def settle(h, carry):
            for d in range(1, peers):
                over(h, d).wait_send()

            @pl.when(my_tc == 0)
            def _():
                for d in range(1, peers):
                    home(h, d).wait_send()

            for copy in spread(h):
                copy.wait()
            for copy in give(h):
                copy.wait()
            return carry

        lax.fori_loop(0, parts, settle, 0)

    f32 = lambda *dims: jax.ShapeDtypeStruct(dims, jnp.float32)
    vmem = lambda *dims: pltpu.VMEM(dims, jnp.float32)
    anywhere = pl.BlockSpec(memory_space=pl.ANY)
    near = pl.BlockSpec(memory_space=pltpu.VMEM)
    dma = lambda *dims: pltpu.SemaphoreType.DMA(dims)
    return pl.pallas_call(
        kernel,
        in_specs=[anywhere] * 3 + [near] * 5,
        out_specs=[anywhere] * 4,
        out_shape=(
            f32(strips, rows, LANES),
            f32(3, rows, cols),
            f32(rows, cols),
            f32(peers * slab, kept),
        ),
        scratch_shapes=[
            vmem(4, full, cols + 2 * LANES),
            vmem(4, tall, cols),
            vmem(3, tall, cols),
            vmem(steps * (tc + 1) * lump_rows(strips, block), LANES),
            vmem(outer, block, 2 * inner),
            vmem(steps * outer * piece, LANES),
            vmem(tc, 3, block, cols),
            vmem(tc, block, cols),
            vmem(some * slab, LANES),
            vmem((tr + peers) * 2 * inner, LANES),
            vmem(2, outer, SUB, inner),
            vmem(2 * outer, inner, kept),
            dma(3 * loads),
            dma(24),
            dma(24),
            dma(steps),
            dma(steps),
            dma(steps),
            dma(tc),
            dma(tc),
            dma(some),
            dma(some),
            dma(tr),
            dma(peers),
            dma(parts, peers),
            dma(parts, peers),
            dma(parts, peers),
            dma(parts, tr),
            dma(steps),
            dma(parts, strips),
            dma(parts, strips),
            dma(parts, strips),
        ],
        compiler_params=pltpu.CompilerParams(
            vmem_limit_bytes=66 * 1000 * 1000, collective_id=0, has_side_effects=True
        ),
        name="mega",
    )(
        shift_plane,
        height,
        dipole,
        jnp.asarray(row_angles),
        jnp.asarray(row_matrix),
        jnp.asarray(col_angles),
        jnp.asarray(col_matrix),
        jnp.asarray(back_matrix),
    )


def lump_rows(strips, block):
    return 2 * strips * block


def local_kernels(shift_plane, height, dipole):
    tc = lax.axis_size("tc")
    cols = height.shape[1]
    outer, inner = factors(cols * tc)
    speed, unit, base = mega(shift_plane, height, dipole, outer, inner)[:3]
    return finish(speed, unit, base)


def finish(speed, unit, base):
    rows, cols = base.shape
    block = min(64, rows)

    def kernel(s_ref, u_ref, b_ref, v_ref, d_ref):
        for j in range(cols // LANES):
            lanes = slice(j * LANES, (j + 1) * LANES)
            s = s_ref[j]
            for f in range(3):
                v_ref[f, :, lanes] = s * u_ref[f, :, lanes]
            d_ref[:, lanes] = b_ref[:, lanes] + 0.5 * s * s

    plane = pl.BlockSpec((block, cols), lambda i: (i, 0))
    triple = pl.BlockSpec((3, block, cols), lambda i: (0, i, 0))
    return pl.pallas_call(
        kernel,
        grid=(rows // block,),
        in_specs=[pl.BlockSpec((cols // LANES, block, LANES), lambda i: (0, i, 0)), triple, plane],
        out_specs=(triple, plane),
        out_shape=(
            jax.ShapeDtypeStruct(unit.shape, jnp.float32),
            jax.ShapeDtypeStruct(base.shape, jnp.float32),
        ),
        compiler_params=params(),
        name="finish",
    )(speed, unit, base)


def fits(rows, cols, tr, tc):
    col_outer, col_inner = factors(cols * tc)
    row_outer, row_inner = factors(rows * tr)
    peers = tr * tc
    return (
        tc == 2
        and col_outer == row_outer == peers == 16
        and col_inner // 2 == LANES
        and rows // tc == row_inner
        and rows % (tc * tc * SUB) == 0
        and rows % (SUB * tc) == 0
        and col_outer % tc == 0
    )


def solution(mesh):
    in_specs = (
        P(None, ("groups", "tr"), "tc"),
        P(("groups", "tr"), "tc"),
        P(("groups", "tr"), "tc"),
    )
    out_specs = (P(None, ("groups", "tr"), "tc"), P(("groups", "tr"), "tc"))

    def chosen(shift_plane, height, dipole):
        rows, cols = height.shape
        if fits(rows, cols, lax.axis_size("tr"), lax.axis_size("tc")):
            return local_kernels(shift_plane, height, dipole)
        return local(shift_plane, height, dipole)

    step = jax.shard_map(
        chosen, mesh=mesh, in_specs=in_specs, out_specs=out_specs, check_vma=False
    )
    return step
```

```python
import math

import jax
import jax.numpy as jnp
import numpy as np
from jax import lax
from jax.experimental import pallas as pl
from jax.experimental.pallas import tpu as pltpu
from jax.sharding import PartitionSpec as P

largest_wavenumber = lax.Precision.HIGHEST


def padded_2(x, sides, width):
    for axis, dim in sides:
        devices, length = (lax.axis_size(axis), x.shape[dim])
        up = [(i, (i + 1) % devices) for i in range(devices)]
        down = [(j, i) for i, j in up]
        last = lax.slice_in_dim(x, length - width, length, axis=dim)
        initial = lax.slice_in_dim(x, 0, width, axis=dim)
        before = lax.ppermute(last, axis, up)
        after = lax.ppermute(initial, axis, down)
        x = jnp.concatenate([before, x, after], axis=dim)
    return x


def rows_first(field):
    return (
        field[..., :-4, :]
        - 8.0 * field[..., 1:-3, :]
        + 8.0 * field[..., 3:-1, :]
        - field[..., 4:, :]
    ) / 12.0


def cols_first(field):
    return (
        field[..., :-4] - 8.0 * field[..., 1:-3] + 8.0 * field[..., 3:-1] - field[..., 4:]
    ) / 12.0


def rows_second(field):
    return (
        -field[..., :-4, :]
        + 16.0 * field[..., 1:-3, :]
        - 30.0 * field[..., 2:-2, :]
        + 16.0 * field[..., 3:-1, :]
        - field[..., 4:, :]
    ) / 12.0


def second_column_split(field):
    return (
        -field[..., :-4]
        + 16.0 * field[..., 1:-3]
        - 30.0 * field[..., 2:-2]
        + 16.0 * field[..., 3:-1]
        - field[..., 4:]
    ) / 12.0


def surface(grad_a, grad_b, curve_aa, curve_bb, curve_ab):
    tan_a = (1.0 + grad_a[0], grad_a[1], grad_a[2])
    tan_b = (grad_b[0], 1.0 + grad_b[1], grad_b[2])
    normal = (
        tan_a[1] * tan_b[2] - tan_a[2] * tan_b[1],
        tan_a[2] * tan_b[0] - tan_a[0] * tan_b[2],
        tan_a[0] * tan_b[1] - tan_a[1] * tan_b[0],
    )
    area_stretch_factor = jnp.sqrt(
        normal[0] * normal[0] + normal[1] * normal[1] + normal[2] * normal[2]
    )
    unit = (
        normal[0] / area_stretch_factor,
        normal[1] / area_stretch_factor,
        normal[2] / area_stretch_factor,
    )
    first_edge_term = tan_a[0] * tan_a[0] + tan_a[1] * tan_a[1] + tan_a[2] * tan_a[2]
    first_f = tan_a[0] * tan_b[0] + tan_a[1] * tan_b[1] + tan_a[2] * tan_b[2]
    first_g = tan_b[0] * tan_b[0] + tan_b[1] * tan_b[1] + tan_b[2] * tan_b[2]
    second_l = curve_aa[0] * unit[0] + curve_aa[1] * unit[1] + curve_aa[2] * unit[2]
    second_m = curve_ab[0] * unit[0] + curve_ab[1] * unit[1] + curve_ab[2] * unit[2]
    second_n = curve_bb[0] * unit[0] + curve_bb[1] * unit[1] + curve_bb[2] * unit[2]
    curvature = (first_edge_term * second_n - 2.0 * first_f * second_m + first_g * second_l) / (
        2.0 * area_stretch_factor * area_stretch_factor
    )
    omega = (grad_a[3] / area_stretch_factor, grad_b[3] / area_stretch_factor)
    return (unit, curvature, omega)


def factors(length):
    inner = min(length, 256)
    return (length // inner, inner)


def angles(count_one, count_two, modulus):
    sample_lattice = (
        jnp.arange(count_one, dtype=jnp.int32)[:, None]
        * jnp.arange(count_two, dtype=jnp.int32)[None, :]
        % modulus
    )
    theta = sample_lattice.astype(jnp.float32) * (2.0 * math.pi / modulus)
    return (jnp.cos(theta), jnp.sin(theta))


def rotation(cos_table, sin_table, sense):
    top = jnp.stack([cos_table, sense * sin_table])
    low = jnp.stack([-sense * sin_table, cos_table])
    return jnp.stack([top, low])


def twisted(sheet_portion, cos_table, sin_table, sense):
    twist_re = sheet_portion[0] * cos_table + sense * sheet_portion[1] * sin_table
    twist_im = sheet_portion[1] * cos_table - sense * sheet_portion[0] * sin_table
    return jnp.stack([twist_re, twist_im])


def forward(values, length, kept, real_input):
    outer, inner = factors(length)
    cos_outer, sin_outer = angles(outer, outer, outer)
    if real_input:
        leading = values.shape[:-1]
        sample_lattice = values.reshape(leading + (outer, inner))
        lookup_array = jnp.stack([cos_outer, -sin_outer])
        sheet_portion = jnp.einsum(
            "...lm,zln->z...nm", sample_lattice, lookup_array, precision=largest_wavenumber
        )
    else:
        leading = values.shape[1:-1]
        sample_lattice = values.reshape((2,) + leading + (outer, inner))
        sheet_portion = jnp.einsum(
            "s...ab,tsac->t...cb",
            sample_lattice,
            rotation(cos_outer, sin_outer, 1.0),
            precision=largest_wavenumber,
        )
    cos_twist, sin_twist = angles(outer, inner, length)
    sheet_portion = twisted(sheet_portion, cos_twist, sin_twist, 1.0)
    cos_inner, sin_inner = angles(inner, kept, inner)
    result = jnp.einsum(
        "s...cb,tsbd->t...cd",
        sheet_portion,
        rotation(cos_inner, sin_inner, 1.0),
        precision=largest_wavenumber,
    )
    return result.reshape((2,) + leading + (outer * kept,))


def inverse(values, length, kept, want_imag):
    outer, inner = factors(length)
    leading = values.shape[1:-1]
    sample_lattice = values.reshape((2,) + leading + (outer, kept))
    cos_inner, sin_inner = angles(kept, inner, inner)
    sheet_portion = jnp.einsum(
        "s...cd,tsdb->t...cb",
        sample_lattice,
        rotation(cos_inner, sin_inner, -1.0),
        precision=largest_wavenumber,
    )
    cos_twist, sin_twist = angles(outer, inner, length)
    sheet_portion = twisted(sheet_portion, cos_twist, sin_twist, -1.0)
    cos_outer, sin_outer = angles(outer, outer, outer)
    if want_imag:
        result = jnp.einsum(
            "s...cb,tsca->t...ab",
            sheet_portion,
            rotation(cos_outer, sin_outer, -1.0),
            precision=largest_wavenumber,
        )
        return result.reshape((2,) + leading + (length,)) / length
    lookup_array = jnp.stack([cos_outer, -sin_outer])
    result = jnp.einsum(
        "s...cb,sca->...ab", sheet_portion, lookup_array, precision=largest_wavenumber
    )
    return result.reshape(leading + (length,)) / length


def wavenumbers(length, kept, positions):
    outer, inner = factors(length)
    number = positions // kept + outer * (positions % kept)
    signed = jnp.where(number >= length // 2, number - length, number)
    return (signed.astype(jnp.float32) / length, number == length // 2)


def local(shift_plane, height, dipole):
    fields = jnp.concatenate([shift_plane, height[None], dipole[None]], 0)
    padded = padded_2(fields, (("tr", 1), ("tc", 2)), 2)
    grad_a = rows_first(padded)[..., 2:-2]
    grad_b = cols_first(padded)[..., 2:-2, :]
    curve_aa = rows_second(padded[:3])[..., 2:-2]
    curve_bb = second_column_split(padded[:3])[..., 2:-2, :]
    curve_ab = rows_first(cols_first(padded[:3]))
    unit, curvature, omega = surface(grad_a, grad_b, curve_aa, curve_bb, curve_ab)
    vorticity = jnp.stack([omega[0], omega[1]])
    sheet_rows = lax.all_to_all(vorticity, "tc", split_axis=1, concat_axis=2, tiled=True)
    col_count = sheet_rows.shape[-1]
    row_count = height.shape[0] * lax.axis_size("tr")
    col_outer, col_inner = factors(col_count)
    row_outer, row_inner = factors(row_count)
    kept = col_inner // 2
    row_spec = forward(sheet_rows, col_count, kept, True)
    stacked = row_spec.reshape((4,) + row_spec.shape[2:])
    columns = lax.all_to_all(stacked, ("tr", "tc"), split_axis=2, concat_axis=1, tiled=True)
    columns = jnp.swapaxes(columns, 1, 2)
    local_width = columns.shape[1]
    full = forward(columns.reshape((2, 2) + columns.shape[1:]), row_count, row_inner, False)
    complete_real_part = full[0]
    full_im = full[1]
    place = lax.axis_index(("tr", "tc")) * local_width + jnp.arange(local_width, dtype=jnp.int32)
    freq_two, nyquist_two = wavenumbers(col_count, kept, place)
    freq_one, nyquist_one = wavenumbers(
        row_count, row_inner, jnp.arange(row_count, dtype=jnp.int32)
    )
    freq_one = freq_one[None, :]
    freq_two = freq_two[:, None]
    radius = jnp.sqrt(freq_one * freq_one + freq_two * freq_two)
    live = (
        jnp.logical_not(nyquist_one[None, :])
        & jnp.logical_not(nyquist_two[:, None])
        & (radius > 0.0)
    )
    factor = jnp.where(live, 0.5 / jnp.where(live, radius, 1.0), 0.0)
    summed_re = factor * (freq_one * complete_real_part[0] + freq_two * complete_real_part[1])
    summed_im = factor * (freq_one * full_im[0] + freq_two * full_im[1])
    speed_parts = inverse(jnp.stack([summed_im, -summed_re]), row_count, row_inner, True)
    partial_value = jnp.swapaxes(speed_parts, 1, 2)
    back_rows = lax.all_to_all(partial_value, ("tr", "tc"), split_axis=1, concat_axis=2, tiled=True)
    weights = (
        jnp.full((col_outer, kept), 2.0, jnp.float32).at[0, 0].set(1.0).reshape(col_outer * kept)
    )
    speed_rows = inverse(back_rows * weights, col_count, kept, False)
    speed = lax.all_to_all(speed_rows, "tc", split_axis=1, concat_axis=0, tiled=True)
    velocity_update = jnp.stack([speed * unit[0], speed * unit[1], speed * unit[2]])
    dipole_update = -2.0 * 0.5 * 0.5 * height + 0.3 * curvature + 0.5 * speed * speed
    return (velocity_update, dipole_update)


LANES = 128
SUB = 8
VMEM_BYTES = 58 * 1024 * 1024


def params():
    return pltpu.CompilerParams(vmem_limit_bytes=VMEM_BYTES)


def two_halves(table):
    table = np.asarray(table, np.float32)
    high = table.astype(jnp.bfloat16)
    low = (table - high.astype(np.float32)).astype(jnp.bfloat16)
    return np.stack([high, low])


def unit_circle(count_one, count_two, modulus):
    theta = np.arange(count_one)[:, None] * np.arange(count_two)[None, :] % modulus
    theta = theta * (2.0 * math.pi / modulus)
    return np.cos(theta), np.sin(theta)


def split(x):
    high = x.astype(jnp.bfloat16)
    low = (x - high.astype(jnp.float32)).astype(jnp.bfloat16)
    return high, low


def product(a, b):
    dot = lambda p, q: jnp.dot(p, q, preferred_element_type=jnp.float32)
    return dot(a[0], b[0]) + (dot(a[0], b[1]) + dot(a[1], b[0]))


def plus(p, q):
    return q if p is None else p if q is None else p + q


def minus(p, q):
    if q is None:
        return p
    return -q if p is None else p - q


def turned(z, number, size, sense):
    re, im = z
    number = number % size
    if number == 0:
        return z
    if 4 * number == size:
        if sense > 0:
            return (im, None if re is None else -re)
        return (None if im is None else -im, re)
    c = math.cos(2.0 * math.pi * number / size)
    s = -sense * math.sin(2.0 * math.pi * number / size)
    if 8 * number == size:
        r = math.sqrt(0.5)
        if im is None:
            return (re * r, re * (-sense * r))
        if sense > 0:
            return ((re + im) * r, (im - re) * r)
        return ((re - im) * r, (im + re) * r)
    if im is None:
        return (re * c, re * s)
    return (re * c - im * s, re * s + im * c)


def butterflies(z, sense):
    size = len(z)
    if size == 1:
        return z
    even = butterflies(z[0::2], sense)
    odd = butterflies(z[1::2], sense)
    if odd[0] is None:
        return even + even
    odd = [turned(o, k, size, sense) for k, o in enumerate(odd)]
    head = [(plus(e[0], o[0]), plus(e[1], o[1])) for e, o in zip(even, odd)]
    tail = [(minus(e[0], o[0]), minus(e[1], o[1])) for e, o in zip(even, odd)]
    return head + tail


def twist(z, c, s, sense):
    re, im = z
    if im is None:
        return (re * c, re * s * (-sense))
    if sense > 0:
        return (re * c + im * s, im * c - re * s)
    return (re * c - im * s, im * c + re * s)


MESH = pl.DeviceIdType.MESH


def window(ref, start, size):
    return ref.at[pl.ds(pl.multiple_of(start, SUB), size), :]


def mega(shift_plane, height, dipole, outer, inner):
    rows, cols = height.shape
    tr, tc = lax.axis_size("tr"), lax.axis_size("tc")
    peers = tr * tc
    some = peers // 2
    half = rows // tc
    block = min(32, half)
    steps = half // block
    kept = inner // 2
    per = outer // tc
    tall = block + 2 * SUB
    full = rows + 2 * SUB
    strips = cols // LANES
    groups = block // SUB
    span = 4
    parts = 4
    short = inner // parts
    piece = 4 * block
    slab = 4 * inner
    plane = outer * 4 * inner
    length = outer * inner
    c, s = unit_circle(inner, kept, inner)
    row_matrix = two_halves(np.block([[c, -s], [s, c]]))
    c, s = unit_circle(inner, inner, inner)
    col_matrix = two_halves(np.concatenate([c, s], 0))
    c, s = unit_circle(kept, inner, inner)
    back_matrix = two_halves(np.block([[c, s], [-s, c]]) * (2.0 / length))
    c, s = unit_circle(outer, inner, length)
    row_angles = np.stack([c, s]).astype(np.float32)
    col_angles = np.concatenate([c, s]).T.astype(np.float32)

    def kernel(
        sp_ref, h_ref, d_ref, row_tw, row_m, col_tw, col_m, back_m,
        speed_ref, unit_ref, base_ref, plain_ref,
        pad, slope, bend, work, mid, stage, unit_buf, base_buf, split_in, back, tw_row, tw_col,
        load_sem, edge_send, edge_recv, side_send, side_recv, swap_send, swap_recv, keep_sem, unit_sem, base_sem,
        split_send, split_recv, plain_send, plain_recv,
        over_send, over_recv, home_send, home_recv, stay_sem, speed_sem, cross_send, cross_recv,
    ):
        my_tr, my_tc = lax.axis_index("tr"), lax.axis_index("tc")
        me = my_tr * tc + my_tc
        mine = me % some
        side = me // some
        opens = side * some
        place = lambda q: {"tr": q // tc, "tc": q % tc}

        def remote(source, target, send, recv, q):
            return pltpu.make_async_remote_copy(
                source, target, send, recv, device_id=place(q), device_id_type=MESH
            )

        fields = ((sp_ref, slice(0, 2)), (h_ref, 2), (d_ref, 3))
        body = slice(SUB, SUB + rows)

        def cell(ref, r, lanes):
            return ref.at[:, r, lanes] if ref is sp_ref else ref.at[r, lanes]

        def strip(j):
            return pl.ds(pl.multiple_of(j * LANES, LANES), LANES)

        def load(j, carry):
            for n, (ref, f) in enumerate(fields):
                source = cell(ref, slice(0, rows), strip(j))
                pltpu.make_async_copy(source, pad.at[f, 1 + j, body, :], load_sem.at[n]).start()
            return carry

        lax.fori_loop(0, strips, load, 0)
        barrier = pltpu.get_barrier_semaphore()
        for d in range(1, peers):
            pl.semaphore_signal(barrier, inc=1, device_id=place(me ^ d), device_id_type=MESH)
        pl.semaphore_wait(barrier, peers - 1)

        down, up, other = (my_tr + 1) % tr, (my_tr + tr - 1) % tr, 1 - my_tc
        first, final = slice(0, SUB), slice(rows - SUB, rows)
        left, right = slice(0, LANES), slice(cols - LANES, cols)
        before, after = slice(0, SUB), slice(SUB + rows, full)
        interior = slice(1, 1 + strips)
        ends = ((final, before, down), (first, after, up))
        corners = tuple(
            (r, lanes, to_r, to_strip, to_tr)
            for r, to_r, to_tr in ends
            for lanes, to_strip in ((right, 0), (left, 1 + strips))
        )

        def edge_wait(region, k):
            return remote(region, region, edge_send.at[k], edge_recv.at[k], me ^ 1)

        def end_wait(k):
            return edge_wait(pad.at[:, interior, ends[k][1], :], k)

        def corner_wait(k):
            _, _, to_r, to_strip, _ = corners[k]
            return edge_wait(pad.at[:, to_strip, to_r, :], 2 + k)

        def side_rows(i, t):
            return t * half + i * block

        def side_wait(i, t, k):
            r = pl.ds(pl.multiple_of(side_rows(i, t) + SUB, SUB), block)
            region = pad.at[:, k * (1 + strips), r, :]
            return remote(
                region, region, side_send.at[i, t, k], side_recv.at[i, t, k], me ^ 1
            )

        def send_ends(j, carry):
            for k, (r, to_r, to_tr) in enumerate(ends):
                for ref, f in fields:
                    remote(
                        cell(ref, r, strip(j)),
                        pad.at[f, 1 + j, to_r, :],
                        edge_send.at[k],
                        edge_recv.at[k],
                        to_tr * tc + my_tc,
                    ).start()
            return carry

        def send_sides(i, carry):
            for t in range(tc):
                start = side_rows(i, t)
                r = pl.ds(pl.multiple_of(start, SUB), block)
                to_r = pl.ds(pl.multiple_of(start + SUB, SUB), block)
                for k, lanes in enumerate((right, left)):
                    for ref, f in fields:
                        remote(
                            cell(ref, r, lanes),
                            pad.at[f, k * (1 + strips), to_r, :],
                            side_send.at[i, t, k],
                            side_recv.at[i, t, k],
                            my_tr * tc + other,
                        ).start()
            return carry

        lax.fori_loop(0, strips, send_ends, 0)
        lax.fori_loop(0, steps, send_sides, 0)
        for k, (r, lanes, to_r, to_strip, to_tr) in enumerate(corners):
            for ref, f in fields:
                remote(
                    cell(ref, r, lanes),
                    pad.at[f, to_strip, to_r, :],
                    edge_send.at[2 + k],
                    edge_recv.at[2 + k],
                    to_tr * tc + other,
                ).start()

        for t in range(2):
            for n in range(outer):
                tw_row[t, n] = jnp.broadcast_to(row_tw[t, n : n + 1, :], (SUB, inner))

        for n, (_, f) in enumerate(fields):
            region = pad.at[f, interior, body, :]
            pltpu.make_async_copy(region, region, load_sem.at[n]).wait()
        for k in range(2):
            end_wait(k).wait_recv()

        def fill(g, carry):
            r = pl.ds(pl.multiple_of(g * SUB, SUB), SUB)
            x = col_tw[r, :]
            for k in range(2 * outer):
                tw_col[k, r, :] = jnp.broadcast_to(x[:, k : k + 1], (SUB, kept))
            return carry

        lane = lax.broadcasted_iota(jnp.int32, (SUB, LANES), 1)

        def ahead(x, n):
            y = [pltpu.roll(v, LANES - n, 1) for v in x]
            return [jnp.where(lane < LANES - n, a, b) for a, b in zip(y, y[1:])]

        def behind(x, n):
            y = [pltpu.roll(v, n, 1) for v in x]
            return [jnp.where(lane < n, a, b) for a, b in zip(y, y[1:])]

        def at(ref, f, g, k):
            return ref[f, SUB * (g + 1) + k : SUB * (g + 2) + k, :]

        def slant(ref, f, g):
            return 8.0 * (at(ref, f, g, 1) - at(ref, f, g, -1)) - (
                at(ref, f, g, 2) - at(ref, f, g, -2)
            )

        def cross(ta, tb):
            return (
                ta[1] * tb[2] - ta[2] * tb[1],
                ta[2] * tb[0] - ta[0] * tb[2],
                ta[0] * tb[1] - ta[1] * tb[0],
            )

        def views(base, j):
            return (
                pad.at[:, 1 + j, pl.ds(pl.multiple_of(base, SUB), tall), :],
                slope.at[:, j],
                bend.at[:, j],
            )

        def omega(i):
            def one(t, carry):
                base = t * half + i * block

                def along(g, carry):
                    source = pl.ds(pl.multiple_of(base + g * SUB, SUB), SUB)
                    r = pl.ds(pl.multiple_of(g * SUB, SUB), SUB)
                    for f in range(4):
                        x = [pad[f, j, source, :] for j in range(strips + 2)]
                        y = [a - v for a, v in zip(ahead(x, 2), x)]
                        one, two = behind(y, 1), behind(y, 2)
                        for j in range(strips):
                            slope[f, j, r, :] = 8.0 * one[j] - (y[j + 1] + two[j])
                    return carry

                lax.fori_loop(1, 1 + groups, along, 0)
                def across(j, carry):
                    near, slopes, bends = views(base, j)
                    for g in range(groups):
                        ga = [slant(near, f, g) for f in range(4)]
                        gb = [at(slopes, f, g, 0) for f in range(4)]
                        n = cross((12.0 + ga[0], ga[1], ga[2]), (gb[0], 12.0 + gb[1], gb[2]))
                        inv = 12.0 * lax.rsqrt(n[0] * n[0] + n[1] * n[1] + n[2] * n[2])
                        for p, v in enumerate((ga[3], gb[3])):
                            start = (((i * (tc + 1) + t) * 2 + p) * strips + j) * block + g * SUB
                            window(work, start, SUB)[...] = v * inv
                    return carry

                lax.fori_loop(0, strips, across, 0)
                return carry

            lax.fori_loop(0, tc, one, 0)

        def out_copies(i, t):
            r = pl.ds(pl.multiple_of(t * half + i * block, SUB), block)
            return (
                pltpu.make_async_copy(unit_buf.at[t], unit_ref.at[:, r, :], unit_sem.at[t]),
                pltpu.make_async_copy(base_buf.at[t], base_ref.at[r, :], base_sem.at[t]),
            )

        def geometry(i, carry):
            def one(t, carry):
                base = t * half + i * block

                def along(g, carry):
                    source = pl.ds(pl.multiple_of(base + g * SUB, SUB), SUB)
                    r = pl.ds(pl.multiple_of(g * SUB, SUB), SUB)
                    for f in range(3):
                        x = [pad[f, j, source, :] for j in range(strips + 2)]
                        p1, p2, m1, m2 = ahead(x, 1), ahead(x, 2), behind(x, 1), behind(x, 2)
                        for j in range(strips):
                            a, b, c, d = m2[j], m1[j], p1[j + 1], p2[j + 1]
                            slope[f, j, r, :] = ((a - d) + 8.0 * (c - b)) * (1.0 / 12.0)
                            bend[f, j, r, :] = (
                                16.0 * (b + c) - (a + d) - 30.0 * x[j + 1]
                            ) * (1.0 / 12.0)
                    return carry

                lax.fori_loop(0, tall // SUB, along, 0)
                @pl.when(i > 0)
                def _():
                    for copy in out_copies(i, t):
                        copy.wait()

                def across(j, carry):
                    near, slopes, bends = views(base, j)
                    for g in range(groups):
                        ga = [slant(near, f, g) * (1.0 / 12.0) for f in range(3)]
                        gb = [at(slopes, f, g, 0) for f in range(3)]
                        ta = (1.0 + ga[0], ga[1], ga[2])
                        tb = (gb[0], 1.0 + gb[1], gb[2])
                        n = cross(ta, tb)
                        inv = lax.rsqrt(n[0] * n[0] + n[1] * n[1] + n[2] * n[2])
                        out = slice(g * SUB, (g + 1) * SUB)
                        unit = [v * inv for v in n]
                        for f in range(3):
                            unit_buf[t, f, out, strip(j)] = unit[f]
                        big_e = ta[0] * ta[0] + ta[1] * ta[1] + ta[2] * ta[2]
                        big_f = ta[0] * tb[0] + ta[1] * tb[1] + ta[2] * tb[2]
                        big_g = tb[0] * tb[0] + tb[1] * tb[1] + tb[2] * tb[2]
                        sl = sm = sn = None
                        for f in range(3):
                            pair = lambda k: (
                                at(near, f, g, -k) + at(near, f, g, k)
                            )
                            aa = 16.0 * pair(1) - pair(2) - 30.0 * at(near, f, g, 0)
                            sl = plus(sl, aa * unit[f])
                            sm = plus(sm, slant(slopes, f, g) * unit[f])
                            sn = plus(sn, at(bends, f, g, 0) * unit[f])
                        top = big_e * sn + (1.0 / 12.0) * (big_g * sl - 2.0 * big_f * sm)
                        base_buf[t, out, strip(j)] = (
                            -0.5 * at(near, 2, g, 0) + top * (0.15 * inv * inv)
                        )
                    return carry

                lax.fori_loop(0, strips, across, 0)
                for copy in out_copies(i, t):
                    copy.start()
                return carry

            lax.fori_loop(0, tc, one, 0)
            return carry

        lump = 2 * strips * block

        def swap(i):
            start = i * (tc + 1)
            return remote(
                window(work, (start + 1 - my_tc) * lump, lump),
                window(work, (start + tc) * lump, lump),
                swap_send.at[i],
                swap_recv.at[i],
                my_tr * tc + 1 - my_tc,
            )

        def transform(i):
            slots = [i * (tc + 1) + jnp.where(my_tc == k, k, tc) for k in range(tc)]

            def part(p, carry):
                def step(g, carry):
                    r = pl.ds(pl.multiple_of(g * SUB, SUB), SUB)
                    for j in range(inner // LANES):
                        lanes = slice(j * LANES, (j + 1) * LANES)
                        z = []
                        for l in range(outer):
                            strip = (l % per) * (inner // LANES) + j
                            start = ((slots[l // per] * 2 + p) * strips + strip) * block + g * SUB
                            z.append((window(work, start, SUB)[...], None))
                        z = butterflies(z, 1.0)
                        for n in range(outer):
                            re, im = z[n]
                            if n:
                                re, im = twist(z[n], tw_row[0, n, :, lanes], tw_row[1, n, :, lanes], 1.0)
                            if im is None:
                                im = jnp.zeros_like(re)
                            mid[n, r, lanes] = re
                            mid[n, r, inner + j * LANES : inner + (j + 1) * LANES] = im
                    return carry

                lax.fori_loop(0, groups, step, 0)

                def close(n, carry):
                    x = mid[pl.ds(n * span, span)].reshape(span * block, 2 * inner)
                    y = product(split(x), (row_m[0], row_m[1]))
                    for k in range(span):
                        for c in range(2):
                            start = (((i * outer + n * span + k) * 2 + c) * 2 + p) * block
                            window(stage, start, block)[...] = y[
                                k * block : (k + 1) * block, c * kept : (c + 1) * kept
                            ]
                    return carry

                lax.fori_loop(0, outer // span, close, 0)
                return carry

            lax.fori_loop(0, 2, part, 0)

        def cut(i, n):
            return window(stage, (i * outer + n) * piece, piece)

        def landing(ref, who, i):
            return window(ref, who * slab + i * piece, piece)

        def keep(i):
            return pltpu.make_async_copy(
                cut(i, 2 * mine + 1), landing(split_in, mine, i), keep_sem.at[i]
            )

        def keep_plain(i):
            return pltpu.make_async_copy(
                cut(i, 2 * my_tr), landing(plain_ref, me, i), stay_sem.at[i]
            )

        def send_plain(i, d):
            j = my_tr ^ d
            remote(
                cut(i, 2 * j),
                landing(plain_ref, me, i),
                plain_send.at[d],
                plain_recv.at[me],
                j * tc,
            ).start()

        def send(i):
            for d in range(1, some):
                remote(
                    cut(i, 2 * (mine ^ d) + 1),
                    landing(split_in, mine, i),
                    split_send.at[d],
                    split_recv.at[mine],
                    me ^ d,
                ).start()
            keep(i).start()

            for d in range(tr // 2, tr):
                send_plain(i, d)

        def send_near(i, carry):
            @pl.when(my_tc == 0)
            def _():
                keep_plain(i).start()

            @pl.when(my_tc != 0)
            def _():
                send_plain(i, 0)

            for d in range(1, tr // 2):
                send_plain(i, d)
            return carry

        def turn(i, carry):
            @pl.when(i < steps)
            def _():
                for t in range(tc):
                    for k in range(2):
                        side_wait(i, t, k).wait_recv()
                omega(i)
                swap(i).start()

            @pl.when(i != 1)
            def _():
                k = jnp.where(i == 0, 0, i - 1)
                swap(k).wait_recv()
                transform(k)
                send(k)

            return carry

        lax.fori_loop(0, steps + 1, turn, 0)
        lax.fori_loop(0, steps, send_near, 0)
        lax.fori_loop(0, inner // SUB, fill, 0)

        def columns(x_ref, count, residue, out_ref, out_start, dispatch):
            def fall(g, carry):
                r = pl.ds(pl.multiple_of(g * SUB, SUB), SUB)
                row = (g // groups) * piece + (g % groups) * SUB
                for p in range(2):
                    z = [
                        tuple(
                            window(x_ref, a * slab + row + (2 * c + p) * block, SUB)[...]
                            for c in range(2)
                        )
                        for a in range(count)
                    ] + [None] * (outer - count)
                    z = butterflies(z, 1.0)
                    for k in range(outer):
                        v = z[k]
                        if k:
                            v = twist(v, tw_col[k, r, :], tw_col[outer + k, r, :], 1.0)
                        for c in range(2):
                            start = (k * 4 + 2 * p + c) * inner + g * SUB
                            window(work, start, SUB)[...] = v[c]
                return carry

            lax.fori_loop(0, inner // SUB, fall, 0)
            lane = lax.broadcasted_iota(jnp.int32, (1, kept), 1)
            fre_two = (residue + outer * lane).astype(jnp.float32) * (1.0 / length)
            weights = (col_m[0], col_m[1])

            def spin(k, carry):
                x = [window(work, (k * 4 + b) * inner, inner)[...] for b in range(4)]
                y = product(weights, split(jnp.concatenate(x, 1)))
                both = []
                for p in range(2):
                    lo = slice((2 * p) * kept, (2 * p + 1) * kept)
                    hi = slice((2 * p + 1) * kept, (2 * p + 2) * kept)
                    both.append((y[:inner, lo] + y[inner:, hi], y[:inner, hi] - y[inner:, lo]))
                number = k + outer * lax.broadcasted_iota(jnp.int32, (inner, kept), 0)
                signed = jnp.where(number >= length // 2, number - length, number)
                fre_one = signed.astype(jnp.float32) * (1.0 / length)
                square = fre_one * fre_one + fre_two * fre_two
                live = (number != length // 2) & (square > 0.0)
                factor = jnp.where(live, 0.5 * lax.rsqrt(jnp.where(live, square, 1.0)), 0.0)
                one = factor * fre_one
                two = factor * fre_two
                sum_re = one * both[0][0] + two * both[1][0]
                sum_im = one * both[0][1] + two * both[1][1]
                y = product(weights, split(jnp.concatenate([sum_im, -sum_re], 1)))
                window(work, k * 4 * inner, inner)[...] = y[:inner, :kept] - y[inner:, kept:]
                window(work, (k * 4 + 1) * inner, inner)[...] = y[:inner, kept:] + y[inner:, :kept]
                return carry

            lax.fori_loop(0, outer, spin, 0)

            def leave(h, carry):
                def rise(g, carry):
                    row = h * short + g * SUB
                    r = pl.ds(pl.multiple_of(row, SUB), SUB)
                    z = []
                    for k in range(outer):
                        v = tuple(
                            window(work, (k * 4 + c) * inner + row, SUB)[...] for c in range(2)
                        )
                        if k:
                            v = twist(v, tw_col[k, r, :], tw_col[outer + k, r, :], -1.0)
                        z.append(v)
                    z = butterflies(z, -1.0)
                    for a in range(outer):
                        for c in range(2):
                            start = out_start + ((a * parts + h) * 2 + c) * short + g * SUB
                            window(out_ref, start, SUB)[...] = z[a][c] * (1.0 / length)
                    return carry

                lax.fori_loop(0, short // SUB, rise, 0)
                dispatch(h)
                return carry

            lax.fori_loop(0, parts, leave, 0)

        def slot(n, h):
            return window(back, (n * parts + h) * 2 * short, 2 * short)

        split_slot = tr + side * some + mine
        plain_slot = my_tr

        def over(h, d):
            q = me ^ d
            a = q ^ opens
            return remote(
                window(work, plane + (a * parts + h) * 2 * short, 2 * short),
                slot(split_slot, h),
                over_send.at[h, d],
                over_recv.at[h, side * some + mine],
                q,
            )

        def over_here(h):
            a = me ^ opens
            return pltpu.make_async_copy(
                window(work, plane + (a * parts + h) * 2 * short, 2 * short),
                slot(split_slot, h),
                over_send.at[h, 0],
            )

        def home(h, d):
            q = me ^ d
            return remote(
                window(split_in, (q * parts + h) * 2 * short, 2 * short),
                slot(plain_slot, h),
                home_send.at[h, d],
                home_recv.at[h, my_tr],
                q,
            )

        def home_here(h):
            return pltpu.make_async_copy(
                window(split_in, (me * parts + h) * 2 * short, 2 * short),
                slot(plain_slot, h),
                home_send.at[h, 0],
            )

        order = [*range(some, peers), *range(1, some)]

        def dispatch_split(h):
            for d in order:
                over(h, d).start()
            over_here(h).start()

        def dispatch_plain(h):
            for d in order:
                home(h, d).start()
            home_here(h).start()

        for i in range(steps):
            swap(i).wait_send()
            keep(i).wait()

        def arrived(ref, who, sem, send):
            return remote(
                window(ref, who * slab, slab), window(ref, who * slab, slab), send, sem, me ^ 1
            )

        for d in range(1, some):
            arrived(split_in, mine ^ d, split_recv.at[mine ^ d], split_send.at[d]).wait_recv()
        columns(split_in, some, 2 * mine + 1, work, plane, dispatch_split)

        for d in range(1, some):
            arrived(split_in, mine, split_recv.at[mine], split_send.at[d]).wait_send()
        for d in range(1, tr):
            arrived(plain_ref, me, plain_recv.at[me], plain_send.at[d]).wait_send()

        @pl.when(my_tc != 0)
        def _():
            arrived(plain_ref, me, plain_recv.at[me], plain_send.at[0]).wait_send()

        @pl.when(my_tc == 0)
        def _():
            for i in range(steps):
                keep_plain(i).wait()
            for d in range(1, peers):
                arrived(plain_ref, me ^ d, plain_recv.at[me ^ d], plain_send.at[0]).wait_recv()
            copy = pltpu.make_async_copy(plain_ref, stage, stay_sem.at[0])
            copy.start()
            copy.wait()
            columns(stage, outer, 2 * my_tr, split_in, 0, dispatch_plain)

        for k in range(4):
            corner_wait(k).wait_recv()
        lax.fori_loop(0, steps, geometry, 0)
        for t in range(tc):
            for copy in out_copies(steps - 1, t):
                copy.wait()
        for k in range(2):
            end_wait(k).wait_send()
        for k in range(4):
            corner_wait(k).wait_send()

        def side_done(i, carry):
            for t in range(tc):
                for k in range(2):
                    side_wait(i, t, k).wait_send()
            return carry

        lax.fori_loop(0, steps, side_done, 0)

        roomy = outer * 4 * short

        def spread(h):
            start = roomy + (h * tc + my_tc) * strips * short
            r = pl.ds(pl.multiple_of(my_tc * half + h * short, SUB), short)
            return [
                pltpu.make_async_copy(
                    stage.at[pl.ds(pl.multiple_of(start + j * short, SUB), short), :],
                    speed_ref.at[j, r, :],
                    speed_sem.at[h, j],
                )
                for j in range(strips)
            ]

        def give(h):
            start = roomy + (h * tc + 1 - my_tc) * strips * short
            r = pl.ds(pl.multiple_of(my_tc * half + h * short, SUB), short)
            return [
                remote(
                    stage.at[pl.ds(pl.multiple_of(start + j * short, SUB), short), :],
                    speed_ref.at[j, r, :],
                    cross_send.at[h, j],
                    cross_recv.at[h, j],
                    my_tr * tc + 1 - my_tc,
                )
                for j in range(strips)
            ]

        def inverse(h, carry):
            over_here(h).wait()

            @pl.when(my_tc == 0)
            def _():
                home_here(h).wait()

            for d in range(1, peers):
                n = (side * some + mine) ^ d
                remote(
                    slot(0, h), slot(0, h), over_send.at[h, d], over_recv.at[h, n], me ^ d
                ).wait_recv()
            for d in range(tr):
                n = my_tr ^ d
                copy = remote(
                    slot(0, h), slot(0, h), home_send.at[h, d], home_recv.at[h, n], me ^ 1
                )
                if d:
                    copy.wait_recv()
                else:
                    pl.when(my_tc != 0)(copy.wait_recv)

            lane = lax.broadcasted_iota(jnp.int32, (short, kept), 1)
            weights = (back_m[0], back_m[1])

            def start(j, carry):
                weight = jnp.where((lane == 0) & (j == 0), 0.5, 1.0)
                take = lambda n, c: window(back, ((n * parts + h) * 2 + c) * short, short)[...]
                even = jnp.concatenate([take(j, c) * weight for c in range(2)], 1)
                odd = jnp.concatenate(
                    [take(tr + j, c) + take(tr + some + j, c) for c in range(2)], 1
                )
                y = product(split(jnp.concatenate([even, odd], 0)), weights)
                for k in range(2):
                    for b in range(4):
                        window(stage, ((2 * j + k) * 4 + b) * short, short)[...] = y[
                            k * short : (k + 1) * short, b * LANES : (b + 1) * LANES
                        ]
                return carry

            lax.fori_loop(0, outer // 2, start, 0)

            def step(g, carry):
                for j in range(inner // LANES):
                    lanes = slice(j * LANES, (j + 1) * LANES)
                    z = []
                    for n in range(outer):
                        v = tuple(
                            window(
                                stage,
                                (n * 4 + c * (inner // LANES) + j) * short + g * SUB,
                                SUB,
                            )[...]
                            for c in range(2)
                        )
                        if n:
                            v = twist(v, tw_row[0, n, :, lanes], tw_row[1, n, :, lanes], -1.0)
                        z.append(v)
                    z = butterflies(z, -1.0)
                    for l in range(outer):
                        strip = (l % per) * (inner // LANES) + j
                        at_row = roomy + ((h * tc + l // per) * strips + strip) * short + g * SUB
                        window(stage, at_row, SUB)[...] = z[l][0]
                return carry

            lax.fori_loop(0, short // SUB, step, 0)
            for copy in spread(h) + give(h):
                copy.start()
            return carry

        lax.fori_loop(0, parts, inverse, 0)

        def settle(h, carry):
            for d in range(1, peers):
                over(h, d).wait_send()

            @pl.when(my_tc == 0)
            def _():
                for d in range(1, peers):
                    home(h, d).wait_send()

            for copy in spread(h):
                copy.wait()
            for copy in give(h):
                copy.wait()
            return carry

        lax.fori_loop(0, parts, settle, 0)

    f32 = lambda *dims: jax.ShapeDtypeStruct(dims, jnp.float32)
    vmem = lambda *dims: pltpu.VMEM(dims, jnp.float32)
    anywhere = pl.BlockSpec(memory_space=pl.ANY)
    near = pl.BlockSpec(memory_space=pltpu.VMEM)
    dma = lambda *dims: pltpu.SemaphoreType.DMA(dims)
    return pl.pallas_call(
        kernel,
        in_specs=[anywhere] * 3 + [near] * 5,
        out_specs=[anywhere] * 4,
        out_shape=(
            f32(strips, rows, LANES),
            f32(3, rows, cols),
            f32(rows, cols),
            f32(peers * slab, kept),
        ),
        scratch_shapes=[
            vmem(4, strips + 2, full, LANES),
            vmem(4, strips, tall, LANES),
            vmem(3, strips, tall, LANES),
            vmem(steps * (tc + 1) * lump_rows(strips, block), LANES),
            vmem(outer, block, 2 * inner),
            vmem(steps * outer * piece, LANES),
            vmem(tc, 3, block, cols),
            vmem(tc, block, cols),
            vmem(some * slab, LANES),
            vmem((tr + peers) * 2 * inner, LANES),
            vmem(2, outer, SUB, inner),
            vmem(2 * outer, inner, kept),
            dma(3),
            dma(6),
            dma(6),
            dma(steps, tc, 2),
            dma(steps, tc, 2),
            dma(steps),
            dma(steps),
            dma(steps),
            dma(tc),
            dma(tc),
            dma(some),
            dma(some),
            dma(tr),
            dma(peers),
            dma(parts, peers),
            dma(parts, peers),
            dma(parts, peers),
            dma(parts, tr),
            dma(steps),
            dma(parts, strips),
            dma(parts, strips),
            dma(parts, strips),
        ],
        compiler_params=pltpu.CompilerParams(
            vmem_limit_bytes=66 * 1000 * 1000, collective_id=0, has_side_effects=True
        ),
        name="mega",
    )(
        shift_plane,
        height,
        dipole,
        jnp.asarray(row_angles),
        jnp.asarray(row_matrix),
        jnp.asarray(col_angles),
        jnp.asarray(col_matrix),
        jnp.asarray(back_matrix),
    )


def lump_rows(strips, block):
    return 2 * strips * block


def local_kernels(shift_plane, height, dipole):
    tc = lax.axis_size("tc")
    cols = height.shape[1]
    outer, inner = factors(cols * tc)
    speed, unit, base = mega(shift_plane, height, dipole, outer, inner)[:3]
    return finish(speed, unit, base)


def finish(speed, unit, base):
    rows, cols = base.shape
    block = min(64, rows)

    def kernel(s_ref, u_ref, b_ref, v_ref, d_ref):
        for j in range(cols // LANES):
            lanes = slice(j * LANES, (j + 1) * LANES)
            s = s_ref[j]
            for f in range(3):
                v_ref[f, :, lanes] = s * u_ref[f, :, lanes]
            d_ref[:, lanes] = b_ref[:, lanes] + 0.5 * s * s

    plane = pl.BlockSpec((block, cols), lambda i: (i, 0))
    triple = pl.BlockSpec((3, block, cols), lambda i: (0, i, 0))
    return pl.pallas_call(
        kernel,
        grid=(rows // block,),
        in_specs=[pl.BlockSpec((cols // LANES, block, LANES), lambda i: (0, i, 0)), triple, plane],
        out_specs=(triple, plane),
        out_shape=(
            jax.ShapeDtypeStruct(unit.shape, jnp.float32),
            jax.ShapeDtypeStruct(base.shape, jnp.float32),
        ),
        compiler_params=params(),
        name="finish",
    )(speed, unit, base)


def fits(rows, cols, tr, tc):
    col_outer, col_inner = factors(cols * tc)
    row_outer, row_inner = factors(rows * tr)
    peers = tr * tc
    return (
        tc == 2
        and col_outer == row_outer == peers == 16
        and col_inner // 2 == LANES
        and rows // tc == row_inner
        and rows % (tc * tc * SUB) == 0
        and rows % (SUB * tc) == 0
        and col_outer % tc == 0
    )


def solution(mesh):
    in_specs = (
        P(None, ("groups", "tr"), "tc"),
        P(("groups", "tr"), "tc"),
        P(("groups", "tr"), "tc"),
    )
    out_specs = (P(None, ("groups", "tr"), "tc"), P(("groups", "tr"), "tc"))

    def chosen(shift_plane, height, dipole):
        rows, cols = height.shape
        if fits(rows, cols, lax.axis_size("tr"), lax.axis_size("tc")):
            return local_kernels(shift_plane, height, dipole)
        return local(shift_plane, height, dipole)

    step = jax.shard_map(
        chosen, mesh=mesh, in_specs=in_specs, out_specs=out_specs, check_vma=False
    )
    return step
```

```python
import math

import jax
import jax.numpy as jnp
import numpy as np
from jax import lax
from jax.experimental import pallas as pl
from jax.experimental.pallas import tpu as pltpu
from jax.sharding import PartitionSpec as P

largest_wavenumber = lax.Precision.HIGHEST


def padded_2(x, sides, width):
    for axis, dim in sides:
        devices, length = (lax.axis_size(axis), x.shape[dim])
        up = [(i, (i + 1) % devices) for i in range(devices)]
        down = [(j, i) for i, j in up]
        last = lax.slice_in_dim(x, length - width, length, axis=dim)
        initial = lax.slice_in_dim(x, 0, width, axis=dim)
        before = lax.ppermute(last, axis, up)
        after = lax.ppermute(initial, axis, down)
        x = jnp.concatenate([before, x, after], axis=dim)
    return x


def rows_first(field):
    return (
        field[..., :-4, :]
        - 8.0 * field[..., 1:-3, :]
        + 8.0 * field[..., 3:-1, :]
        - field[..., 4:, :]
    ) / 12.0


def cols_first(field):
    return (
        field[..., :-4] - 8.0 * field[..., 1:-3] + 8.0 * field[..., 3:-1] - field[..., 4:]
    ) / 12.0


def rows_second(field):
    return (
        -field[..., :-4, :]
        + 16.0 * field[..., 1:-3, :]
        - 30.0 * field[..., 2:-2, :]
        + 16.0 * field[..., 3:-1, :]
        - field[..., 4:, :]
    ) / 12.0


def second_column_split(field):
    return (
        -field[..., :-4]
        + 16.0 * field[..., 1:-3]
        - 30.0 * field[..., 2:-2]
        + 16.0 * field[..., 3:-1]
        - field[..., 4:]
    ) / 12.0


def surface(grad_a, grad_b, curve_aa, curve_bb, curve_ab):
    tan_a = (1.0 + grad_a[0], grad_a[1], grad_a[2])
    tan_b = (grad_b[0], 1.0 + grad_b[1], grad_b[2])
    normal = (
        tan_a[1] * tan_b[2] - tan_a[2] * tan_b[1],
        tan_a[2] * tan_b[0] - tan_a[0] * tan_b[2],
        tan_a[0] * tan_b[1] - tan_a[1] * tan_b[0],
    )
    area_stretch_factor = jnp.sqrt(
        normal[0] * normal[0] + normal[1] * normal[1] + normal[2] * normal[2]
    )
    unit = (
        normal[0] / area_stretch_factor,
        normal[1] / area_stretch_factor,
        normal[2] / area_stretch_factor,
    )
    first_edge_term = tan_a[0] * tan_a[0] + tan_a[1] * tan_a[1] + tan_a[2] * tan_a[2]
    first_f = tan_a[0] * tan_b[0] + tan_a[1] * tan_b[1] + tan_a[2] * tan_b[2]
    first_g = tan_b[0] * tan_b[0] + tan_b[1] * tan_b[1] + tan_b[2] * tan_b[2]
    second_l = curve_aa[0] * unit[0] + curve_aa[1] * unit[1] + curve_aa[2] * unit[2]
    second_m = curve_ab[0] * unit[0] + curve_ab[1] * unit[1] + curve_ab[2] * unit[2]
    second_n = curve_bb[0] * unit[0] + curve_bb[1] * unit[1] + curve_bb[2] * unit[2]
    curvature = (first_edge_term * second_n - 2.0 * first_f * second_m + first_g * second_l) / (
        2.0 * area_stretch_factor * area_stretch_factor
    )
    omega = (grad_a[3] / area_stretch_factor, grad_b[3] / area_stretch_factor)
    return (unit, curvature, omega)


def factors(length):
    inner = min(length, 256)
    return (length // inner, inner)


def angles(count_one, count_two, modulus):
    sample_lattice = (
        jnp.arange(count_one, dtype=jnp.int32)[:, None]
        * jnp.arange(count_two, dtype=jnp.int32)[None, :]
        % modulus
    )
    theta = sample_lattice.astype(jnp.float32) * (2.0 * math.pi / modulus)
    return (jnp.cos(theta), jnp.sin(theta))


def rotation(cos_table, sin_table, sense):
    top = jnp.stack([cos_table, sense * sin_table])
    low = jnp.stack([-sense * sin_table, cos_table])
    return jnp.stack([top, low])


def twisted(sheet_portion, cos_table, sin_table, sense):
    twist_re = sheet_portion[0] * cos_table + sense * sheet_portion[1] * sin_table
    twist_im = sheet_portion[1] * cos_table - sense * sheet_portion[0] * sin_table
    return jnp.stack([twist_re, twist_im])


def forward(values, length, kept, real_input):
    outer, inner = factors(length)
    cos_outer, sin_outer = angles(outer, outer, outer)
    if real_input:
        leading = values.shape[:-1]
        sample_lattice = values.reshape(leading + (outer, inner))
        lookup_array = jnp.stack([cos_outer, -sin_outer])
        sheet_portion = jnp.einsum(
            "...lm,zln->z...nm", sample_lattice, lookup_array, precision=largest_wavenumber
        )
    else:
        leading = values.shape[1:-1]
        sample_lattice = values.reshape((2,) + leading + (outer, inner))
        sheet_portion = jnp.einsum(
            "s...ab,tsac->t...cb",
            sample_lattice,
            rotation(cos_outer, sin_outer, 1.0),
            precision=largest_wavenumber,
        )
    cos_twist, sin_twist = angles(outer, inner, length)
    sheet_portion = twisted(sheet_portion, cos_twist, sin_twist, 1.0)
    cos_inner, sin_inner = angles(inner, kept, inner)
    result = jnp.einsum(
        "s...cb,tsbd->t...cd",
        sheet_portion,
        rotation(cos_inner, sin_inner, 1.0),
        precision=largest_wavenumber,
    )
    return result.reshape((2,) + leading + (outer * kept,))


def inverse(values, length, kept, want_imag):
    outer, inner = factors(length)
    leading = values.shape[1:-1]
    sample_lattice = values.reshape((2,) + leading + (outer, kept))
    cos_inner, sin_inner = angles(kept, inner, inner)
    sheet_portion = jnp.einsum(
        "s...cd,tsdb->t...cb",
        sample_lattice,
        rotation(cos_inner, sin_inner, -1.0),
        precision=largest_wavenumber,
    )
    cos_twist, sin_twist = angles(outer, inner, length)
    sheet_portion = twisted(sheet_portion, cos_twist, sin_twist, -1.0)
    cos_outer, sin_outer = angles(outer, outer, outer)
    if want_imag:
        result = jnp.einsum(
            "s...cb,tsca->t...ab",
            sheet_portion,
            rotation(cos_outer, sin_outer, -1.0),
            precision=largest_wavenumber,
        )
        return result.reshape((2,) + leading + (length,)) / length
    lookup_array = jnp.stack([cos_outer, -sin_outer])
    result = jnp.einsum(
        "s...cb,sca->...ab", sheet_portion, lookup_array, precision=largest_wavenumber
    )
    return result.reshape(leading + (length,)) / length


def wavenumbers(length, kept, positions):
    outer, inner = factors(length)
    number = positions // kept + outer * (positions % kept)
    signed = jnp.where(number >= length // 2, number - length, number)
    return (signed.astype(jnp.float32) / length, number == length // 2)


def local(shift_plane, height, dipole):
    fields = jnp.concatenate([shift_plane, height[None], dipole[None]], 0)
    padded = padded_2(fields, (("tr", 1), ("tc", 2)), 2)
    grad_a = rows_first(padded)[..., 2:-2]
    grad_b = cols_first(padded)[..., 2:-2, :]
    curve_aa = rows_second(padded[:3])[..., 2:-2]
    curve_bb = second_column_split(padded[:3])[..., 2:-2, :]
    curve_ab = rows_first(cols_first(padded[:3]))
    unit, curvature, omega = surface(grad_a, grad_b, curve_aa, curve_bb, curve_ab)
    vorticity = jnp.stack([omega[0], omega[1]])
    sheet_rows = lax.all_to_all(vorticity, "tc", split_axis=1, concat_axis=2, tiled=True)
    col_count = sheet_rows.shape[-1]
    row_count = height.shape[0] * lax.axis_size("tr")
    col_outer, col_inner = factors(col_count)
    row_outer, row_inner = factors(row_count)
    kept = col_inner // 2
    row_spec = forward(sheet_rows, col_count, kept, True)
    stacked = row_spec.reshape((4,) + row_spec.shape[2:])
    columns = lax.all_to_all(stacked, ("tr", "tc"), split_axis=2, concat_axis=1, tiled=True)
    columns = jnp.swapaxes(columns, 1, 2)
    local_width = columns.shape[1]
    full = forward(columns.reshape((2, 2) + columns.shape[1:]), row_count, row_inner, False)
    complete_real_part = full[0]
    full_im = full[1]
    place = lax.axis_index(("tr", "tc")) * local_width + jnp.arange(local_width, dtype=jnp.int32)
    freq_two, nyquist_two = wavenumbers(col_count, kept, place)
    freq_one, nyquist_one = wavenumbers(
        row_count, row_inner, jnp.arange(row_count, dtype=jnp.int32)
    )
    freq_one = freq_one[None, :]
    freq_two = freq_two[:, None]
    radius = jnp.sqrt(freq_one * freq_one + freq_two * freq_two)
    live = (
        jnp.logical_not(nyquist_one[None, :])
        & jnp.logical_not(nyquist_two[:, None])
        & (radius > 0.0)
    )
    factor = jnp.where(live, 0.5 / jnp.where(live, radius, 1.0), 0.0)
    summed_re = factor * (freq_one * complete_real_part[0] + freq_two * complete_real_part[1])
    summed_im = factor * (freq_one * full_im[0] + freq_two * full_im[1])
    speed_parts = inverse(jnp.stack([summed_im, -summed_re]), row_count, row_inner, True)
    partial_value = jnp.swapaxes(speed_parts, 1, 2)
    back_rows = lax.all_to_all(partial_value, ("tr", "tc"), split_axis=1, concat_axis=2, tiled=True)
    weights = (
        jnp.full((col_outer, kept), 2.0, jnp.float32).at[0, 0].set(1.0).reshape(col_outer * kept)
    )
    speed_rows = inverse(back_rows * weights, col_count, kept, False)
    speed = lax.all_to_all(speed_rows, "tc", split_axis=1, concat_axis=0, tiled=True)
    velocity_update = jnp.stack([speed * unit[0], speed * unit[1], speed * unit[2]])
    dipole_update = -2.0 * 0.5 * 0.5 * height + 0.3 * curvature + 0.5 * speed * speed
    return (velocity_update, dipole_update)


LANES = 128
SUB = 8
VMEM_BYTES = 58 * 1024 * 1024


def params():
    return pltpu.CompilerParams(vmem_limit_bytes=VMEM_BYTES)


def two_halves(table):
    table = np.asarray(table, np.float32)
    high = table.astype(jnp.bfloat16)
    low = (table - high.astype(np.float32)).astype(jnp.bfloat16)
    return np.stack([high, low])


def unit_circle(count_one, count_two, modulus):
    theta = np.arange(count_one)[:, None] * np.arange(count_two)[None, :] % modulus
    theta = theta * (2.0 * math.pi / modulus)
    return np.cos(theta), np.sin(theta)


def split(x):
    high = x.astype(jnp.bfloat16)
    low = (x - high.astype(jnp.float32)).astype(jnp.bfloat16)
    return high, low


def product(a, b):
    dot = lambda p, q: jnp.dot(p, q, preferred_element_type=jnp.float32)
    return dot(a[0], b[0]) + (dot(a[0], b[1]) + dot(a[1], b[0]))


def plus(p, q):
    return q if p is None else p if q is None else p + q


def minus(p, q):
    if q is None:
        return p
    return -q if p is None else p - q


def turned(z, number, size, sense):
    re, im = z
    number = number % size
    if number == 0:
        return z
    if 4 * number == size:
        if sense > 0:
            return (im, None if re is None else -re)
        return (None if im is None else -im, re)
    c = math.cos(2.0 * math.pi * number / size)
    s = -sense * math.sin(2.0 * math.pi * number / size)
    if 8 * number == size:
        r = math.sqrt(0.5)
        if im is None:
            return (re * r, re * (-sense * r))
        if sense > 0:
            return ((re + im) * r, (im - re) * r)
        return ((re - im) * r, (im + re) * r)
    if im is None:
        return (re * c, re * s)
    return (re * c - im * s, re * s + im * c)


def butterflies(z, sense):
    size = len(z)
    if size == 1:
        return z
    even = butterflies(z[0::2], sense)
    odd = butterflies(z[1::2], sense)
    if odd[0] is None:
        return even + even
    odd = [turned(o, k, size, sense) for k, o in enumerate(odd)]
    head = [(plus(e[0], o[0]), plus(e[1], o[1])) for e, o in zip(even, odd)]
    tail = [(minus(e[0], o[0]), minus(e[1], o[1])) for e, o in zip(even, odd)]
    return head + tail


def twist(z, c, s, sense):
    re, im = z
    if im is None:
        return (re * c, re * s * (-sense))
    if sense > 0:
        return (re * c + im * s, im * c - re * s)
    return (re * c - im * s, im * c + re * s)


MESH = pl.DeviceIdType.MESH


def window(ref, start, size):
    return ref.at[pl.ds(pl.multiple_of(start, SUB), size), :]


def mega(shift_plane, height, dipole, outer, inner):
    rows, cols = height.shape
    tr, tc = lax.axis_size("tr"), lax.axis_size("tc")
    peers = tr * tc
    some = peers // 2
    half = rows // tc
    block = min(16, half)
    steps = half // block
    lag = steps // 4
    kept = inner // 2
    per = outer // tc
    tall = block + 2 * SUB
    full = rows + 2 * SUB
    strips = cols // LANES
    groups = block // SUB
    span = LANES // block
    parts = 4
    short = inner // parts
    piece = 4 * block
    slab = 4 * inner
    plane = outer * 4 * inner
    length = outer * inner
    c, s = unit_circle(inner, kept, inner)
    row_matrix = two_halves(np.block([[c, -s], [s, c]]))
    c, s = unit_circle(inner, inner, inner)
    fold = np.concatenate([c[: inner // 2 + 1], s[1 : inner // 2]], 0)
    col_matrix = np.stack([two_halves(fold), two_halves(fold.T)])
    c, s = unit_circle(kept, inner, inner)
    back_matrix = two_halves(np.block([[c, s], [-s, c]]) * (2.0 / length))
    c, s = unit_circle(outer, inner, length)
    row_angles = np.stack([c, s]).astype(np.float32)
    col_angles = np.concatenate([c, s]).T.astype(np.float32)

    def kernel(
        sp_ref, h_ref, d_ref, row_tw, row_m, col_tw, col_m, back_m,
        speed_ref, unit_ref, base_ref, plain_ref,
        pad, slope, bend, work, mid, stage, unit_buf, base_buf, split_in, back, tw_row, tw_col,
        load_sem, edge_send, edge_recv, side_send, side_recv, swap_send, swap_recv, keep_sem, unit_sem, base_sem,
        split_send, split_recv, plain_send, plain_recv,
        over_send, over_recv, home_send, home_recv, stay_sem, speed_sem, cross_send, cross_recv,
    ):
        my_tr, my_tc = lax.axis_index("tr"), lax.axis_index("tc")
        me = my_tr * tc + my_tc
        mine = me % some
        side = me // some
        opens = side * some
        few = some // 2
        outermost = (me < few) | (me >= peers - few)
        inner_device = jnp.logical_not(outermost)
        my_plain = (me + few) % some
        place = lambda q: {"tr": q // tc, "tc": q % tc}

        def remote(source, target, send, recv, q):
            return pltpu.make_async_remote_copy(
                source, target, send, recv, device_id=place(q), device_id_type=MESH
            )

        fields = ((sp_ref, slice(0, 2)), (h_ref, 2), (d_ref, 3))
        body = slice(SUB, SUB + rows)

        def cell(ref, r, lanes):
            return ref.at[:, r, lanes] if ref is sp_ref else ref.at[r, lanes]

        def strip(j):
            return pl.ds(pl.multiple_of(j * LANES, LANES), LANES)

        def load(j, carry):
            for n, (ref, f) in enumerate(fields):
                source = cell(ref, slice(0, rows), strip(j))
                pltpu.make_async_copy(source, pad.at[f, 1 + j, body, :], load_sem.at[n]).start()
            return carry

        lax.fori_loop(0, strips, load, 0)
        barrier = pltpu.get_barrier_semaphore()
        for d in range(1, peers):
            pl.semaphore_signal(barrier, inc=1, device_id=place(me ^ d), device_id_type=MESH)
        pl.semaphore_wait(barrier, peers - 1)

        down, up, other = (my_tr + 1) % tr, (my_tr + tr - 1) % tr, 1 - my_tc
        first, final = slice(0, SUB), slice(rows - SUB, rows)
        left, right = slice(0, LANES), slice(cols - LANES, cols)
        before, after = slice(0, SUB), slice(SUB + rows, full)
        interior = slice(1, 1 + strips)
        ends = ((final, before, down), (first, after, up))
        corners = tuple(
            (r, lanes, to_r, to_strip, to_tr)
            for r, to_r, to_tr in ends
            for lanes, to_strip in ((right, 0), (left, 1 + strips))
        )

        def edge_wait(region, k):
            return remote(region, region, edge_send.at[k], edge_recv.at[k], me ^ 1)

        def end_wait(k):
            return edge_wait(pad.at[:, interior, ends[k][1], :], k)

        def corner_wait(k):
            _, _, to_r, to_strip, _ = corners[k]
            return edge_wait(pad.at[:, to_strip, to_r, :], 2 + k)

        def side_rows(i, t):
            return t * half + i * block

        def side_wait(i, t, k):
            r = pl.ds(pl.multiple_of(side_rows(i, t) + SUB, SUB), block)
            region = pad.at[:, k * (1 + strips), r, :]
            return remote(
                region, region, side_send.at[i, t, k], side_recv.at[i, t, k], me ^ 1
            )

        def send_ends(j, carry):
            for k, (r, to_r, to_tr) in enumerate(ends):
                for ref, f in fields:
                    remote(
                        cell(ref, r, strip(j)),
                        pad.at[f, 1 + j, to_r, :],
                        edge_send.at[k],
                        edge_recv.at[k],
                        to_tr * tc + my_tc,
                    ).start()
            return carry

        def send_sides(i, carry):
            for t in range(tc):
                start = side_rows(i, t)
                r = pl.ds(pl.multiple_of(start, SUB), block)
                to_r = pl.ds(pl.multiple_of(start + SUB, SUB), block)
                for k, lanes in enumerate((right, left)):
                    for ref, f in fields:
                        remote(
                            cell(ref, r, lanes),
                            pad.at[f, k * (1 + strips), to_r, :],
                            side_send.at[i, t, k],
                            side_recv.at[i, t, k],
                            my_tr * tc + other,
                        ).start()
            return carry

        lax.fori_loop(0, strips, send_ends, 0)
        lax.fori_loop(0, steps, send_sides, 0)
        for k, (r, lanes, to_r, to_strip, to_tr) in enumerate(corners):
            for ref, f in fields:
                remote(
                    cell(ref, r, lanes),
                    pad.at[f, to_strip, to_r, :],
                    edge_send.at[2 + k],
                    edge_recv.at[2 + k],
                    to_tr * tc + other,
                ).start()

        for t in range(2):
            for n in range(outer):
                tw_row[t, n] = jnp.broadcast_to(row_tw[t, n : n + 1, :], (SUB, inner))

        for n, (_, f) in enumerate(fields):
            region = pad.at[f, interior, body, :]
            pltpu.make_async_copy(region, region, load_sem.at[n]).wait()
        for k in range(2):
            end_wait(k).wait_recv()

        def fill(g, carry):
            r = pl.ds(pl.multiple_of(g * SUB, SUB), SUB)
            x = col_tw[r, :]
            for k in range(2 * outer):
                tw_col[k, r, :] = jnp.broadcast_to(x[:, k : k + 1], (SUB, kept))
            return carry

        lane = lax.broadcasted_iota(jnp.int32, (SUB, LANES), 1)

        def ahead(x, n):
            y = [pltpu.roll(v, LANES - n, 1) for v in x]
            return [jnp.where(lane < LANES - n, a, b) for a, b in zip(y, y[1:])]

        def behind(x, n):
            y = [pltpu.roll(v, n, 1) for v in x]
            return [jnp.where(lane < n, a, b) for a, b in zip(y, y[1:])]

        def at(ref, f, g, k):
            return ref[f, SUB * (g + 1) + k : SUB * (g + 2) + k, :]

        def slant(ref, f, g):
            return 8.0 * (at(ref, f, g, 1) - at(ref, f, g, -1)) - (
                at(ref, f, g, 2) - at(ref, f, g, -2)
            )

        def cross(ta, tb):
            return (
                ta[1] * tb[2] - ta[2] * tb[1],
                ta[2] * tb[0] - ta[0] * tb[2],
                ta[0] * tb[1] - ta[1] * tb[0],
            )

        def views(base, j):
            return (
                pad.at[:, 1 + j, pl.ds(pl.multiple_of(base, SUB), tall), :],
                slope.at[:, j],
                bend.at[:, j],
            )

        def omega(i):
            def one(u, carry):
                t = jnp.where(u == 0, 1 - my_tc, my_tc)
                base = t * half + i * block

                def along(g, carry):
                    source = pl.ds(pl.multiple_of(base + g * SUB, SUB), SUB)
                    r = pl.ds(pl.multiple_of(g * SUB, SUB), SUB)
                    for f in range(4):
                        x = [pad[f, j, source, :] for j in range(strips + 2)]
                        y = [a - v for a, v in zip(ahead(x, 2), x)]
                        one, two = behind(y, 1), behind(y, 2)
                        for j in range(strips):
                            slope[f, j, r, :] = 8.0 * one[j] - (y[j + 1] + two[j])
                    return carry

                lax.fori_loop(1, 1 + groups, along, 0)
                def across(j, carry):
                    near, slopes, bends = views(base, j)
                    for g in range(groups):
                        ga = [slant(near, f, g) for f in range(4)]
                        gb = [at(slopes, f, g, 0) for f in range(4)]
                        n = cross((12.0 + ga[0], ga[1], ga[2]), (gb[0], 12.0 + gb[1], gb[2]))
                        inv = 12.0 * lax.rsqrt(n[0] * n[0] + n[1] * n[1] + n[2] * n[2])
                        for p, v in enumerate((ga[3], gb[3])):
                            start = (((i * (tc + 1) + t) * 2 + p) * strips + j) * block + g * SUB
                            window(work, start, SUB)[...] = v * inv
                    return carry

                lax.fori_loop(0, strips, across, 0, unroll=2)

                @pl.when(u == 0)
                def _():
                    swap(i).start()

                return carry

            lax.fori_loop(0, tc, one, 0)

        def out_copies(i, t):
            r = pl.ds(pl.multiple_of(t * half + i * block, SUB), block)
            return (
                pltpu.make_async_copy(unit_buf.at[t], unit_ref.at[:, r, :], unit_sem.at[t]),
                pltpu.make_async_copy(base_buf.at[t], base_ref.at[r, :], base_sem.at[t]),
            )

        def geometry(i, carry):
            def one(t, carry):
                base = t * half + i * block

                def along(g, carry):
                    source = pl.ds(pl.multiple_of(base + g * SUB, SUB), SUB)
                    r = pl.ds(pl.multiple_of(g * SUB, SUB), SUB)
                    for f in range(3):
                        x = [pad[f, j, source, :] for j in range(strips + 2)]
                        p1, p2, m1, m2 = ahead(x, 1), ahead(x, 2), behind(x, 1), behind(x, 2)
                        for j in range(strips):
                            a, b, c, d = m2[j], m1[j], p1[j + 1], p2[j + 1]
                            slope[f, j, r, :] = ((a - d) + 8.0 * (c - b)) * (1.0 / 12.0)
                            bend[f, j, r, :] = (
                                16.0 * (b + c) - (a + d) - 30.0 * x[j + 1]
                            ) * (1.0 / 12.0)
                    return carry

                lax.fori_loop(0, tall // SUB, along, 0)
                @pl.when(i > 0)
                def _():
                    for copy in out_copies(i, t):
                        copy.wait()

                def across(j, carry):
                    near, slopes, bends = views(base, j)
                    for g in range(groups):
                        ga = [slant(near, f, g) * (1.0 / 12.0) for f in range(3)]
                        gb = [at(slopes, f, g, 0) for f in range(3)]
                        ta = (1.0 + ga[0], ga[1], ga[2])
                        tb = (gb[0], 1.0 + gb[1], gb[2])
                        n = cross(ta, tb)
                        inv = lax.rsqrt(n[0] * n[0] + n[1] * n[1] + n[2] * n[2])
                        out = slice(g * SUB, (g + 1) * SUB)
                        unit = [v * inv for v in n]
                        for f in range(3):
                            unit_buf[t, f, out, strip(j)] = unit[f]
                        big_e = ta[0] * ta[0] + ta[1] * ta[1] + ta[2] * ta[2]
                        big_f = ta[0] * tb[0] + ta[1] * tb[1] + ta[2] * tb[2]
                        big_g = tb[0] * tb[0] + tb[1] * tb[1] + tb[2] * tb[2]
                        sl = sm = sn = None
                        for f in range(3):
                            pair = lambda k: (
                                at(near, f, g, -k) + at(near, f, g, k)
                            )
                            aa = 16.0 * pair(1) - pair(2) - 30.0 * at(near, f, g, 0)
                            sl = plus(sl, aa * unit[f])
                            sm = plus(sm, slant(slopes, f, g) * unit[f])
                            sn = plus(sn, at(bends, f, g, 0) * unit[f])
                        top = big_e * sn + (1.0 / 12.0) * (big_g * sl - 2.0 * big_f * sm)
                        base_buf[t, out, strip(j)] = (
                            -0.5 * at(near, 2, g, 0) + top * (0.15 * inv * inv)
                        )
                    return carry

                lax.fori_loop(0, strips, across, 0, unroll=2)
                for copy in out_copies(i, t):
                    copy.start()
                return carry

            lax.fori_loop(0, tc, one, 0)
            return carry

        lump = 2 * strips * block

        def swap(i):
            start = i * (tc + 1)
            return remote(
                window(work, (start + 1 - my_tc) * lump, lump),
                window(work, (start + tc) * lump, lump),
                swap_send.at[i],
                swap_recv.at[i],
                my_tr * tc + 1 - my_tc,
            )

        def transform(i):
            slots = [i * (tc + 1) + jnp.where(my_tc == k, k, tc) for k in range(tc)]

            def part(p, carry):
                def step(g, carry):
                    r = pl.ds(pl.multiple_of(g * SUB, SUB), SUB)
                    for j in range(inner // LANES):
                        lanes = slice(j * LANES, (j + 1) * LANES)
                        z = []
                        for l in range(outer):
                            strip = (l % per) * (inner // LANES) + j
                            start = ((slots[l // per] * 2 + p) * strips + strip) * block + g * SUB
                            z.append((window(work, start, SUB)[...], None))
                        z = butterflies(z, 1.0)
                        for n in range(outer):
                            re, im = z[n]
                            if n:
                                re, im = twist(z[n], tw_row[0, n, :, lanes], tw_row[1, n, :, lanes], 1.0)
                            if im is None:
                                im = jnp.zeros_like(re)
                            mid[n, r, lanes] = re
                            mid[n, r, inner + j * LANES : inner + (j + 1) * LANES] = im
                    return carry

                lax.fori_loop(0, groups, step, 0)

                def close(n, carry):
                    x = mid[pl.ds(n * span, span)].reshape(span * block, 2 * inner)
                    y = product(split(x), (row_m[0], row_m[1]))
                    for k in range(span):
                        for c in range(2):
                            start = (((i * outer + n * span + k) * 2 + c) * 2 + p) * block
                            window(stage, start, block)[...] = y[
                                k * block : (k + 1) * block, c * kept : (c + 1) * kept
                            ]
                    return carry

                lax.fori_loop(0, outer // span, close, 0)
                return carry

            lax.fori_loop(0, 2, part, 0)

        def cut(i, n):
            return window(stage, (i * outer + n) * piece, piece)

        def landing(ref, who, i):
            return window(ref, who * slab + i * piece, piece)

        def keep(i):
            return pltpu.make_async_copy(
                cut(i, 2 * mine + 1), landing(split_in, mine, i), keep_sem.at[i]
            )

        def keep_plain(i):
            return pltpu.make_async_copy(
                cut(i, 2 * my_plain), landing(plain_ref, me, i), stay_sem.at[i]
            )

        def send_plain(i, t, far):
            j = (1 - side if far else side) * few + (me ^ t) % few
            remote(
                cut(i, 2 * j),
                landing(plain_ref, me, i),
                plain_send.at[far * few + t],
                plain_recv.at[me],
                few + j,
            ).start()

        def send(i):
            for d in range(1, some):
                remote(
                    cut(i, 2 * (mine ^ d) + 1),
                    landing(split_in, mine, i),
                    split_send.at[d],
                    split_recv.at[mine],
                    me ^ d,
                ).start()
            keep(i).start()


            @pl.when(inner_device)
            def _():
                send_far(i, 0)

            @pl.when(outermost & (i >= lag))
            def _():
                send_far(i - lag, 0)

        def send_far(i, carry):
            for t in range(few):
                send_plain(i, t, 1)
            return carry

        def send_near(i, carry):
            @pl.when(inner_device)
            def _():
                keep_plain(i).start()

            @pl.when(outermost)
            def _():
                send_plain(i, 0, 0)

            for t in range(1, few):
                send_plain(i, t, 0)
            return carry

        def turn(i, carry):
            @pl.when(i < steps)
            def _():
                for t in range(tc):
                    for k in range(2):
                        side_wait(i, t, k).wait_recv()
                omega(i)

            @pl.when(i != 1)
            def _():
                k = jnp.where(i == 0, 0, i - 1)
                swap(k).wait_recv()
                transform(k)
                send(k)

            return carry

        lax.fori_loop(0, steps + 1, turn, 0)

        @pl.when(outermost)
        def _():
            lax.fori_loop(steps - lag, steps, send_far, 0)

        lax.fori_loop(0, steps, send_near, 0)
        lax.fori_loop(0, inner // SUB, fill, 0)

        def columns(x_ref, count, residue, out_ref, out_start, dispatch):
            def fall(g, carry):
                r = pl.ds(pl.multiple_of(g * SUB, SUB), SUB)
                row = (g // groups) * piece + (g % groups) * SUB
                for p in range(2):
                    z = [
                        tuple(
                            window(x_ref, a * slab + row + (2 * c + p) * block, SUB)[...]
                            for c in range(2)
                        )
                        for a in range(count)
                    ] + [None] * (outer - count)
                    z = butterflies(z, 1.0)
                    for k in range(outer):
                        v = z[k]
                        if k:
                            v = twist(v, tw_col[k, r, :], tw_col[outer + k, r, :], 1.0)
                        for c in range(2):
                            start = (k * 4 + 2 * p + c) * inner + g * SUB
                            window(work, start, SUB)[...] = v[c]
                return carry

            lax.fori_loop(0, inner // SUB, fall, 0)
            lane = lax.broadcasted_iota(jnp.int32, (1, kept), 1)
            fre_two = (residue + outer * lane).astype(jnp.float32) * (1.0 / length)
            mid_row = inner // 2
            row = lax.broadcasted_iota(jnp.int32, (mid_row, kept), 0)
            top_row = lax.broadcasted_iota(jnp.int32, (SUB, kept), 0) == 0

            def headed(a, x):
                return jnp.concatenate([jnp.where(top_row, a[:SUB], x[:SUB]), x[SUB:]], 0)

            zero = jnp.zeros((SUB, kept), jnp.float32)

            def spin(k, carry):
                x = [window(work, (k * 4 + b) * inner, inner)[...] for b in range(4)]
                y = product((col_m[0, 0], col_m[0, 1]), split(jnp.concatenate(x, 1)))
                block_of = lambda t, b: y[
                    t * mid_row : (t + 1) * mid_row, b * kept : (b + 1) * kept
                ]
                rises, falls = [], []
                for p in range(2):
                    c_re, c_im = block_of(0, 2 * p), block_of(0, 2 * p + 1)
                    s_re, s_im = block_of(1, 2 * p), block_of(1, 2 * p + 1)
                    rises.append((c_re + headed(zero, s_im), c_im - headed(zero, s_re)))
                    falls.append((headed(s_re, c_re - s_im), headed(s_im, c_im + s_re)))

                def weighed(signed, both):
                    fre_one = signed.astype(jnp.float32) * (1.0 / length)
                    square = fre_one * fre_one + fre_two * fre_two
                    live = (signed != -(length // 2)) & (square > 0.0)
                    factor = jnp.where(
                        live, (0.5 / length) * lax.rsqrt(jnp.where(live, square, 1.0)), 0.0
                    )
                    one = factor * fre_one
                    two = factor * fre_two
                    return (
                        one * both[0][0] + two * both[1][0],
                        one * both[0][1] + two * both[1][1],
                    )

                a_re, a_im = weighed(k + outer * row, rises)
                b_re, b_im = weighed(
                    k - outer * jnp.where(row == 0, mid_row, row), falls
                )
                w_re = jnp.concatenate([headed(a_im, a_im + b_im), headed(b_im, a_re - b_re)], 0)
                w_im = jnp.concatenate(
                    [headed(-a_re, -a_re - b_re), headed(-b_re, a_im - b_im)], 0
                )
                y = product((col_m[1, 0], col_m[1, 1]), split(jnp.concatenate([w_re, w_im], 1)))
                window(work, k * 4 * inner, inner)[...] = y[:, :kept]
                window(work, (k * 4 + 1) * inner, inner)[...] = y[:, kept:]
                return carry

            lax.fori_loop(0, outer, spin, 0)

            def leave(h, carry):
                def rise(g, carry):
                    row = h * short + g * SUB
                    r = pl.ds(pl.multiple_of(row, SUB), SUB)
                    z = []
                    for k in range(outer):
                        v = tuple(
                            window(work, (k * 4 + c) * inner + row, SUB)[...] for c in range(2)
                        )
                        if k:
                            v = twist(v, tw_col[k, r, :], tw_col[outer + k, r, :], -1.0)
                        z.append(v)
                    z = butterflies(z, -1.0)
                    for a in range(outer):
                        for c in range(2):
                            start = out_start + ((a * parts + h) * 2 + c) * short + g * SUB
                            window(out_ref, start, SUB)[...] = z[a][c]
                    return carry

                lax.fori_loop(0, short // SUB, rise, 0)
                dispatch(h)
                return carry

            lax.fori_loop(0, parts, leave, 0)

        def slot(n, h):
            return window(back, (n * parts + h) * 2 * short, 2 * short)

        split_slot = some + me
        plain_slot = my_plain

        def over(h, d):
            q = me ^ d
            a = q ^ opens
            return remote(
                window(work, plane + (a * parts + h) * 2 * short, 2 * short),
                slot(split_slot, h),
                over_send.at[h, d],
                over_recv.at[h, me],
                q,
            )

        def over_here(h):
            a = me ^ opens
            return pltpu.make_async_copy(
                window(work, plane + (a * parts + h) * 2 * short, 2 * short),
                slot(split_slot, h),
                over_send.at[h, 0],
            )

        def home(h, d):
            q = me ^ d
            return remote(
                window(split_in, (q * parts + h) * 2 * short, 2 * short),
                slot(plain_slot, h),
                home_send.at[h, d],
                home_recv.at[h, my_plain],
                q,
            )

        def home_here(h):
            return pltpu.make_async_copy(
                window(split_in, (me * parts + h) * 2 * short, 2 * short),
                slot(plain_slot, h),
                home_send.at[h, 0],
            )

        order = [*range(some, peers), *range(1, some)]

        def dispatch_split(h):
            for d in order:
                over(h, d).start()
            over_here(h).start()

        def dispatch_plain(h):
            for d in order:
                home(h, d).start()
            home_here(h).start()

        for i in range(steps):
            swap(i).wait_send()
            keep(i).wait()

        def arrived(ref, who, sem, send):
            return remote(
                window(ref, who * slab, slab), window(ref, who * slab, slab), send, sem, me ^ 1
            )

        for d in range(1, some):
            arrived(split_in, mine ^ d, split_recv.at[mine ^ d], split_send.at[d]).wait_recv()
        columns(split_in, some, 2 * mine + 1, work, plane, dispatch_split)

        for d in range(1, some):
            arrived(split_in, mine, split_recv.at[mine], split_send.at[d]).wait_send()
        for d in range(1, some):
            arrived(plain_ref, me, plain_recv.at[me], plain_send.at[d]).wait_send()

        @pl.when(outermost)
        def _():
            arrived(plain_ref, me, plain_recv.at[me], plain_send.at[0]).wait_send()

        @pl.when(inner_device)
        def _():
            for i in range(steps):
                keep_plain(i).wait()
            for d in range(1, peers):
                arrived(plain_ref, me ^ d, plain_recv.at[me ^ d], plain_send.at[0]).wait_recv()
            copy = pltpu.make_async_copy(plain_ref, stage, stay_sem.at[0])
            copy.start()
            copy.wait()
            columns(stage, outer, 2 * my_plain, split_in, 0, dispatch_plain)

        for k in range(4):
            corner_wait(k).wait_recv()
        lax.fori_loop(0, steps, geometry, 0)
        for t in range(tc):
            for copy in out_copies(steps - 1, t):
                copy.wait()
        for k in range(2):
            end_wait(k).wait_send()
        for k in range(4):
            corner_wait(k).wait_send()

        def side_done(i, carry):
            for t in range(tc):
                for k in range(2):
                    side_wait(i, t, k).wait_send()
            return carry

        lax.fori_loop(0, steps, side_done, 0)

        roomy = outer * 4 * short

        def spread(h):
            start = roomy + (h * tc + my_tc) * strips * short
            r = pl.ds(pl.multiple_of(my_tc * half + h * short, SUB), short)
            return [
                pltpu.make_async_copy(
                    stage.at[pl.ds(pl.multiple_of(start + j * short, SUB), short), :],
                    speed_ref.at[j, r, :],
                    speed_sem.at[h, j],
                )
                for j in range(strips)
            ]

        def give(h):
            start = roomy + (h * tc + 1 - my_tc) * strips * short
            r = pl.ds(pl.multiple_of(my_tc * half + h * short, SUB), short)
            return [
                remote(
                    stage.at[pl.ds(pl.multiple_of(start + j * short, SUB), short), :],
                    speed_ref.at[j, r, :],
                    cross_send.at[h, j],
                    cross_recv.at[h, j],
                    my_tr * tc + 1 - my_tc,
                )
                for j in range(strips)
            ]

        def inverse(h, carry):
            over_here(h).wait()

            @pl.when(inner_device)
            def _():
                home_here(h).wait()

            for d in range(1, peers):
                n = me ^ d
                remote(
                    slot(0, h), slot(0, h), over_send.at[h, d], over_recv.at[h, n], me ^ d
                ).wait_recv()
            for d in range(some):
                n = my_plain ^ d
                copy = remote(
                    slot(0, h), slot(0, h), home_send.at[h, d], home_recv.at[h, n], me ^ 1
                )
                if d:
                    copy.wait_recv()
                else:
                    pl.when(outermost)(copy.wait_recv)

            lane = lax.broadcasted_iota(jnp.int32, (short, kept), 1)
            weights = (back_m[0], back_m[1])

            def start(j, carry):
                weight = jnp.where((lane == 0) & (j == 0), 0.5, 1.0)
                take = lambda n, c: window(back, ((n * parts + h) * 2 + c) * short, short)[...]
                even = jnp.concatenate([take(j, c) * weight for c in range(2)], 1)
                odd = jnp.concatenate(
                    [take(some + j, c) + take(2 * some + j, c) for c in range(2)], 1
                )
                y = product(split(jnp.concatenate([even, odd], 0)), weights)
                for k in range(2):
                    for b in range(4):
                        window(stage, ((2 * j + k) * 4 + b) * short, short)[...] = y[
                            k * short : (k + 1) * short, b * LANES : (b + 1) * LANES
                        ]
                return carry

            lax.fori_loop(0, outer // 2, start, 0)

            def step(g, carry):
                for j in range(inner // LANES):
                    lanes = slice(j * LANES, (j + 1) * LANES)
                    z = []
                    for n in range(outer):
                        v = tuple(
                            window(
                                stage,
                                (n * 4 + c * (inner // LANES) + j) * short + g * SUB,
                                SUB,
                            )[...]
                            for c in range(2)
                        )
                        if n:
                            v = twist(v, tw_row[0, n, :, lanes], tw_row[1, n, :, lanes], -1.0)
                        z.append(v)
                    z = butterflies(z, -1.0)
                    for l in range(outer):
                        strip = (l % per) * (inner // LANES) + j
                        at_row = roomy + ((h * tc + l // per) * strips + strip) * short + g * SUB
                        window(stage, at_row, SUB)[...] = z[l][0]
                return carry

            lax.fori_loop(0, short // SUB, step, 0)
            for copy in spread(h) + give(h):
                copy.start()
            return carry

        lax.fori_loop(0, parts, inverse, 0)

        def settle(h, carry):
            for d in range(1, peers):
                over(h, d).wait_send()

            @pl.when(inner_device)
            def _():
                for d in range(1, peers):
                    home(h, d).wait_send()

            for copy in spread(h):
                copy.wait()
            for copy in give(h):
                copy.wait()
            return carry

        lax.fori_loop(0, parts, settle, 0)

    f32 = lambda *dims: jax.ShapeDtypeStruct(dims, jnp.float32)
    vmem = lambda *dims: pltpu.VMEM(dims, jnp.float32)
    anywhere = pl.BlockSpec(memory_space=pl.ANY)
    near = pl.BlockSpec(memory_space=pltpu.VMEM)
    dma = lambda *dims: pltpu.SemaphoreType.DMA(dims)
    return pl.pallas_call(
        kernel,
        in_specs=[anywhere] * 3 + [near] * 5,
        out_specs=[anywhere] * 4,
        out_shape=(
            f32(strips, rows, LANES),
            f32(3, rows, cols),
            f32(rows, cols),
            f32(peers * slab, kept),
        ),
        scratch_shapes=[
            vmem(4, strips + 2, full, LANES),
            vmem(4, strips, tall, LANES),
            vmem(3, strips, tall, LANES),
            vmem(steps * (tc + 1) * lump_rows(strips, block), LANES),
            vmem(outer, block, 2 * inner),
            vmem(steps * outer * piece, LANES),
            vmem(tc, 3, block, cols),
            vmem(tc, block, cols),
            vmem(some * slab, LANES),
            vmem((some + peers) * 2 * inner, LANES),
            vmem(2, outer, SUB, inner),
            vmem(2 * outer, inner, kept),
            dma(3),
            dma(6),
            dma(6),
            dma(steps, tc, 2),
            dma(steps, tc, 2),
            dma(steps),
            dma(steps),
            dma(steps),
            dma(tc),
            dma(tc),
            dma(some),
            dma(some),
            dma(some),
            dma(peers),
            dma(parts, peers),
            dma(parts, peers),
            dma(parts, peers),
            dma(parts, some),
            dma(steps),
            dma(parts, strips),
            dma(parts, strips),
            dma(parts, strips),
        ],
        compiler_params=pltpu.CompilerParams(
            vmem_limit_bytes=66 * 1000 * 1000, collective_id=0, has_side_effects=True
        ),
        name="mega",
    )(
        shift_plane,
        height,
        dipole,
        jnp.asarray(row_angles),
        jnp.asarray(row_matrix),
        jnp.asarray(col_angles),
        jnp.asarray(col_matrix),
        jnp.asarray(back_matrix),
    )


def lump_rows(strips, block):
    return 2 * strips * block


def local_kernels(shift_plane, height, dipole):
    tc = lax.axis_size("tc")
    cols = height.shape[1]
    outer, inner = factors(cols * tc)
    speed, unit, base = mega(shift_plane, height, dipole, outer, inner)[:3]
    return finish(speed, unit, base)


def finish(speed, unit, base):
    rows, cols = base.shape
    block = min(128, rows)

    def kernel(s_ref, u_ref, b_ref, v_ref, d_ref):
        for j in range(cols // LANES):
            lanes = slice(j * LANES, (j + 1) * LANES)
            s = s_ref[j]
            for f in range(3):
                v_ref[f, :, lanes] = s * u_ref[f, :, lanes]
            d_ref[:, lanes] = b_ref[:, lanes] + 0.5 * s * s

    plane = pl.BlockSpec((block, cols), lambda i: (i, 0))
    triple = pl.BlockSpec((3, block, cols), lambda i: (0, i, 0))
    return pl.pallas_call(
        kernel,
        grid=(rows // block,),
        in_specs=[pl.BlockSpec((cols // LANES, block, LANES), lambda i: (0, i, 0)), triple, plane],
        out_specs=(triple, plane),
        out_shape=(
            jax.ShapeDtypeStruct(unit.shape, jnp.float32),
            jax.ShapeDtypeStruct(base.shape, jnp.float32),
        ),
        compiler_params=params(),
        name="finish",
    )(speed, unit, base)


def fits(rows, cols, tr, tc):
    col_outer, col_inner = factors(cols * tc)
    row_outer, row_inner = factors(rows * tr)
    peers = tr * tc
    return (
        tc == 2
        and col_outer == row_outer == peers == 16
        and col_inner // 2 == LANES
        and rows // tc == row_inner
        and rows % (tc * tc * SUB) == 0
        and rows % (SUB * tc) == 0
        and col_outer % tc == 0
    )


def solution(mesh):
    in_specs = (
        P(None, ("groups", "tr"), "tc"),
        P(("groups", "tr"), "tc"),
        P(("groups", "tr"), "tc"),
    )
    out_specs = (P(None, ("groups", "tr"), "tc"), P(("groups", "tr"), "tc"))

    def chosen(shift_plane, height, dipole):
        rows, cols = height.shape
        if fits(rows, cols, lax.axis_size("tr"), lax.axis_size("tc")):
            return local_kernels(shift_plane, height, dipole)
        return local(shift_plane, height, dipole)

    step = jax.shard_map(
        chosen, mesh=mesh, in_specs=in_specs, out_specs=out_specs, check_vma=False
    )
    return step
```

```python
import math

import jax
import jax.numpy as jnp
import numpy as np
from jax import lax
from jax.experimental import pallas as pl
from jax.experimental.pallas import tpu as pltpu
from jax.sharding import PartitionSpec as P

largest_wavenumber = lax.Precision.HIGHEST


def padded_2(x, sides, width):
    for axis, dim in sides:
        devices, length = (lax.axis_size(axis), x.shape[dim])
        up = [(i, (i + 1) % devices) for i in range(devices)]
        down = [(j, i) for i, j in up]
        last = lax.slice_in_dim(x, length - width, length, axis=dim)
        initial = lax.slice_in_dim(x, 0, width, axis=dim)
        before = lax.ppermute(last, axis, up)
        after = lax.ppermute(initial, axis, down)
        x = jnp.concatenate([before, x, after], axis=dim)
    return x


def rows_first(field):
    return (
        field[..., :-4, :]
        - 8.0 * field[..., 1:-3, :]
        + 8.0 * field[..., 3:-1, :]
        - field[..., 4:, :]
    ) / 12.0


def cols_first(field):
    return (
        field[..., :-4] - 8.0 * field[..., 1:-3] + 8.0 * field[..., 3:-1] - field[..., 4:]
    ) / 12.0


def rows_second(field):
    return (
        -field[..., :-4, :]
        + 16.0 * field[..., 1:-3, :]
        - 30.0 * field[..., 2:-2, :]
        + 16.0 * field[..., 3:-1, :]
        - field[..., 4:, :]
    ) / 12.0


def second_column_split(field):
    return (
        -field[..., :-4]
        + 16.0 * field[..., 1:-3]
        - 30.0 * field[..., 2:-2]
        + 16.0 * field[..., 3:-1]
        - field[..., 4:]
    ) / 12.0


def surface(grad_a, grad_b, curve_aa, curve_bb, curve_ab):
    tan_a = (1.0 + grad_a[0], grad_a[1], grad_a[2])
    tan_b = (grad_b[0], 1.0 + grad_b[1], grad_b[2])
    normal = (
        tan_a[1] * tan_b[2] - tan_a[2] * tan_b[1],
        tan_a[2] * tan_b[0] - tan_a[0] * tan_b[2],
        tan_a[0] * tan_b[1] - tan_a[1] * tan_b[0],
    )
    area_stretch_factor = jnp.sqrt(
        normal[0] * normal[0] + normal[1] * normal[1] + normal[2] * normal[2]
    )
    unit = (
        normal[0] / area_stretch_factor,
        normal[1] / area_stretch_factor,
        normal[2] / area_stretch_factor,
    )
    first_edge_term = tan_a[0] * tan_a[0] + tan_a[1] * tan_a[1] + tan_a[2] * tan_a[2]
    first_f = tan_a[0] * tan_b[0] + tan_a[1] * tan_b[1] + tan_a[2] * tan_b[2]
    first_g = tan_b[0] * tan_b[0] + tan_b[1] * tan_b[1] + tan_b[2] * tan_b[2]
    second_l = curve_aa[0] * unit[0] + curve_aa[1] * unit[1] + curve_aa[2] * unit[2]
    second_m = curve_ab[0] * unit[0] + curve_ab[1] * unit[1] + curve_ab[2] * unit[2]
    second_n = curve_bb[0] * unit[0] + curve_bb[1] * unit[1] + curve_bb[2] * unit[2]
    curvature = (first_edge_term * second_n - 2.0 * first_f * second_m + first_g * second_l) / (
        2.0 * area_stretch_factor * area_stretch_factor
    )
    omega = (grad_a[3] / area_stretch_factor, grad_b[3] / area_stretch_factor)
    return (unit, curvature, omega)


def factors(length):
    inner = min(length, 256)
    return (length // inner, inner)


def angles(count_one, count_two, modulus):
    sample_lattice = (
        jnp.arange(count_one, dtype=jnp.int32)[:, None]
        * jnp.arange(count_two, dtype=jnp.int32)[None, :]
        % modulus
    )
    theta = sample_lattice.astype(jnp.float32) * (2.0 * math.pi / modulus)
    return (jnp.cos(theta), jnp.sin(theta))


def rotation(cos_table, sin_table, sense):
    top = jnp.stack([cos_table, sense * sin_table])
    low = jnp.stack([-sense * sin_table, cos_table])
    return jnp.stack([top, low])


def twisted(sheet_portion, cos_table, sin_table, sense):
    twist_re = sheet_portion[0] * cos_table + sense * sheet_portion[1] * sin_table
    twist_im = sheet_portion[1] * cos_table - sense * sheet_portion[0] * sin_table
    return jnp.stack([twist_re, twist_im])


def forward(values, length, kept, real_input):
    outer, inner = factors(length)
    cos_outer, sin_outer = angles(outer, outer, outer)
    if real_input:
        leading = values.shape[:-1]
        sample_lattice = values.reshape(leading + (outer, inner))
        lookup_array = jnp.stack([cos_outer, -sin_outer])
        sheet_portion = jnp.einsum(
            "...lm,zln->z...nm", sample_lattice, lookup_array, precision=largest_wavenumber
        )
    else:
        leading = values.shape[1:-1]
        sample_lattice = values.reshape((2,) + leading + (outer, inner))
        sheet_portion = jnp.einsum(
            "s...ab,tsac->t...cb",
            sample_lattice,
            rotation(cos_outer, sin_outer, 1.0),
            precision=largest_wavenumber,
        )
    cos_twist, sin_twist = angles(outer, inner, length)
    sheet_portion = twisted(sheet_portion, cos_twist, sin_twist, 1.0)
    cos_inner, sin_inner = angles(inner, kept, inner)
    result = jnp.einsum(
        "s...cb,tsbd->t...cd",
        sheet_portion,
        rotation(cos_inner, sin_inner, 1.0),
        precision=largest_wavenumber,
    )
    return result.reshape((2,) + leading + (outer * kept,))


def inverse(values, length, kept, want_imag):
    outer, inner = factors(length)
    leading = values.shape[1:-1]
    sample_lattice = values.reshape((2,) + leading + (outer, kept))
    cos_inner, sin_inner = angles(kept, inner, inner)
    sheet_portion = jnp.einsum(
        "s...cd,tsdb->t...cb",
        sample_lattice,
        rotation(cos_inner, sin_inner, -1.0),
        precision=largest_wavenumber,
    )
    cos_twist, sin_twist = angles(outer, inner, length)
    sheet_portion = twisted(sheet_portion, cos_twist, sin_twist, -1.0)
    cos_outer, sin_outer = angles(outer, outer, outer)
    if want_imag:
        result = jnp.einsum(
            "s...cb,tsca->t...ab",
            sheet_portion,
            rotation(cos_outer, sin_outer, -1.0),
            precision=largest_wavenumber,
        )
        return result.reshape((2,) + leading + (length,)) / length
    lookup_array = jnp.stack([cos_outer, -sin_outer])
    result = jnp.einsum(
        "s...cb,sca->...ab", sheet_portion, lookup_array, precision=largest_wavenumber
    )
    return result.reshape(leading + (length,)) / length


def wavenumbers(length, kept, positions):
    outer, inner = factors(length)
    number = positions // kept + outer * (positions % kept)
    signed = jnp.where(number >= length // 2, number - length, number)
    return (signed.astype(jnp.float32) / length, number == length // 2)


def local(shift_plane, height, dipole):
    fields = jnp.concatenate([shift_plane, height[None], dipole[None]], 0)
    padded = padded_2(fields, (("tr", 1), ("tc", 2)), 2)
    grad_a = rows_first(padded)[..., 2:-2]
    grad_b = cols_first(padded)[..., 2:-2, :]
    curve_aa = rows_second(padded[:3])[..., 2:-2]
    curve_bb = second_column_split(padded[:3])[..., 2:-2, :]
    curve_ab = rows_first(cols_first(padded[:3]))
    unit, curvature, omega = surface(grad_a, grad_b, curve_aa, curve_bb, curve_ab)
    vorticity = jnp.stack([omega[0], omega[1]])
    sheet_rows = lax.all_to_all(vorticity, "tc", split_axis=1, concat_axis=2, tiled=True)
    col_count = sheet_rows.shape[-1]
    row_count = height.shape[0] * lax.axis_size("tr")
    col_outer, col_inner = factors(col_count)
    row_outer, row_inner = factors(row_count)
    kept = col_inner // 2
    row_spec = forward(sheet_rows, col_count, kept, True)
    stacked = row_spec.reshape((4,) + row_spec.shape[2:])
    columns = lax.all_to_all(stacked, ("tr", "tc"), split_axis=2, concat_axis=1, tiled=True)
    columns = jnp.swapaxes(columns, 1, 2)
    local_width = columns.shape[1]
    full = forward(columns.reshape((2, 2) + columns.shape[1:]), row_count, row_inner, False)
    complete_real_part = full[0]
    full_im = full[1]
    place = lax.axis_index(("tr", "tc")) * local_width + jnp.arange(local_width, dtype=jnp.int32)
    freq_two, nyquist_two = wavenumbers(col_count, kept, place)
    freq_one, nyquist_one = wavenumbers(
        row_count, row_inner, jnp.arange(row_count, dtype=jnp.int32)
    )
    freq_one = freq_one[None, :]
    freq_two = freq_two[:, None]
    radius = jnp.sqrt(freq_one * freq_one + freq_two * freq_two)
    live = (
        jnp.logical_not(nyquist_one[None, :])
        & jnp.logical_not(nyquist_two[:, None])
        & (radius > 0.0)
    )
    factor = jnp.where(live, 0.5 / jnp.where(live, radius, 1.0), 0.0)
    summed_re = factor * (freq_one * complete_real_part[0] + freq_two * complete_real_part[1])
    summed_im = factor * (freq_one * full_im[0] + freq_two * full_im[1])
    speed_parts = inverse(jnp.stack([summed_im, -summed_re]), row_count, row_inner, True)
    partial_value = jnp.swapaxes(speed_parts, 1, 2)
    back_rows = lax.all_to_all(partial_value, ("tr", "tc"), split_axis=1, concat_axis=2, tiled=True)
    weights = (
        jnp.full((col_outer, kept), 2.0, jnp.float32).at[0, 0].set(1.0).reshape(col_outer * kept)
    )
    speed_rows = inverse(back_rows * weights, col_count, kept, False)
    speed = lax.all_to_all(speed_rows, "tc", split_axis=1, concat_axis=0, tiled=True)
    velocity_update = jnp.stack([speed * unit[0], speed * unit[1], speed * unit[2]])
    dipole_update = -2.0 * 0.5 * 0.5 * height + 0.3 * curvature + 0.5 * speed * speed
    return (velocity_update, dipole_update)


LANES = 128
SUB = 8
VMEM_BYTES = 58 * 1024 * 1024


def params():
    return pltpu.CompilerParams(vmem_limit_bytes=VMEM_BYTES)


def two_halves(table):
    table = np.asarray(table, np.float32)
    high = table.astype(jnp.bfloat16)
    low = (table - high.astype(np.float32)).astype(jnp.bfloat16)
    return np.stack([high, low])


def unit_circle(count_one, count_two, modulus):
    theta = np.arange(count_one)[:, None] * np.arange(count_two)[None, :] % modulus
    theta = theta * (2.0 * math.pi / modulus)
    return np.cos(theta), np.sin(theta)


def split(x):
    high = x.astype(jnp.bfloat16)
    low = (x - high.astype(jnp.float32)).astype(jnp.bfloat16)
    return high, low


def product(a, b):
    dot = lambda p, q: jnp.dot(p, q, preferred_element_type=jnp.float32)
    return dot(a[0], b[0]) + (dot(a[0], b[1]) + dot(a[1], b[0]))


def plus(p, q):
    return q if p is None else p if q is None else p + q


def minus(p, q):
    if q is None:
        return p
    return -q if p is None else p - q


def turned(z, number, size, sense):
    re, im = z
    number = number % size
    if number == 0:
        return z
    if 4 * number == size:
        if sense > 0:
            return (im, None if re is None else -re)
        return (None if im is None else -im, re)
    c = math.cos(2.0 * math.pi * number / size)
    s = -sense * math.sin(2.0 * math.pi * number / size)
    if 8 * number == size:
        r = math.sqrt(0.5)
        if im is None:
            return (re * r, re * (-sense * r))
        if sense > 0:
            return ((re + im) * r, (im - re) * r)
        return ((re - im) * r, (im + re) * r)
    if im is None:
        return (re * c, re * s)
    return (re * c - im * s, re * s + im * c)


def butterflies(z, sense):
    size = len(z)
    if size == 1:
        return z
    even = butterflies(z[0::2], sense)
    odd = butterflies(z[1::2], sense)
    if odd[0] is None:
        return even + even
    odd = [turned(o, k, size, sense) for k, o in enumerate(odd)]
    head = [(plus(e[0], o[0]), plus(e[1], o[1])) for e, o in zip(even, odd)]
    tail = [(minus(e[0], o[0]), minus(e[1], o[1])) for e, o in zip(even, odd)]
    return head + tail


def twist(z, c, s, sense):
    re, im = z
    if im is None:
        return (re * c, re * s * (-sense))
    if sense > 0:
        return (re * c + im * s, im * c - re * s)
    return (re * c - im * s, im * c + re * s)


MESH = pl.DeviceIdType.MESH


def window(ref, start, size):
    return ref.at[pl.ds(pl.multiple_of(start, SUB), size), :]


def mega(shift_plane, height, dipole, outer, inner):
    rows, cols = height.shape
    tr, tc = lax.axis_size("tr"), lax.axis_size("tc")
    peers = tr * tc
    some = peers // 2
    half = rows // tc
    block = min(16, half)
    steps = half // block
    lag = steps // 2
    kept = inner // 2
    per = outer // tc
    tall = block + 2 * SUB
    full = rows + 2 * SUB
    strips = cols // LANES
    groups = block // SUB
    span = LANES // block
    parts = 4
    short = inner // parts
    piece = 4 * block
    slab = 4 * inner
    plane = outer * 4 * inner
    length = outer * inner
    c, s = unit_circle(inner, kept, inner)
    row_matrix = two_halves(np.block([[c, -s], [s, c]]))
    c, s = unit_circle(inner, inner, inner)
    fold = np.concatenate([c[: inner // 2 + 1], s[1 : inner // 2]], 0)
    col_matrix = np.stack([two_halves(fold), two_halves(fold.T)])
    c, s = unit_circle(kept, inner, inner)
    back_matrix = two_halves(np.block([[c, s], [-s, c]]) * (2.0 / length))
    c, s = unit_circle(outer, inner, length)
    row_angles = np.stack([c, s]).astype(np.float32)
    col_angles = np.concatenate([c, s]).T.astype(np.float32)

    def kernel(
        sp_ref, h_ref, d_ref, row_tw, row_m, col_tw, col_m, back_m,
        speed_ref, unit_ref, base_ref, plain_ref,
        pad, slope, bend, work, mid, stage, unit_buf, base_buf, split_in, back, tw_row, tw_col,
        load_sem, edge_send, edge_recv, side_send, side_recv, swap_send, swap_recv, keep_sem, unit_sem, base_sem,
        split_send, split_recv, plain_send, plain_recv,
        over_send, over_recv, home_send, home_recv, stay_sem, speed_sem, cross_send, cross_recv,
    ):
        my_tr, my_tc = lax.axis_index("tr"), lax.axis_index("tc")
        me = my_tr * tc + my_tc
        mine = me % some
        side = me // some
        opens = side * some
        quarter = tr // 4
        outermost = (my_tr < quarter) | (my_tr >= tr - quarter)
        place = lambda q: {"tr": q // tc, "tc": q % tc}

        def remote(source, target, send, recv, q):
            return pltpu.make_async_remote_copy(
                source, target, send, recv, device_id=place(q), device_id_type=MESH
            )

        fields = ((sp_ref, slice(0, 2)), (h_ref, 2), (d_ref, 3))
        body = slice(SUB, SUB + rows)

        def cell(ref, r, lanes):
            return ref.at[:, r, lanes] if ref is sp_ref else ref.at[r, lanes]

        def strip(j):
            return pl.ds(pl.multiple_of(j * LANES, LANES), LANES)

        def load(j, carry):
            for n, (ref, f) in enumerate(fields):
                source = cell(ref, slice(0, rows), strip(j))
                pltpu.make_async_copy(source, pad.at[f, 1 + j, body, :], load_sem.at[n]).start()
            return carry

        lax.fori_loop(0, strips, load, 0)
        barrier = pltpu.get_barrier_semaphore()
        for d in range(1, peers):
            pl.semaphore_signal(barrier, inc=1, device_id=place(me ^ d), device_id_type=MESH)
        pl.semaphore_wait(barrier, peers - 1)

        down, up, other = (my_tr + 1) % tr, (my_tr + tr - 1) % tr, 1 - my_tc
        first, final = slice(0, SUB), slice(rows - SUB, rows)
        left, right = slice(0, LANES), slice(cols - LANES, cols)
        before, after = slice(0, SUB), slice(SUB + rows, full)
        interior = slice(1, 1 + strips)
        ends = ((final, before, down), (first, after, up))
        corners = tuple(
            (r, lanes, to_r, to_strip, to_tr)
            for r, to_r, to_tr in ends
            for lanes, to_strip in ((right, 0), (left, 1 + strips))
        )

        def edge_wait(region, k):
            return remote(region, region, edge_send.at[k], edge_recv.at[k], me ^ 1)

        def end_wait(k):
            return edge_wait(pad.at[:, interior, ends[k][1], :], k)

        def corner_wait(k):
            _, _, to_r, to_strip, _ = corners[k]
            return edge_wait(pad.at[:, to_strip, to_r, :], 2 + k)

        def side_rows(i, t):
            return t * half + i * block

        def side_wait(i, t, k):
            r = pl.ds(pl.multiple_of(side_rows(i, t) + SUB, SUB), block)
            region = pad.at[:, k * (1 + strips), r, :]
            return remote(
                region, region, side_send.at[i, t, k], side_recv.at[i, t, k], me ^ 1
            )

        def send_ends(j, carry):
            for k, (r, to_r, to_tr) in enumerate(ends):
                for ref, f in fields:
                    remote(
                        cell(ref, r, strip(j)),
                        pad.at[f, 1 + j, to_r, :],
                        edge_send.at[k],
                        edge_recv.at[k],
                        to_tr * tc + my_tc,
                    ).start()
            return carry

        def send_sides(i, carry):
            for t in range(tc):
                start = side_rows(i, t)
                r = pl.ds(pl.multiple_of(start, SUB), block)
                to_r = pl.ds(pl.multiple_of(start + SUB, SUB), block)
                for k, lanes in enumerate((right, left)):
                    for ref, f in fields:
                        remote(
                            cell(ref, r, lanes),
                            pad.at[f, k * (1 + strips), to_r, :],
                            side_send.at[i, t, k],
                            side_recv.at[i, t, k],
                            my_tr * tc + other,
                        ).start()
            return carry

        lax.fori_loop(0, strips, send_ends, 0)
        lax.fori_loop(0, steps, send_sides, 0)
        for k, (r, lanes, to_r, to_strip, to_tr) in enumerate(corners):
            for ref, f in fields:
                remote(
                    cell(ref, r, lanes),
                    pad.at[f, to_strip, to_r, :],
                    edge_send.at[2 + k],
                    edge_recv.at[2 + k],
                    to_tr * tc + other,
                ).start()

        for t in range(2):
            for n in range(outer):
                tw_row[t, n] = jnp.broadcast_to(row_tw[t, n : n + 1, :], (SUB, inner))

        for n, (_, f) in enumerate(fields):
            region = pad.at[f, interior, body, :]
            pltpu.make_async_copy(region, region, load_sem.at[n]).wait()
        for k in range(2):
            end_wait(k).wait_recv()

        def fill(g, carry):
            r = pl.ds(pl.multiple_of(g * SUB, SUB), SUB)
            x = col_tw[r, :]
            for k in range(2 * outer):
                tw_col[k, r, :] = jnp.broadcast_to(x[:, k : k + 1], (SUB, kept))
            return carry

        lane = lax.broadcasted_iota(jnp.int32, (SUB, LANES), 1)

        def ahead(x, n):
            y = [pltpu.roll(v, LANES - n, 1) for v in x]
            return [jnp.where(lane < LANES - n, a, b) for a, b in zip(y, y[1:])]

        def behind(x, n):
            y = [pltpu.roll(v, n, 1) for v in x]
            return [jnp.where(lane < n, a, b) for a, b in zip(y, y[1:])]

        def at(ref, f, g, k):
            return ref[f, SUB * (g + 1) + k : SUB * (g + 2) + k, :]

        def slant(ref, f, g):
            return 8.0 * (at(ref, f, g, 1) - at(ref, f, g, -1)) - (
                at(ref, f, g, 2) - at(ref, f, g, -2)
            )

        def cross(ta, tb):
            return (
                ta[1] * tb[2] - ta[2] * tb[1],
                ta[2] * tb[0] - ta[0] * tb[2],
                ta[0] * tb[1] - ta[1] * tb[0],
            )

        def views(base, j):
            return (
                pad.at[:, 1 + j, pl.ds(pl.multiple_of(base, SUB), tall), :],
                slope.at[:, j],
                bend.at[:, j],
            )

        def omega(i):
            def one(u, carry):
                t = jnp.where(u == 0, 1 - my_tc, my_tc)
                base = t * half + i * block

                def along(g, carry):
                    source = pl.ds(pl.multiple_of(base + g * SUB, SUB), SUB)
                    r = pl.ds(pl.multiple_of(g * SUB, SUB), SUB)
                    for f in range(4):
                        x = [pad[f, j, source, :] for j in range(strips + 2)]
                        y = [a - v for a, v in zip(ahead(x, 2), x)]
                        one, two = behind(y, 1), behind(y, 2)
                        for j in range(strips):
                            slope[f, j, r, :] = 8.0 * one[j] - (y[j + 1] + two[j])
                    return carry

                lax.fori_loop(1, 1 + groups, along, 0)
                def across(j, carry):
                    near, slopes, bends = views(base, j)
                    for g in range(groups):
                        ga = [slant(near, f, g) for f in range(4)]
                        gb = [at(slopes, f, g, 0) for f in range(4)]
                        n = cross((12.0 + ga[0], ga[1], ga[2]), (gb[0], 12.0 + gb[1], gb[2]))
                        inv = 12.0 * lax.rsqrt(n[0] * n[0] + n[1] * n[1] + n[2] * n[2])
                        for p, v in enumerate((ga[3], gb[3])):
                            start = (((i * (tc + 1) + t) * 2 + p) * strips + j) * block + g * SUB
                            window(work, start, SUB)[...] = v * inv
                    return carry

                lax.fori_loop(0, strips, across, 0, unroll=2)

                @pl.when(u == 0)
                def _():
                    swap(i).start()

                return carry

            lax.fori_loop(0, tc, one, 0)

        def out_copies(i, t):
            r = pl.ds(pl.multiple_of(t * half + i * block, SUB), block)
            return (
                pltpu.make_async_copy(unit_buf.at[t], unit_ref.at[:, r, :], unit_sem.at[t]),
                pltpu.make_async_copy(base_buf.at[t], base_ref.at[r, :], base_sem.at[t]),
            )

        def geometry(i, carry):
            def one(t, carry):
                base = t * half + i * block

                def along(g, carry):
                    source = pl.ds(pl.multiple_of(base + g * SUB, SUB), SUB)
                    r = pl.ds(pl.multiple_of(g * SUB, SUB), SUB)
                    for f in range(3):
                        x = [pad[f, j, source, :] for j in range(strips + 2)]
                        p1, p2, m1, m2 = ahead(x, 1), ahead(x, 2), behind(x, 1), behind(x, 2)
                        for j in range(strips):
                            a, b, c, d = m2[j], m1[j], p1[j + 1], p2[j + 1]
                            slope[f, j, r, :] = ((a - d) + 8.0 * (c - b)) * (1.0 / 12.0)
                            bend[f, j, r, :] = (
                                16.0 * (b + c) - (a + d) - 30.0 * x[j + 1]
                            ) * (1.0 / 12.0)
                    return carry

                lax.fori_loop(0, tall // SUB, along, 0)
                @pl.when(i > 0)
                def _():
                    for copy in out_copies(i, t):
                        copy.wait()

                def across(j, carry):
                    near, slopes, bends = views(base, j)
                    for g in range(groups):
                        ga = [slant(near, f, g) * (1.0 / 12.0) for f in range(3)]
                        gb = [at(slopes, f, g, 0) for f in range(3)]
                        ta = (1.0 + ga[0], ga[1], ga[2])
                        tb = (gb[0], 1.0 + gb[1], gb[2])
                        n = cross(ta, tb)
                        inv = lax.rsqrt(n[0] * n[0] + n[1] * n[1] + n[2] * n[2])
                        out = slice(g * SUB, (g + 1) * SUB)
                        unit = [v * inv for v in n]
                        for f in range(3):
                            unit_buf[t, f, out, strip(j)] = unit[f]
                        big_e = ta[0] * ta[0] + ta[1] * ta[1] + ta[2] * ta[2]
                        big_f = ta[0] * tb[0] + ta[1] * tb[1] + ta[2] * tb[2]
                        big_g = tb[0] * tb[0] + tb[1] * tb[1] + tb[2] * tb[2]
                        sl = sm = sn = None
                        for f in range(3):
                            pair = lambda k: (
                                at(near, f, g, -k) + at(near, f, g, k)
                            )
                            aa = 16.0 * pair(1) - pair(2) - 30.0 * at(near, f, g, 0)
                            sl = plus(sl, aa * unit[f])
                            sm = plus(sm, slant(slopes, f, g) * unit[f])
                            sn = plus(sn, at(bends, f, g, 0) * unit[f])
                        top = big_e * sn + (1.0 / 12.0) * (big_g * sl - 2.0 * big_f * sm)
                        base_buf[t, out, strip(j)] = (
                            -0.5 * at(near, 2, g, 0) + top * (0.15 * inv * inv)
                        )
                    return carry

                lax.fori_loop(0, strips, across, 0, unroll=2)
                for copy in out_copies(i, t):
                    copy.start()
                return carry

            lax.fori_loop(0, tc, one, 0)
            return carry

        lump = 2 * strips * block

        def swap(i):
            start = i * (tc + 1)
            return remote(
                window(work, (start + 1 - my_tc) * lump, lump),
                window(work, (start + tc) * lump, lump),
                swap_send.at[i],
                swap_recv.at[i],
                my_tr * tc + 1 - my_tc,
            )

        def transform(i):
            slots = [i * (tc + 1) + jnp.where(my_tc == k, k, tc) for k in range(tc)]

            def part(p, carry):
                def step(g, carry):
                    r = pl.ds(pl.multiple_of(g * SUB, SUB), SUB)
                    for j in range(inner // LANES):
                        lanes = slice(j * LANES, (j + 1) * LANES)
                        z = []
                        for l in range(outer):
                            strip = (l % per) * (inner // LANES) + j
                            start = ((slots[l // per] * 2 + p) * strips + strip) * block + g * SUB
                            z.append((window(work, start, SUB)[...], None))
                        z = butterflies(z, 1.0)
                        for n in range(outer):
                            re, im = z[n]
                            if n:
                                re, im = twist(z[n], tw_row[0, n, :, lanes], tw_row[1, n, :, lanes], 1.0)
                            if im is None:
                                im = jnp.zeros_like(re)
                            mid[n, r, lanes] = re
                            mid[n, r, inner + j * LANES : inner + (j + 1) * LANES] = im
                    return carry

                lax.fori_loop(0, groups, step, 0)

                def close(n, carry):
                    x = mid[pl.ds(n * span, span)].reshape(span * block, 2 * inner)
                    y = product(split(x), (row_m[0], row_m[1]))
                    for k in range(span):
                        for c in range(2):
                            start = (((i * outer + n * span + k) * 2 + c) * 2 + p) * block
                            window(stage, start, block)[...] = y[
                                k * block : (k + 1) * block, c * kept : (c + 1) * kept
                            ]
                    return carry

                lax.fori_loop(0, outer // span, close, 0)
                return carry

            lax.fori_loop(0, 2, part, 0)

        def cut(i, n):
            return window(stage, (i * outer + n) * piece, piece)

        def landing(ref, who, i):
            return window(ref, who * slab + i * piece, piece)

        def keep(i):
            return pltpu.make_async_copy(
                cut(i, 2 * mine + 1), landing(split_in, mine, i), keep_sem.at[i]
            )

        def keep_plain(i):
            return pltpu.make_async_copy(
                cut(i, 2 * my_tr), landing(plain_ref, me, i), stay_sem.at[i]
            )

        def send_plain(i, d):
            j = my_tr ^ d
            remote(
                cut(i, 2 * j),
                landing(plain_ref, me, i),
                plain_send.at[d],
                plain_recv.at[me],
                j * tc,
            ).start()

        def send(i):
            for d in range(1, some):
                remote(
                    cut(i, 2 * (mine ^ d) + 1),
                    landing(split_in, mine, i),
                    split_send.at[d],
                    split_recv.at[mine],
                    me ^ d,
                ).start()
            keep(i).start()


            @pl.when(jnp.logical_not(outermost))
            def _():
                send_far(i, 0)

            @pl.when(outermost & (i >= lag))
            def _():
                send_far(i - lag, 0)

        def send_far(i, carry):
            for d in range(tr // 2, tr):
                send_plain(i, d)
            return carry

        def send_near(i, carry):
            @pl.when(my_tc == 0)
            def _():
                keep_plain(i).start()

            @pl.when(my_tc != 0)
            def _():
                send_plain(i, 0)

            for d in range(1, tr // 2):
                send_plain(i, d)
            return carry

        def turn(i, carry):
            @pl.when(i < steps)
            def _():
                for t in range(tc):
                    for k in range(2):
                        side_wait(i, t, k).wait_recv()
                omega(i)

            @pl.when(i != 1)
            def _():
                k = jnp.where(i == 0, 0, i - 1)
                swap(k).wait_recv()
                transform(k)
                send(k)

            return carry

        lax.fori_loop(0, steps + 1, turn, 0)

        @pl.when(outermost)
        def _():
            lax.fori_loop(steps - lag, steps, send_far, 0)

        lax.fori_loop(0, steps, send_near, 0)
        lax.fori_loop(0, inner // SUB, fill, 0)

        def columns(x_ref, count, residue, out_ref, out_start, dispatch):
            def fall(g, carry):
                r = pl.ds(pl.multiple_of(g * SUB, SUB), SUB)
                row = (g // groups) * piece + (g % groups) * SUB
                for p in range(2):
                    z = [
                        tuple(
                            window(x_ref, a * slab + row + (2 * c + p) * block, SUB)[...]
                            for c in range(2)
                        )
                        for a in range(count)
                    ] + [None] * (outer - count)
                    z = butterflies(z, 1.0)
                    for k in range(outer):
                        v = z[k]
                        if k:
                            v = twist(v, tw_col[k, r, :], tw_col[outer + k, r, :], 1.0)
                        for c in range(2):
                            start = (k * 4 + 2 * p + c) * inner + g * SUB
                            window(work, start, SUB)[...] = v[c]
                return carry

            lax.fori_loop(0, inner // SUB, fall, 0)
            lane = lax.broadcasted_iota(jnp.int32, (1, kept), 1)
            fre_two = (residue + outer * lane).astype(jnp.float32) * (1.0 / length)
            mid_row = inner // 2
            row = lax.broadcasted_iota(jnp.int32, (mid_row, kept), 0)
            top_row = lax.broadcasted_iota(jnp.int32, (SUB, kept), 0) == 0

            def headed(a, x):
                return jnp.concatenate([jnp.where(top_row, a[:SUB], x[:SUB]), x[SUB:]], 0)

            zero = jnp.zeros((SUB, kept), jnp.float32)

            def spin(k, carry):
                x = [window(work, (k * 4 + b) * inner, inner)[...] for b in range(4)]
                y = product((col_m[0, 0], col_m[0, 1]), split(jnp.concatenate(x, 1)))
                block_of = lambda t, b: y[
                    t * mid_row : (t + 1) * mid_row, b * kept : (b + 1) * kept
                ]
                rises, falls = [], []
                for p in range(2):
                    c_re, c_im = block_of(0, 2 * p), block_of(0, 2 * p + 1)
                    s_re, s_im = block_of(1, 2 * p), block_of(1, 2 * p + 1)
                    rises.append((c_re + headed(zero, s_im), c_im - headed(zero, s_re)))
                    falls.append((headed(s_re, c_re - s_im), headed(s_im, c_im + s_re)))

                def weighed(signed, both):
                    fre_one = signed.astype(jnp.float32) * (1.0 / length)
                    square = fre_one * fre_one + fre_two * fre_two
                    live = (signed != -(length // 2)) & (square > 0.0)
                    factor = jnp.where(
                        live, (0.5 / length) * lax.rsqrt(jnp.where(live, square, 1.0)), 0.0
                    )
                    one = factor * fre_one
                    two = factor * fre_two
                    return (
                        one * both[0][0] + two * both[1][0],
                        one * both[0][1] + two * both[1][1],
                    )

                a_re, a_im = weighed(k + outer * row, rises)
                b_re, b_im = weighed(
                    k - outer * jnp.where(row == 0, mid_row, row), falls
                )
                w_re = jnp.concatenate([headed(a_im, a_im + b_im), headed(b_im, a_re - b_re)], 0)
                w_im = jnp.concatenate(
                    [headed(-a_re, -a_re - b_re), headed(-b_re, a_im - b_im)], 0
                )
                y = product((col_m[1, 0], col_m[1, 1]), split(jnp.concatenate([w_re, w_im], 1)))
                window(work, k * 4 * inner, inner)[...] = y[:, :kept]
                window(work, (k * 4 + 1) * inner, inner)[...] = y[:, kept:]
                return carry

            lax.fori_loop(0, outer, spin, 0)

            def leave(h, carry):
                def rise(g, carry):
                    row = h * short + g * SUB
                    r = pl.ds(pl.multiple_of(row, SUB), SUB)
                    z = []
                    for k in range(outer):
                        v = tuple(
                            window(work, (k * 4 + c) * inner + row, SUB)[...] for c in range(2)
                        )
                        if k:
                            v = twist(v, tw_col[k, r, :], tw_col[outer + k, r, :], -1.0)
                        z.append(v)
                    z = butterflies(z, -1.0)
                    for a in range(outer):
                        for c in range(2):
                            start = out_start + ((a * parts + h) * 2 + c) * short + g * SUB
                            window(out_ref, start, SUB)[...] = z[a][c]
                    return carry

                lax.fori_loop(0, short // SUB, rise, 0)
                dispatch(h)
                return carry

            lax.fori_loop(0, parts, leave, 0)

        def slot(n, h):
            return window(back, (n * parts + h) * 2 * short, 2 * short)

        split_slot = tr + side * some + mine
        plain_slot = my_tr

        def over(h, d):
            q = me ^ d
            a = q ^ opens
            return remote(
                window(work, plane + (a * parts + h) * 2 * short, 2 * short),
                slot(split_slot, h),
                over_send.at[h, d],
                over_recv.at[h, side * some + mine],
                q,
            )

        def over_here(h):
            a = me ^ opens
            return pltpu.make_async_copy(
                window(work, plane + (a * parts + h) * 2 * short, 2 * short),
                slot(split_slot, h),
                over_send.at[h, 0],
            )

        def home(h, d):
            q = me ^ d
            return remote(
                window(split_in, (q * parts + h) * 2 * short, 2 * short),
                slot(plain_slot, h),
                home_send.at[h, d],
                home_recv.at[h, my_tr],
                q,
            )

        def home_here(h):
            return pltpu.make_async_copy(
                window(split_in, (me * parts + h) * 2 * short, 2 * short),
                slot(plain_slot, h),
                home_send.at[h, 0],
            )

        order = [*range(some, peers), *range(1, some)]

        def dispatch_split(h):
            for d in order:
                over(h, d).start()
            over_here(h).start()

        def dispatch_plain(h):
            for d in order:
                home(h, d).start()
            home_here(h).start()

        for i in range(steps):
            swap(i).wait_send()
            keep(i).wait()

        def arrived(ref, who, sem, send):
            return remote(
                window(ref, who * slab, slab), window(ref, who * slab, slab), send, sem, me ^ 1
            )

        for d in range(1, some):
            arrived(split_in, mine ^ d, split_recv.at[mine ^ d], split_send.at[d]).wait_recv()
        columns(split_in, some, 2 * mine + 1, work, plane, dispatch_split)

        for d in range(1, some):
            arrived(split_in, mine, split_recv.at[mine], split_send.at[d]).wait_send()
        for d in range(1, tr):
            arrived(plain_ref, me, plain_recv.at[me], plain_send.at[d]).wait_send()

        @pl.when(my_tc != 0)
        def _():
            arrived(plain_ref, me, plain_recv.at[me], plain_send.at[0]).wait_send()

        @pl.when(my_tc == 0)
        def _():
            for i in range(steps):
                keep_plain(i).wait()
            for d in range(1, peers):
                arrived(plain_ref, me ^ d, plain_recv.at[me ^ d], plain_send.at[0]).wait_recv()
            copy = pltpu.make_async_copy(plain_ref, stage, stay_sem.at[0])
            copy.start()
            copy.wait()
            columns(stage, outer, 2 * my_tr, split_in, 0, dispatch_plain)

        for k in range(4):
            corner_wait(k).wait_recv()
        lax.fori_loop(0, steps, geometry, 0)
        for t in range(tc):
            for copy in out_copies(steps - 1, t):
                copy.wait()
        for k in range(2):
            end_wait(k).wait_send()
        for k in range(4):
            corner_wait(k).wait_send()

        def side_done(i, carry):
            for t in range(tc):
                for k in range(2):
                    side_wait(i, t, k).wait_send()
            return carry

        lax.fori_loop(0, steps, side_done, 0)

        roomy = outer * 4 * short

        def spread(h):
            start = roomy + (h * tc + my_tc) * strips * short
            r = pl.ds(pl.multiple_of(my_tc * half + h * short, SUB), short)
            return [
                pltpu.make_async_copy(
                    stage.at[pl.ds(pl.multiple_of(start + j * short, SUB), short), :],
                    speed_ref.at[j, r, :],
                    speed_sem.at[h, j],
                )
                for j in range(strips)
            ]

        def give(h):
            start = roomy + (h * tc + 1 - my_tc) * strips * short
            r = pl.ds(pl.multiple_of(my_tc * half + h * short, SUB), short)
            return [
                remote(
                    stage.at[pl.ds(pl.multiple_of(start + j * short, SUB), short), :],
                    speed_ref.at[j, r, :],
                    cross_send.at[h, j],
                    cross_recv.at[h, j],
                    my_tr * tc + 1 - my_tc,
                )
                for j in range(strips)
            ]

        def inverse(h, carry):
            over_here(h).wait()

            @pl.when(my_tc == 0)
            def _():
                home_here(h).wait()

            for d in range(1, peers):
                n = (side * some + mine) ^ d
                remote(
                    slot(0, h), slot(0, h), over_send.at[h, d], over_recv.at[h, n], me ^ d
                ).wait_recv()
            for d in range(tr):
                n = my_tr ^ d
                copy = remote(
                    slot(0, h), slot(0, h), home_send.at[h, d], home_recv.at[h, n], me ^ 1
                )
                if d:
                    copy.wait_recv()
                else:
                    pl.when(my_tc != 0)(copy.wait_recv)

            lane = lax.broadcasted_iota(jnp.int32, (short, kept), 1)
            weights = (back_m[0], back_m[1])

            def start(j, carry):
                weight = jnp.where((lane == 0) & (j == 0), 0.5, 1.0)
                take = lambda n, c: window(back, ((n * parts + h) * 2 + c) * short, short)[...]
                even = jnp.concatenate([take(j, c) * weight for c in range(2)], 1)
                odd = jnp.concatenate(
                    [take(tr + j, c) + take(tr + some + j, c) for c in range(2)], 1
                )
                y = product(split(jnp.concatenate([even, odd], 0)), weights)
                for k in range(2):
                    for b in range(4):
                        window(stage, ((2 * j + k) * 4 + b) * short, short)[...] = y[
                            k * short : (k + 1) * short, b * LANES : (b + 1) * LANES
                        ]
                return carry

            lax.fori_loop(0, outer // 2, start, 0)

            def step(g, carry):
                for j in range(inner // LANES):
                    lanes = slice(j * LANES, (j + 1) * LANES)
                    z = []
                    for n in range(outer):
                        v = tuple(
                            window(
                                stage,
                                (n * 4 + c * (inner // LANES) + j) * short + g * SUB,
                                SUB,
                            )[...]
                            for c in range(2)
                        )
                        if n:
                            v = twist(v, tw_row[0, n, :, lanes], tw_row[1, n, :, lanes], -1.0)
                        z.append(v)
                    z = butterflies(z, -1.0)
                    for l in range(outer):
                        strip = (l % per) * (inner // LANES) + j
                        at_row = roomy + ((h * tc + l // per) * strips + strip) * short + g * SUB
                        window(stage, at_row, SUB)[...] = z[l][0]
                return carry

            lax.fori_loop(0, short // SUB, step, 0)
            for copy in spread(h) + give(h):
                copy.start()
            return carry

        lax.fori_loop(0, parts, inverse, 0)

        def settle(h, carry):
            for d in range(1, peers):
                over(h, d).wait_send()

            @pl.when(my_tc == 0)
            def _():
                for d in range(1, peers):
                    home(h, d).wait_send()

            for copy in spread(h):
                copy.wait()
            for copy in give(h):
                copy.wait()
            return carry

        lax.fori_loop(0, parts, settle, 0)

    f32 = lambda *dims: jax.ShapeDtypeStruct(dims, jnp.float32)
    vmem = lambda *dims: pltpu.VMEM(dims, jnp.float32)
    anywhere = pl.BlockSpec(memory_space=pl.ANY)
    near = pl.BlockSpec(memory_space=pltpu.VMEM)
    dma = lambda *dims: pltpu.SemaphoreType.DMA(dims)
    return pl.pallas_call(
        kernel,
        in_specs=[anywhere] * 3 + [near] * 5,
        out_specs=[anywhere] * 4,
        out_shape=(
            f32(strips, rows, LANES),
            f32(3, rows, cols),
            f32(rows, cols),
            f32(peers * slab, kept),
        ),
        scratch_shapes=[
            vmem(4, strips + 2, full, LANES),
            vmem(4, strips, tall, LANES),
            vmem(3, strips, tall, LANES),
            vmem(steps * (tc + 1) * lump_rows(strips, block), LANES),
            vmem(outer, block, 2 * inner),
            vmem(steps * outer * piece, LANES),
            vmem(tc, 3, block, cols),
            vmem(tc, block, cols),
            vmem(some * slab, LANES),
            vmem((tr + peers) * 2 * inner, LANES),
            vmem(2, outer, SUB, inner),
            vmem(2 * outer, inner, kept),
            dma(3),
            dma(6),
            dma(6),
            dma(steps, tc, 2),
            dma(steps, tc, 2),
            dma(steps),
            dma(steps),
            dma(steps),
            dma(tc),
            dma(tc),
            dma(some),
            dma(some),
            dma(tr),
            dma(peers),
            dma(parts, peers),
            dma(parts, peers),
            dma(parts, peers),
            dma(parts, tr),
            dma(steps),
            dma(parts, strips),
            dma(parts, strips),
            dma(parts, strips),
        ],
        compiler_params=pltpu.CompilerParams(
            vmem_limit_bytes=66 * 1000 * 1000, collective_id=0, has_side_effects=True
        ),
        name="mega",
    )(
        shift_plane,
        height,
        dipole,
        jnp.asarray(row_angles),
        jnp.asarray(row_matrix),
        jnp.asarray(col_angles),
        jnp.asarray(col_matrix),
        jnp.asarray(back_matrix),
    )


def lump_rows(strips, block):
    return 2 * strips * block


def local_kernels(shift_plane, height, dipole):
    tc = lax.axis_size("tc")
    cols = height.shape[1]
    outer, inner = factors(cols * tc)
    speed, unit, base = mega(shift_plane, height, dipole, outer, inner)[:3]
    return finish(speed, unit, base)


def finish(speed, unit, base):
    rows, cols = base.shape
    block = min(128, rows)

    def kernel(s_ref, u_ref, b_ref, v_ref, d_ref):
        for j in range(cols // LANES):
            lanes = slice(j * LANES, (j + 1) * LANES)
            s = s_ref[j]
            for f in range(3):
                v_ref[f, :, lanes] = s * u_ref[f, :, lanes]
            d_ref[:, lanes] = b_ref[:, lanes] + 0.5 * s * s

    plane = pl.BlockSpec((block, cols), lambda i: (i, 0))
    triple = pl.BlockSpec((3, block, cols), lambda i: (0, i, 0))
    return pl.pallas_call(
        kernel,
        grid=(rows // block,),
        in_specs=[pl.BlockSpec((cols // LANES, block, LANES), lambda i: (0, i, 0)), triple, plane],
        out_specs=(triple, plane),
        out_shape=(
            jax.ShapeDtypeStruct(unit.shape, jnp.float32),
            jax.ShapeDtypeStruct(base.shape, jnp.float32),
        ),
        compiler_params=params(),
        name="finish",
    )(speed, unit, base)


def fits(rows, cols, tr, tc):
    col_outer, col_inner = factors(cols * tc)
    row_outer, row_inner = factors(rows * tr)
    peers = tr * tc
    return (
        tc == 2
        and col_outer == row_outer == peers == 16
        and col_inner // 2 == LANES
        and rows // tc == row_inner
        and rows % (tc * tc * SUB) == 0
        and rows % (SUB * tc) == 0
        and col_outer % tc == 0
    )


def solution(mesh):
    in_specs = (
        P(None, ("groups", "tr"), "tc"),
        P(("groups", "tr"), "tc"),
        P(("groups", "tr"), "tc"),
    )
    out_specs = (P(None, ("groups", "tr"), "tc"), P(("groups", "tr"), "tc"))

    def chosen(shift_plane, height, dipole):
        rows, cols = height.shape
        if fits(rows, cols, lax.axis_size("tr"), lax.axis_size("tc")):
            return local_kernels(shift_plane, height, dipole)
        return local(shift_plane, height, dipole)

    step = jax.shard_map(
        chosen, mesh=mesh, in_specs=in_specs, out_specs=out_specs, check_vma=False
    )
    return step
```
